32 devices in a mesh: batch: 4 (over y, x), seg: 8 (over z, core).
Axes of the slice: x: 2, y: 2, z: 4, core: 2. Of those that a mesh axis runs over, the one named last changes fastest.
Arguments:
- hidden: bfloat16 [2, 4, 4, 8, 128, 768], P(None, 'batch', None, 'seg'), may hold values from -6 to 6
- seg_doc: int32 [2, 4, 32], P(None, 'batch'), may hold values from 0 to 3, as said below
- seg_attn: bfloat16 [768, 3072], P('seg')
- seg_up: bfloat16 [768, 3072], P('seg'), may hold values from -0.21875 to 0.21875
- seg_down: bfloat16 [768, 3072], P('seg'), may hold values from -0.109375 to 0.109375
- seg_vec: bfloat16 [768, 12], P('seg')
- cross_attn: bfloat16 [768, 3072], P('seg')
- cross_up: bfloat16 [768, 3072], P('seg'), may hold values from -0.21875 to 0.21875
- cross_down: bfloat16 [768, 3072], P('seg'), may hold values from -0.109375 to 0.109375
- cross_vec: bfloat16 [768, 12], P('seg')
- tok_cot: bfloat16 [2, 4, 4, 8, 128, 768], P(None, 'batch', None, 'seg'), may hold values from -6 to 6
- cls_cot: bfloat16 [2, 4, 4, 8, 768], P(None, 'batch', None, 'seg'), may hold values from -6 to 6
Outputs:
- tok_out: bfloat16 [2, 4, 4, 8, 128, 768], P(None, 'batch', None, 'seg')
- cls_out: bfloat16 [2, 4, 4, 8, 768], P(None, 'batch', None, 'seg')
- hidden_grad: float32 [2, 4, 4, 8, 128, 768], P(None, 'batch', None, 'seg')
- seg_attn_grad: float32 [768, 3072], P('seg')
- seg_up_grad: float32 [768, 3072], P('seg')
- seg_down_grad: float32 [768, 3072], P('seg')
- seg_vec_grad: float32 [768, 12], P('seg')
- cross_attn_grad: float32 [768, 3072], P('seg')
- cross_up_grad: float32 [768, 3072], P('seg')
- cross_down_grad: float32 [768, 3072], P('seg')
- cross_vec_grad: float32 [768, 12], P('seg')
The draws below stay inside these ranges and needn't reach their ends.
Inputs may be any that keep to these rules, and one draw needn't show every extreme that they name: `seg_doc`: within one micro-batch and group, document numbers start at 0 and never fall; the segments fall into aligned blocks of 32, each block one document or four documents of 8; both kinds occur in every draw.
All inputs are finite; a program needn't handle non-finite values.
Results may differ from the reference program's by a relative error of at most 0.015.
Values may be sent and summed in bfloat16 or wider, within the bound.
No kernel may reach another device: no remote copies, remote signals or barrier semaphores. Data moves between devices by JAX's collectives and lax.ppermute only.
A program may use at most 256 MiB of HBM per device.

```python
import jax
import jax.numpy as jnp
from jax import lax

D = 768
HEADS = 12
HEAD_DIM = 64
FF = 3072
SEG_LEN = 128
SEG_DEV = 4
MICRO = 2
GROUPS = 4
GROUP_SEGS = 32
LONG_SEGS = 32
SHORT_SEGS = 8
N_SEG = 8


def attn_common(key, out_factor):
    base = jax.random.normal(key, (D, 4 * D), jnp.float32) * D ** (-0.5)
    column = jnp.arange(4 * D)
    factor = jnp.where(column >= 3 * D, out_factor, 1.0)
    return (base * factor).astype(jnp.bfloat16)


def vector_common(key):
    first_key, second_key = jax.random.split(key)
    biases = jax.random.normal(first_key, (D, 12), jnp.float32) * 0.5
    gains = jax.random.uniform(second_key, (D, 12), jnp.float32, 0.6, 1.4)
    column = jnp.arange(12)
    is_gain = jnp.logical_or(column == 3, column == 6)
    return jnp.where(is_gain[None, :], gains, biases).astype(jnp.bfloat16)


def draw_seg_attn(key, part):
    return attn_common(jax.random.fold_in(key, 101), 6.0)


def draw_cross_attn(key, part):
    return attn_common(jax.random.fold_in(key, 202), 4.0)


def draw_seg_vec(key, part):
    return vector_common(jax.random.fold_in(key, 303))


def draw_cross_vec(key, part):
    return vector_common(jax.random.fold_in(key, 404))


def draw_seg_doc(key, part):
    blocks = GROUP_SEGS // LONG_SEGS
    kind = jax.random.randint(jax.random.fold_in(key, 505), (MICRO, GROUPS, blocks), 0, 2)
    kind = kind.at[0, 1, :].set(0).at[0, 0, 0].set(1)
    docs = 1 + 3 * (1 - kind)
    first = jnp.cumsum(docs, axis=-1) - docs
    place = jnp.arange(GROUP_SEGS)
    block_of = place // LONG_SEGS
    within = place % LONG_SEGS
    first_at = first[:, :, block_of]
    kind_at = kind[:, :, block_of]
    return (first_at + (1 - kind_at) * (within // SHORT_SEGS)).astype(jnp.int32)


def steps_of(rng, dims, cuts, least, top_value):
    loudness = 1.0
    for axis_at, shards_of in cuts:
        draws = jax.random.uniform(jax.random.fold_in(jax.random.fold_in(rng, 6), axis_at), (shards_of,), jnp.float32, least / len(cuts), top_value / len(cuts))
        loudness = loudness * jnp.repeat(jnp.exp(draws), dims[axis_at] // shards_of).reshape((-1,) + (1,) * (len(dims) - 1 - axis_at))
    return loudness


def scatter_about(stream_key, dims, deviation, most, cuts=(), dtype=jnp.bfloat16):
    array = deviation * jax.random.normal(stream_key, dims, jnp.float32)
    if cuts:
        array = array * steps_of(stream_key, dims, cuts, -0.22, 0.18)
    return jnp.clip(array, -most, most).astype(dtype)


def setup_inputs(seed: int = 0) -> dict:
    streams_of = jax.random.split(jax.random.key(seed), 13)
    return {
        "hidden": scatter_about(streams_of[0], (MICRO, GROUPS, SEG_DEV, N_SEG, SEG_LEN, D), 1.0, 6.0, ((1, 4), (3, 8))),
        "seg_doc": draw_seg_doc(jax.random.fold_in(streams_of[12], 71), 0),
        "seg_attn": draw_seg_attn(jax.random.fold_in(streams_of[12], 71), 0),
        "seg_up": scatter_about(streams_of[3], (D, FF), D ** -0.5, 0.21875, ((0, 8),)),
        "seg_down": scatter_about(streams_of[4], (D, FF), FF ** -0.5, 0.109375, ((0, 8),)),
        "seg_vec": draw_seg_vec(jax.random.fold_in(streams_of[12], 71), 0),
        "cross_attn": draw_cross_attn(jax.random.fold_in(streams_of[12], 71), 0),
        "cross_up": scatter_about(streams_of[7], (D, FF), D ** -0.5, 0.21875, ((0, 8),)),
        "cross_down": scatter_about(streams_of[8], (D, FF), FF ** -0.5, 0.109375, ((0, 8),)),
        "cross_vec": draw_cross_vec(jax.random.fold_in(streams_of[12], 71), 0),
        "tok_cot": scatter_about(streams_of[10], (MICRO, GROUPS, SEG_DEV, N_SEG, SEG_LEN, D), 1.0, 6.0, ((1, 4), (3, 8))),
        "cls_cot": scatter_about(streams_of[11], (MICRO, GROUPS, SEG_DEV, N_SEG, D), 1.0, 6.0, ((1, 4), (3, 8))),
    }


HIGH = lax.Precision.HIGHEST
NEG_FILL = -1e+30
LN_EPS = 1e-05

@jax.custom_vjp
def low(v):
    return lax.optimization_barrier(v.astype(jnp.bfloat16)).astype(jnp.float32)

@jax.custom_vjp
def low_back(v):
    return v

def low_keep(v):
    return (low(v), None)

def low_pass(kept, grad):
    return (grad,)

def back_keep(v):
    return (v, None)

def back_low(kept, grad):
    return (low(grad),)
low.defvjp(low_keep, low_pass)
low_back.defvjp(back_keep, back_low)

def rounded_both(value):
    return low(low_back(value))

def product(left, right):
    return jnp.dot(left, right, precision=HIGH, preferred_element_type=jnp.float32)

def layer_norm(rows, gain, shift):
    centred = rows - lax.optimization_barrier(jnp.mean(rows, -1, keepdims=True))
    spread = lax.optimization_barrier(jnp.mean(centred * centred, -1, keepdims=True))
    return centred * lax.rsqrt(spread + LN_EPS) * gain + shift

def gelu_exact(value):
    return jax.nn.gelu(value, approximate=False)

def attend(query, keys, values, same):
    scale = HEAD_DIM ** (-0.5)
    scores = low_back(jnp.einsum('blhe,bmhe->bhlm', query, keys, precision=HIGH) * scale)
    if same is not None:
        scores = jnp.where(same[:, None], scores, NEG_FILL)
    top = lax.optimization_barrier(jnp.max(scores, -1, keepdims=True))
    expo = jnp.exp(scores - top)
    probs = expo / lax.optimization_barrier(jnp.sum(expo, -1, keepdims=True))
    return jnp.einsum('bhlm,bmhe->blhe', low(probs), values, precision=HIGH)

def block(rows, weights, same):
    attn, up_proj, down_proj, vec = weights
    batch, length = (rows.shape[0], rows.shape[1])
    flat = rows.reshape(-1, D)
    entry = low(flat)
    query = rounded_both(product(entry, attn[:, :D]) + vec[:, 0])
    keys = rounded_both(product(entry, attn[:, D:2 * D]))
    values = rounded_both(product(entry, attn[:, 2 * D:3 * D]) + vec[:, 1])
    shape = (batch, length, HEADS, HEAD_DIM)
    mixed = attend(query.reshape(shape), keys.reshape(shape), values.reshape(shape), same)
    mixed = rounded_both(mixed.reshape(-1, D))
    branch = low_back(product(mixed, attn[:, 3 * D:]) + vec[:, 2])
    first = layer_norm(flat + branch, vec[:, 3], vec[:, 4])
    inner = low_back(product(low(first), up_proj) + vec[:, 8:].T.reshape(-1))
    activated = low(gelu_exact(inner))
    second = low_back(product(activated, down_proj.T) + vec[:, 5])
    return layer_norm(first + second, vec[:, 6], vec[:, 7]).reshape(rows.shape)

def forward(tokens, seg_weights, cross_weights, seg_doc):
    pieces = tokens.reshape(-1, 32, SEG_LEN, D)

    def run_piece(piece):
        return block(piece, seg_weights, None)
    seg_out = lax.map(jax.checkpoint(run_piece), pieces)
    seg_out = seg_out.reshape(MICRO * GROUPS, GROUP_SEGS, SEG_LEN, D)
    docs = seg_doc.reshape(MICRO * GROUPS, GROUP_SEGS)
    same = docs[:, :, None] == docs[:, None, :]
    cross = block(seg_out[:, :, 0, :], cross_weights, same)
    return (seg_out.reshape(tokens.shape), cross.reshape(MICRO, GROUPS, SEG_DEV, GROUP_SEGS // SEG_DEV, D))

def reference(hidden, seg_doc, seg_attn, seg_up, seg_down, seg_vec, cross_attn, cross_up, cross_down, cross_vec, tok_cot, cls_cot):
    seg_weights = (seg_attn.astype(jnp.float32), seg_up.astype(jnp.float32), seg_down.astype(jnp.float32), seg_vec.astype(jnp.float32))
    cross_weights = (cross_attn.astype(jnp.float32), cross_up.astype(jnp.float32), cross_down.astype(jnp.float32), cross_vec.astype(jnp.float32))

    def run(tokens, seg_set, cross_set):
        return forward(tokens, seg_set, cross_set, seg_doc)
    outputs, pull = jax.vjp(run, hidden.astype(jnp.float32), seg_weights, cross_weights)
    tok_grad, seg_grads, cross_grads = pull((tok_cot.astype(jnp.float32), cls_cot.astype(jnp.float32)))
    return (outputs[0].astype(jnp.bfloat16), outputs[1].astype(jnp.bfloat16), tok_grad, seg_grads[0], seg_grads[1], seg_grads[2], seg_grads[3], cross_grads[0], cross_grads[1], cross_grads[2], cross_grads[3])
```

```python
from functools import partial

import jax
import jax.numpy as jnp
from jax import lax
from jax.experimental import pallas as pl
from jax.experimental.pallas import tpu as pltpu
from jax.sharding import PartitionSpec as P

HEADS = 12
HEAD_DIM = 64
SEG_LEN = 128
PAIRS = HEADS // 2
PAIR = 2 * HEAD_DIM

NEG_FILL = -1e30
LN_EPS = 1e-05
SCALE = HEAD_DIM ** (-0.5)
ROOT_HALF = 0.7071067811865476
PDF_AT_ZERO = 0.3989422804014327
BLOCK = 256
VMEM_LIMIT = 60 * 1024 * 1024

f32 = jnp.float32
bf16 = jnp.bfloat16


def dot_nn(left, right):
    return lax.dot_general(left, right, (((1,), (0,)), ((), ())), preferred_element_type=f32)


def dot_nt(left, right):
    return lax.dot_general(left, right, (((1,), (1,)), ((), ())), preferred_element_type=f32)


def dot_tn(left, right):
    return lax.dot_general(left, right, (((0,), (0,)), ((), ())), preferred_element_type=f32)


def normalise(rows):
    centred = rows - jnp.mean(rows, -1, keepdims=True)
    spread = jnp.mean(centred * centred, -1, keepdims=True)
    inverse = lax.rsqrt(spread + LN_EPS)
    return centred * inverse, inverse


def norm_back(grad, unit, inverse, gain):
    scaled = grad * gain
    return inverse * (
        scaled
        - jnp.mean(scaled, -1, keepdims=True)
        - unit * jnp.mean(scaled * unit, -1, keepdims=True)
    )


def column_sum(rows):
    return jnp.sum(rows, 0, keepdims=True)


def gelu_parts(value):
    cdf = 0.5 * (1.0 + lax.erf(value * ROOT_HALF))
    pdf = PDF_AT_ZERO * jnp.exp(-0.5 * value * value)
    return value * cdf, cdf + value * pdf


def first_half(rows):
    return lax.broadcasted_iota(jnp.int32, (rows, PAIR), 1) < HEAD_DIM


def split_heads(rows, first):
    zero = jnp.zeros_like(rows)
    return jnp.concatenate([jnp.where(first, rows, zero), jnp.where(first, zero, rows)], 0)


def join_heads(stacked, first):
    rows = stacked.shape[0] // 2
    return jnp.where(first, stacked[:rows], stacked[rows:])


def pair_probs(query, keys, mask):
    scores = dot_nt(query, keys) * SCALE
    if mask is not None:
        scores = jnp.where(mask, scores, NEG_FILL)
    top = jnp.max(scores, -1, keepdims=True)
    expo = jnp.exp(scores - top)
    return expo * (1.0 / jnp.sum(expo, -1, keepdims=True))


def pair_forward(qkv_ref, out_ref, rows, pair, width, mask):
    first = first_half(rows.size)
    at = pair * PAIR
    query = split_heads(qkv_ref[rows, at : at + PAIR], first)
    keys = qkv_ref[rows, width + at : width + at + PAIR]
    values = qkv_ref[rows, 2 * width + at : 2 * width + at + PAIR]
    probs = pair_probs(query, keys, mask)
    mixed = join_heads(dot_nn(probs.astype(bf16), values), first)
    out_ref[rows, at : at + PAIR] = mixed.astype(bf16)


def pair_backward(qkv_ref, grad_ref, out_ref, rows, pair, width, mask):
    first = first_half(rows.size)
    at = pair * PAIR
    query = split_heads(qkv_ref[rows, at : at + PAIR], first)
    keys = qkv_ref[rows, width + at : width + at + PAIR]
    values = qkv_ref[rows, 2 * width + at : 2 * width + at + PAIR]
    out_grad = split_heads(grad_ref[rows, at : at + PAIR], first)
    probs = pair_probs(query, keys, mask)
    value_grad = dot_tn(probs.astype(bf16), out_grad)
    prob_grad = dot_nt(out_grad, values)
    score_grad = probs * (prob_grad - jnp.sum(prob_grad * probs, -1, keepdims=True))
    score_grad = score_grad.astype(bf16)
    query_grad = join_heads(dot_nn(score_grad, keys), first) * SCALE
    key_grad = dot_tn(score_grad, query) * SCALE
    out_ref[rows, at : at + PAIR] = query_grad.astype(bf16)
    out_ref[rows, width + at : width + at + PAIR] = key_grad.astype(bf16)
    out_ref[rows, 2 * width + at : 2 * width + at + PAIR] = value_grad.astype(bf16)


def qkv_bias(vec_ref):
    query = vec_ref[0:1, :]
    return jnp.concatenate([query, jnp.zeros_like(query), vec_ref[1:2, :]], 1)


def attn_fwd_kernel(x_ref, w_ref, vec_ref, qkv_ref, mixed_ref, sum_ref):
    width = x_ref.shape[1]
    rows = x_ref[...]
    qkv = dot_nn(rows, w_ref[:, : 3 * width]) + qkv_bias(vec_ref)
    qkv_ref[...] = qkv.astype(bf16)
    for start in range(0, x_ref.shape[0], SEG_LEN):
        for pair in range(PAIRS):
            pair_forward(qkv_ref, mixed_ref, pl.ds(start, SEG_LEN), pair, width, None)
    branch = dot_nn(mixed_ref[...], w_ref[:, 3 * width :])
    sum_ref[...] = rows.astype(f32) + branch + vec_ref[2:3, :]


def ffn_fwd_kernel(sum_ref, up_ref, down_ref, vec_ref, norm_ref, act_ref, slope_ref, second_ref, tok_ref, cls_ref):
    width = sum_ref.shape[1]
    unit, _ = normalise(sum_ref[...])
    normed = unit * vec_ref[3:4, :] + vec_ref[4:5, :]
    low = normed.astype(bf16)
    norm_ref[...] = low
    total = normed + vec_ref[5:6, :]
    for part in range(4):
        cols = pl.ds(part * width, width)
        inner = dot_nn(low, up_ref[:, cols]) + vec_ref[8 + part : 9 + part, :]
        act, slope = gelu_parts(inner)
        act = act.astype(bf16)
        act_ref[:, cols] = act
        slope_ref[:, cols] = slope.astype(bf16)
        total = total + dot_nt(act, down_ref[:, cols])
    second_ref[...] = total
    unit, _ = normalise(total)
    result = unit * vec_ref[6:7, :] + vec_ref[7:8, :]
    tok_ref[...] = result.astype(bf16)
    for index in range(sum_ref.shape[0] // SEG_LEN):
        cls_ref[0, index : index + 1, :] = result[index * SEG_LEN : index * SEG_LEN + 1, :]


def ffn_bwd_kernel(cot_ref, cls_ref, second_ref, sum_ref, slope_ref, up_ref, down_ref, vec_ref, branch_ref, inner_ref, first_ref, sums_ref):
    width = sum_ref.shape[1]

    @pl.when(pl.program_id(0) == 0)
    def _():
        sums_ref[...] = jnp.zeros_like(sums_ref)

    place = lax.broadcasted_iota(jnp.int32, (SEG_LEN, 1), 0) == 0
    parts = []
    for index in range(sum_ref.shape[0] // SEG_LEN):
        rows = cot_ref[index * SEG_LEN : (index + 1) * SEG_LEN, :].astype(f32)
        parts.append(rows + jnp.where(place, cls_ref[0, index : index + 1, :], 0.0))
    grad = jnp.concatenate(parts, 0)
    unit, inverse = normalise(second_ref[...])
    sums_ref[6:7, :] += column_sum(grad * unit)
    sums_ref[7:8, :] += column_sum(grad)
    second_grad = norm_back(grad, unit, inverse, vec_ref[6:7, :])
    branch = second_grad.astype(bf16)
    branch_ref[...] = branch
    sums_ref[5:6, :] += column_sum(branch.astype(f32))
    total = second_grad
    for part in range(4):
        cols = pl.ds(part * width, width)
        act_grad = dot_nn(branch, down_ref[:, cols])
        inner = (act_grad * slope_ref[:, cols].astype(f32)).astype(bf16)
        inner_ref[:, cols] = inner
        sums_ref[8 + part : 9 + part, :] += column_sum(inner.astype(f32))
        total = total + dot_nt(inner, up_ref[:, cols])
    unit, inverse = normalise(sum_ref[...])
    sums_ref[3:4, :] += column_sum(total * unit)
    sums_ref[4:5, :] += column_sum(total)
    first = norm_back(total, unit, inverse, vec_ref[3:4, :])
    first_ref[...] = first
    sums_ref[2:3, :] += column_sum(first.astype(bf16).astype(f32))


def attn_bwd_kernel(first_ref, qkv_ref, w_ref, low_ref, qkv_grad_ref, x_grad_ref, sums_ref, mixed_grad):
    width = first_ref.shape[1]

    @pl.when(pl.program_id(0) == 0)
    def _():
        sums_ref[...] = jnp.zeros_like(sums_ref)

    first = first_ref[...]
    low = first.astype(bf16)
    low_ref[...] = low
    mixed_grad[...] = dot_nt(low, w_ref[:, 3 * width :]).astype(bf16)
    for start in range(0, first_ref.shape[0], SEG_LEN):
        for pair in range(PAIRS):
            pair_backward(qkv_ref, mixed_grad, qkv_grad_ref, pl.ds(start, SEG_LEN), pair, width, None)
    qkv_grad = qkv_grad_ref[...]
    x_grad_ref[...] = first + dot_nt(qkv_grad, w_ref[:, : 3 * width])
    sums_ref[0:1, :] += column_sum(qkv_grad[:, :width].astype(f32))
    sums_ref[1:2, :] += column_sum(qkv_grad[:, 2 * width :].astype(f32))


def cross_kernel(
    x_ref, cot_ref, key_own_ref, key_all_ref, attn_ref, up_ref, down_ref, vec_ref,
    out_ref, x_grad_ref, low_in_ref, qkv_grad_ref, mixed_ref, attn_low_ref,
    norm_ref, inner_ref, branch_ref, act_ref, sums_ref,
    qkv_ref, mixed_grad, slope,
):
    width = x_ref.shape[1]
    count = x_ref.shape[0]
    rows = pl.ds(0, count)

    @pl.when(pl.program_id(0) == 0)
    def _():
        sums_ref[...] = jnp.zeros_like(sums_ref)

    same = key_own_ref[...] == key_all_ref[0]
    mask = jnp.concatenate([same, same], 0)
    entry = x_ref[...]
    low_in = entry.astype(bf16)
    low_in_ref[...] = low_in
    qkv = dot_nn(low_in, attn_ref[:, : 3 * width]) + qkv_bias(vec_ref)
    qkv_ref[...] = qkv.astype(bf16)
    for pair in range(PAIRS):
        pair_forward(qkv_ref, mixed_ref, rows, pair, width, mask)
    first_sum = entry + dot_nn(mixed_ref[...], attn_ref[:, 3 * width :]) + vec_ref[2:3, :]
    unit_one, inverse_one = normalise(first_sum)
    normed = unit_one * vec_ref[3:4, :] + vec_ref[4:5, :]
    low = normed.astype(bf16)
    norm_ref[...] = low
    total = normed + vec_ref[5:6, :]
    for part in range(4):
        cols = pl.ds(part * width, width)
        inner = dot_nn(low, up_ref[:, cols]) + vec_ref[8 + part : 9 + part, :]
        act, rate = gelu_parts(inner)
        act = act.astype(bf16)
        act_ref[:, cols] = act
        slope[:, cols] = rate
        total = total + dot_nt(act, down_ref[:, cols])
    unit_two, inverse_two = normalise(total)
    out_ref[...] = (unit_two * vec_ref[6:7, :] + vec_ref[7:8, :]).astype(bf16)

    grad = cot_ref[...].astype(f32)
    sums_ref[6:7, :] += column_sum(grad * unit_two)
    sums_ref[7:8, :] += column_sum(grad)
    second_grad = norm_back(grad, unit_two, inverse_two, vec_ref[6:7, :])
    branch = second_grad.astype(bf16)
    branch_ref[...] = branch
    sums_ref[5:6, :] += column_sum(branch.astype(f32))
    total = second_grad
    for part in range(4):
        cols = pl.ds(part * width, width)
        inner = (dot_nn(branch, down_ref[:, cols]) * slope[:, cols]).astype(bf16)
        inner_ref[:, cols] = inner
        sums_ref[8 + part : 9 + part, :] += column_sum(inner.astype(f32))
        total = total + dot_nt(inner, up_ref[:, cols])
    sums_ref[3:4, :] += column_sum(total * unit_one)
    sums_ref[4:5, :] += column_sum(total)
    first = norm_back(total, unit_one, inverse_one, vec_ref[3:4, :])
    attn_low = first.astype(bf16)
    attn_low_ref[...] = attn_low
    sums_ref[2:3, :] += column_sum(attn_low.astype(f32))
    mixed_grad[...] = dot_nt(attn_low, attn_ref[:, 3 * width :]).astype(bf16)
    for pair in range(PAIRS):
        pair_backward(qkv_ref, mixed_grad, qkv_grad_ref, rows, pair, width, mask)
    qkv_grad = qkv_grad_ref[...]
    x_grad_ref[...] = first + dot_nt(qkv_grad, attn_ref[:, : 3 * width])
    sums_ref[0:1, :] += column_sum(qkv_grad[:, :width].astype(f32))
    sums_ref[1:2, :] += column_sum(qkv_grad[:, 2 * width :].astype(f32))


def row_spec(width, block=BLOCK):
    return pl.BlockSpec((block, width), lambda i: (i, 0))


def whole_spec(shape):
    return pl.BlockSpec(shape, lambda i: (0,) * len(shape), pipeline_mode=pl.Buffered(1))


def fixed_spec(shape):
    return pl.BlockSpec(shape, lambda i: (0,) * len(shape))


def params():
    return pltpu.CompilerParams(dimension_semantics=("arbitrary",), vmem_limit_bytes=VMEM_LIMIT)


def shaped(*dims, dtype=bf16):
    return jax.ShapeDtypeStruct(dims, dtype)


def cost(flops, nbytes, trans=0):
    return pl.CostEstimate(flops=int(flops), bytes_accessed=int(nbytes), transcendentals=int(trans))


def attn_forward(flat, attn, vec):
    rows, width = flat.shape
    return pl.pallas_call(
        attn_fwd_kernel,
        grid=(rows // BLOCK,),
        in_specs=[row_spec(width), whole_spec(attn.shape), whole_spec(vec.shape)],
        out_specs=[row_spec(3 * width), row_spec(width), row_spec(width)],
        out_shape=[shaped(rows, 3 * width), shaped(rows, width), shaped(rows, width, dtype=f32)],
        compiler_params=params(),
        cost_estimate=cost(2 * rows * width * (4 * width + 2 * SEG_LEN), rows * width * 14 + attn.size * 2),
        name="seg_attn_fwd",
    )(flat, attn, vec)


def ffn_forward(first_sum, up_proj, down_proj, vec):
    rows, width = first_sum.shape
    inner = up_proj.shape[1]
    per = BLOCK // SEG_LEN
    cls_spec = pl.BlockSpec((1, per, width), lambda i: (i, 0, 0))
    return pl.pallas_call(
        ffn_fwd_kernel,
        grid=(rows // BLOCK,),
        in_specs=[row_spec(width), whole_spec(up_proj.shape), whole_spec(down_proj.shape), whole_spec(vec.shape)],
        out_specs=[row_spec(width), row_spec(inner), row_spec(inner), row_spec(width), row_spec(width), cls_spec],
        out_shape=[
            shaped(rows, width), shaped(rows, inner), shaped(rows, inner), shaped(rows, width, dtype=f32),
            shaped(rows, width), shaped(rows // BLOCK, per, width, dtype=f32),
        ],
        compiler_params=params(),
        cost_estimate=cost(4 * rows * width * inner, rows * (width * 12 + inner * 4) + up_proj.size * 4, 2 * rows * inner),
        name="seg_ffn_fwd",
    )(first_sum, up_proj, down_proj, vec)


def ffn_backward(cot, cls_grad, second_sum, first_sum, slope, up_proj, down_proj, vec):
    rows, width = first_sum.shape
    inner = up_proj.shape[1]
    per = BLOCK // SEG_LEN
    cls_spec = pl.BlockSpec((1, per, width), lambda i: (i, 0, 0))
    return pl.pallas_call(
        ffn_bwd_kernel,
        grid=(rows // BLOCK,),
        in_specs=[
            row_spec(width), cls_spec, row_spec(width), row_spec(width), row_spec(inner),
            whole_spec(up_proj.shape), whole_spec(down_proj.shape), whole_spec(vec.shape),
        ],
        out_specs=[row_spec(width), row_spec(inner), row_spec(width), fixed_spec(vec.shape)],
        out_shape=[
            shaped(rows, width), shaped(rows, inner), shaped(rows, width, dtype=f32), shaped(*vec.shape, dtype=f32),
        ],
        compiler_params=params(),
        cost_estimate=cost(4 * rows * width * inner, rows * (width * 16 + inner * 4) + up_proj.size * 4),
        name="seg_ffn_bwd",
    )(cot, cls_grad, second_sum, first_sum, slope, up_proj, down_proj, vec)


def attn_backward(first_grad, qkv, attn):
    rows, width = first_grad.shape
    return pl.pallas_call(
        attn_bwd_kernel,
        grid=(rows // BLOCK,),
        in_specs=[row_spec(width), row_spec(3 * width), whole_spec(attn.shape)],
        out_specs=[row_spec(width), row_spec(3 * width), row_spec(width), fixed_spec((8, width))],
        out_shape=[
            shaped(rows, width), shaped(rows, 3 * width), shaped(rows, width, dtype=f32), shaped(8, width, dtype=f32),
        ],
        scratch_shapes=[pltpu.VMEM((BLOCK, width), bf16)],
        compiler_params=params(),
        cost_estimate=cost(2 * rows * width * (4 * width + 5 * SEG_LEN), rows * width * 22 + attn.size * 2),
        name="seg_attn_bwd",
    )(first_grad, qkv, attn)


def cross_layer(entry, cot, row_key, blocks, attn, up_proj, down_proj, vec):
    rows, width = entry.shape
    inner = up_proj.shape[1]
    block = rows // blocks
    spec = partial(row_spec, block=block)
    return pl.pallas_call(
        cross_kernel,
        grid=(blocks,),
        in_specs=[
            spec(width), spec(width), spec(1), pl.BlockSpec((1, 1, block), lambda i: (i, 0, 0)),
            whole_spec(attn.shape), whole_spec(up_proj.shape), whole_spec(down_proj.shape), whole_spec(vec.shape),
        ],
        out_specs=[
            spec(width), spec(width), spec(width), spec(3 * width), spec(width), spec(width),
            spec(width), spec(inner), spec(width), spec(inner), fixed_spec(vec.shape),
        ],
        out_shape=[
            shaped(rows, width), shaped(rows, width, dtype=f32), shaped(rows, width), shaped(rows, 3 * width),
            shaped(rows, width), shaped(rows, width), shaped(rows, width), shaped(rows, inner),
            shaped(rows, width), shaped(rows, inner), shaped(*vec.shape, dtype=f32),
        ],
        scratch_shapes=[
            pltpu.VMEM((block, 3 * width), bf16), pltpu.VMEM((block, width), bf16), pltpu.VMEM((block, inner), f32),
        ],
        compiler_params=params(),
        cost_estimate=cost(24 * rows * width * 4 * width, rows * width * 40 + attn.size * 6),
        name="cross_layer",
    )(entry, cot, row_key.reshape(rows, 1), row_key.reshape(blocks, 1, block), attn, up_proj, down_proj, vec)


def spread_vec(columns):
    return jnp.concatenate([columns.astype(f32), jnp.zeros((4, columns.shape[1]), f32)], 0)


def gather_rows(matrix):
    return lax.all_gather(matrix, "seg", axis=0, tiled=True)


def scatter_sum(matrix):
    return lax.psum_scatter(matrix, "seg", scatter_dimension=0, tiled=True)


def local(
    hidden, seg_doc, seg_attn, seg_up, seg_down, seg_vec,
    cross_attn, cross_up, cross_down, cross_vec, tok_cot, cls_cot,
):
    micro, _, segments, _, length, width = hidden.shape
    own = seg_attn.shape[0]
    parts = lax.axis_size("seg")
    place = lax.axis_index("seg")
    count = micro * segments
    total = parts * count

    small = jnp.concatenate([cls_cot.reshape(count * width), seg_vec.T.reshape(-1), cross_vec.T.reshape(-1)])
    small = lax.all_gather(small, "seg", axis=0, tiled=False)
    cot_all = small[:, : count * width].reshape(total, width)
    vecs = small[:, count * width :].reshape(parts, 24, own).transpose(1, 0, 2).reshape(24, width)
    seg_vec_full = spread_vec(vecs[:12])
    cross_vec_full = spread_vec(vecs[12:])

    attn_full = gather_rows(seg_attn)
    up_full = gather_rows(seg_up)
    down_full = gather_rows(seg_down)
    cross_attn_full = gather_rows(cross_attn)
    cross_up_full = gather_rows(cross_up)
    cross_down_full = gather_rows(cross_down)

    flat = hidden.reshape(count * length, width)
    qkv, mixed, first_sum = attn_forward(flat, attn_full, seg_vec_full)
    normed, act, slope, second_sum, tok, cls = ffn_forward(first_sum, up_full, down_full, seg_vec_full)

    entry = lax.all_gather(cls.reshape(count, width), "seg", axis=0, tiled=True)
    docs = seg_doc[:, 0].reshape(micro, segments, parts) + (1 << 16) * jnp.arange(micro, dtype=jnp.int32)[:, None, None]
    blocks = micro if total > 256 else 1
    if blocks > 1:
        order = lambda rows: rows.reshape(parts, micro, segments, -1).transpose(1, 0, 2, 3).reshape(total, -1)
        back = lambda rows: rows.reshape(micro, parts, segments, -1).transpose(1, 0, 2, 3).reshape(total, -1)
        row_key = docs.transpose(0, 2, 1).reshape(total)
    else:
        order = back = lambda rows: rows
        row_key = docs.transpose(2, 0, 1).reshape(total)
    (
        cls_out, cls_grad, x_low, x_qkv_grad, x_mixed, x_attn_low, x_norm, x_inner, x_branch, x_act, x_sums,
    ) = cross_layer(
        order(entry), order(cot_all), row_key, blocks,
        cross_attn_full, cross_up_full, cross_down_full, cross_vec_full,
    )
    own_rows = lambda rows: lax.dynamic_slice_in_dim(back(rows), place * count, count, 0)
    own_cols = lambda rows: lax.dynamic_slice_in_dim(rows, place * own, own, 1)
    cls_out = own_rows(cls_out)
    cls_grad = own_rows(cls_grad)

    branch, inner, first_grad, ffn_sums = ffn_backward(
        tok_cot.reshape(count * length, width),
        cls_grad.reshape(cls.shape), second_sum, first_sum, slope, up_full, down_full, seg_vec_full,
    )
    down_grad = dot_tn(branch, act).astype(bf16)
    up_grad = dot_tn(normed, inner).astype(bf16)
    attn_low, qkv_grad, hidden_grad, attn_sums = attn_backward(first_grad, qkv, attn_full)
    attn_grad = jnp.concatenate([dot_tn(flat, qkv_grad), dot_tn(mixed, attn_low)], 1).astype(bf16)

    x_attn_grad = jnp.concatenate(
        [dot_tn(own_cols(x_low), x_qkv_grad), dot_tn(own_cols(x_mixed), x_attn_low)], 1
    )
    x_up_grad = dot_tn(own_cols(x_norm), x_inner)
    x_down_grad = dot_tn(own_cols(x_branch), x_act)

    sums = jnp.concatenate([attn_sums[:2], ffn_sums[2:12]], 0)
    vec_sums = scatter_sum(jnp.stack(jnp.split(sums, parts, 1)).astype(bf16))[0]
    vec_all = jnp.concatenate([vec_sums.astype(f32), own_cols(x_sums[:12])], 0)

    seg_parts = [scatter_sum(down_grad), scatter_sum(up_grad), scatter_sum(attn_grad)]
    down_sum, up_sum, attn_sum, x_down_sum, x_up_sum, x_attn_sum, vec_all = lax.psum(
        (
            seg_parts[0], seg_parts[1], seg_parts[2],
            x_down_grad.astype(bf16), x_up_grad.astype(bf16), x_attn_grad.astype(bf16), vec_all.astype(bf16),
        ),
        "batch",
    )
    vec_all = vec_all.astype(f32)
    return (
        tok.reshape(hidden.shape),
        cls_out.reshape(cls_cot.shape),
        hidden_grad.reshape(hidden.shape),
        attn_sum.astype(f32), up_sum.astype(f32), down_sum.astype(f32), vec_all[:12].T,
        x_attn_sum.astype(f32), x_up_sum.astype(f32), x_down_sum.astype(f32), vec_all[12:].T,
    )


def solution(mesh):
    wide = P(None, "batch", None, "seg", None, None)
    rows = P("seg", None)
    cls = P(None, "batch", None, "seg", None)
    in_specs = (wide, P(None, "batch", None)) + (rows,) * 8 + (wide, cls)
    out_specs = (wide, cls, wide) + (rows,) * 8
    return jax.shard_map(local, mesh=mesh, in_specs=in_specs, out_specs=out_specs, check_vma=False)
```

```python
from functools import partial

import jax
import jax.numpy as jnp
from jax import lax
from jax.experimental import pallas as pl
from jax.experimental.pallas import tpu as pltpu
from jax.sharding import PartitionSpec as P

HEADS = 12
HEAD_DIM = 64
SEG_LEN = 128
PAIRS = HEADS // 2
PAIR = 2 * HEAD_DIM

NEG_FILL = -1e30
LN_EPS = 1e-05
SCALE = HEAD_DIM ** (-0.5)
ROOT_HALF = 0.7071067811865476
PDF_AT_ZERO = 0.3989422804014327
BLOCK = 256
VMEM_LIMIT = 60 * 1024 * 1024

f32 = jnp.float32
bf16 = jnp.bfloat16


def dot_nn(left, right):
    return lax.dot_general(left, right, (((1,), (0,)), ((), ())), preferred_element_type=f32)


def dot_nt(left, right):
    return lax.dot_general(left, right, (((1,), (1,)), ((), ())), preferred_element_type=f32)


def dot_tn(left, right):
    return lax.dot_general(left, right, (((0,), (0,)), ((), ())), preferred_element_type=f32)


def normalise(rows):
    centred = rows - jnp.mean(rows, -1, keepdims=True)
    spread = jnp.mean(centred * centred, -1, keepdims=True)
    inverse = lax.rsqrt(spread + LN_EPS)
    return centred * inverse, inverse


def norm_back(grad, unit, inverse, gain):
    scaled = grad * gain
    return inverse * (
        scaled
        - jnp.mean(scaled, -1, keepdims=True)
        - unit * jnp.mean(scaled * unit, -1, keepdims=True)
    )


def column_sum(rows):
    return jnp.sum(rows, 0, keepdims=True)


def gelu_parts(value):
    cdf = 0.5 * (1.0 + lax.erf(value * ROOT_HALF))
    pdf = PDF_AT_ZERO * jnp.exp(-0.5 * value * value)
    return value * cdf, cdf + value * pdf


def first_half(rows):
    return lax.broadcasted_iota(jnp.int32, (rows, PAIR), 1) < HEAD_DIM


def split_heads(rows, first):
    zero = jnp.zeros_like(rows)
    return jnp.concatenate([jnp.where(first, rows, zero), jnp.where(first, zero, rows)], 0)


def join_heads(stacked, first):
    rows = stacked.shape[0] // 2
    return jnp.where(first, stacked[:rows], stacked[rows:])


def pair_probs(query, keys, mask):
    scores = dot_nt(query, keys) * SCALE
    if mask is not None:
        scores = jnp.where(mask, scores, NEG_FILL)
    top = jnp.max(scores, -1, keepdims=True)
    expo = jnp.exp(scores - top)
    return expo * (1.0 / jnp.sum(expo, -1, keepdims=True))


def pair_forward(qkv_ref, out_ref, rows, pair, width, mask):
    first = first_half(rows.size)
    at = pair * PAIR
    query = split_heads(qkv_ref[rows, at : at + PAIR], first)
    keys = qkv_ref[rows, width + at : width + at + PAIR]
    values = qkv_ref[rows, 2 * width + at : 2 * width + at + PAIR]
    probs = pair_probs(query, keys, mask)
    mixed = join_heads(dot_nn(probs.astype(bf16), values), first)
    out_ref[rows, at : at + PAIR] = mixed.astype(bf16)


def pair_backward(qkv_ref, grad_ref, out_ref, rows, pair, width, mask):
    first = first_half(rows.size)
    at = pair * PAIR
    query = split_heads(qkv_ref[rows, at : at + PAIR], first)
    keys = qkv_ref[rows, width + at : width + at + PAIR]
    values = qkv_ref[rows, 2 * width + at : 2 * width + at + PAIR]
    out_grad = split_heads(grad_ref[rows, at : at + PAIR], first)
    probs = pair_probs(query, keys, mask)
    value_grad = dot_tn(probs.astype(bf16), out_grad)
    prob_grad = dot_nt(out_grad, values)
    score_grad = probs * (prob_grad - jnp.sum(prob_grad * probs, -1, keepdims=True))
    score_grad = score_grad.astype(bf16)
    query_grad = join_heads(dot_nn(score_grad, keys), first) * SCALE
    key_grad = dot_tn(score_grad, query) * SCALE
    out_ref[rows, at : at + PAIR] = query_grad.astype(bf16)
    out_ref[rows, width + at : width + at + PAIR] = key_grad.astype(bf16)
    out_ref[rows, 2 * width + at : 2 * width + at + PAIR] = value_grad.astype(bf16)


class Pieces:
    def __init__(self, shape, arrays, blocks):
        self.shape, self.arrays, self.blocks = shape, arrays, blocks

    def specs(self):
        return [pl.BlockSpec(memory_space=pl.ANY)] * len(self.arrays)

    def scratch(self):
        return [pltpu.VMEM(self.shape, bf16), pltpu.SemaphoreType.DMA((len(self.blocks),))]

    def copies(self, refs, place_ref, full_ref, sems):
        out = []
        for at, (index, source, size, target) in enumerate(self.blocks):
            row, col = target(place_ref[0], place_ref[1], place_ref[2])
            if not isinstance(row, int):
                row = pl.multiple_of(row, size[0])
            if not isinstance(col, int):
                col = pl.multiple_of(col, size[1])
            view = full_ref.at[pl.ds(row, size[0]), pl.ds(col, size[1])]
            out.append(pltpu.make_async_copy(refs[index].at[source], view, sems.at[at]))
        return out


class Weights:
    def __init__(self, *matrices):
        self.matrices = matrices

    def arrays(self, place):
        return [place] + [array for matrix in self.matrices for array in matrix.arrays]

    def specs(self):
        return [pl.BlockSpec(memory_space=pltpu.SMEM)] + [spec for matrix in self.matrices for spec in matrix.specs()]

    def scratch(self):
        return [item for matrix in self.matrices for item in matrix.scratch()]

    def wrap(self, body, step_axis=0):
        many = sum(len(matrix.arrays) for matrix in self.matrices)

        def kernel(place_ref, *refs):
            given, rest = refs[:many], refs[many:]
            cut = len(rest) - 2 * len(self.matrices)
            rest, own = rest[:cut], rest[cut:]
            first = pl.program_id(step_axis) == 0
            views, copies = [], []
            for at, matrix in enumerate(self.matrices):
                views.append(own[2 * at])
                copies.append(partial(matrix.copies, given[: len(matrix.arrays)], place_ref, own[2 * at], own[2 * at + 1]))
                given = given[len(matrix.arrays) :]

            @pl.when(first)
            def _():
                for group in copies:
                    for copy in group():
                        copy.start()

            def ready(at):
                @pl.when(first)
                def _():
                    for copy in copies[at]():
                        copy.wait()

                return views[at]

            body(ready, *rest)

        return kernel


def qkv_bias(vec_ref):
    query = vec_ref[0:1, :]
    return jnp.concatenate([query, jnp.zeros_like(query), vec_ref[1:2, :]], 1)


def attn_fwd_kernel(ready, x_ref, vec_ref, qkv_ref, mixed_ref, sum_ref):
    width = x_ref.shape[1]
    w_ref = ready(0)
    rows = x_ref[...]
    qkv = dot_nn(rows, w_ref[:, : 3 * width]) + qkv_bias(vec_ref)
    qkv_ref[...] = qkv.astype(bf16)
    for start in range(0, x_ref.shape[0], SEG_LEN):
        for pair in range(PAIRS):
            pair_forward(qkv_ref, mixed_ref, pl.ds(start, SEG_LEN), pair, width, None)
    branch = dot_nn(mixed_ref[...], w_ref[:, 3 * width :])
    sum_ref[...] = rows.astype(f32) + branch + vec_ref[2:3, :]


def ffn_fwd_kernel(ready, sum_ref, vec_ref, norm_ref, act_ref, slope_ref, second_ref, tok_ref, cls_ref):
    width = sum_ref.shape[1]
    up_ref = ready(0)
    down_ref = ready(1)
    unit, _ = normalise(sum_ref[...])
    normed = unit * vec_ref[3:4, :] + vec_ref[4:5, :]
    low = normed.astype(bf16)
    norm_ref[...] = low
    total = normed + vec_ref[5:6, :]
    for part in range(4):
        cols = pl.ds(part * width, width)
        inner = dot_nn(low, up_ref[:, cols]) + vec_ref[8 + part : 9 + part, :]
        act, slope = gelu_parts(inner)
        act = act.astype(bf16)
        act_ref[:, cols] = act
        slope_ref[:, cols] = slope.astype(bf16)
        total = total + dot_nt(act, down_ref[:, cols])
    second_ref[...] = total
    unit, _ = normalise(total)
    result = unit * vec_ref[6:7, :] + vec_ref[7:8, :]
    tok_ref[...] = result.astype(bf16)
    for index in range(sum_ref.shape[0] // SEG_LEN):
        cls_ref[0, index : index + 1, :] = result[index * SEG_LEN : index * SEG_LEN + 1, :]


def ffn_bwd_kernel(ready, cot_ref, cls_ref, second_ref, sum_ref, slope_ref, vec_ref, branch_ref, inner_ref, first_ref, low_ref, sums_ref):
    width = sum_ref.shape[1]

    @pl.when(pl.program_id(0) == 0)
    def _():
        sums_ref[...] = jnp.zeros_like(sums_ref)

    place = lax.broadcasted_iota(jnp.int32, (SEG_LEN, 1), 0) == 0
    parts = []
    for index in range(sum_ref.shape[0] // SEG_LEN):
        rows = cot_ref[index * SEG_LEN : (index + 1) * SEG_LEN, :].astype(f32)
        parts.append(rows + jnp.where(place, cls_ref[0, index : index + 1, :], 0.0))
    grad = jnp.concatenate(parts, 0)
    unit, inverse = normalise(second_ref[...])
    sums_ref[6:7, :] += column_sum(grad * unit)
    sums_ref[7:8, :] += column_sum(grad)
    second_grad = norm_back(grad, unit, inverse, vec_ref[6:7, :])
    branch = second_grad.astype(bf16)
    branch_ref[...] = branch
    sums_ref[5:6, :] += column_sum(branch.astype(f32))
    up_ref = ready(0)
    down_ref = ready(1)
    total = second_grad
    for part in range(4):
        cols = pl.ds(part * width, width)
        act_grad = dot_nn(branch, down_ref[:, cols])
        inner = (act_grad * slope_ref[:, cols].astype(f32)).astype(bf16)
        inner_ref[:, cols] = inner
        sums_ref[8 + part : 9 + part, :] += column_sum(inner.astype(f32))
        total = total + dot_nt(inner, up_ref[:, cols])
    unit, inverse = normalise(sum_ref[...])
    sums_ref[3:4, :] += column_sum(total * unit)
    sums_ref[4:5, :] += column_sum(total)
    first = norm_back(total, unit, inverse, vec_ref[3:4, :])
    first_ref[...] = first
    low = first.astype(bf16)
    low_ref[...] = low
    sums_ref[2:3, :] += column_sum(low.astype(f32))


def attn_bwd_kernel(ready, first_ref, low_ref, qkv_ref, qkv_grad_ref, x_grad_ref, sums_ref, mixed_grad):
    width = first_ref.shape[1]

    @pl.when(pl.program_id(0) == 0)
    def _():
        sums_ref[...] = jnp.zeros_like(sums_ref)

    w_ref = ready(0)
    mixed_grad[...] = dot_nt(low_ref[...], w_ref[:, 3 * width :]).astype(bf16)
    for start in range(0, first_ref.shape[0], SEG_LEN):
        for pair in range(PAIRS):
            pair_backward(qkv_ref, mixed_grad, qkv_grad_ref, pl.ds(start, SEG_LEN), pair, width, None)
    qkv_grad = qkv_grad_ref[...]
    x_grad_ref[...] = first_ref[...] + dot_nt(qkv_grad, w_ref[:, : 3 * width])
    sums_ref[0:1, :] += column_sum(qkv_grad[:, :width].astype(f32))
    sums_ref[1:2, :] += column_sum(qkv_grad[:, 2 * width :].astype(f32))


def cross_kernel(
    ready, x_ref, cot_ref, key_own_ref, key_all_ref, vec_ref,
    out_ref, x_grad_ref, low_in_ref, qkv_grad_ref, mixed_ref, attn_low_ref,
    norm_ref, inner_ref, branch_ref, act_ref, sums_ref,
    qkv_ref, mixed_grad, slope,
):
    width = x_ref.shape[1]
    count = x_ref.shape[0]
    rows = pl.ds(0, count)

    @pl.when(pl.program_id(0) == 0)
    def _():
        sums_ref[...] = jnp.zeros_like(sums_ref)

    attn_ref = ready(0)
    same = key_own_ref[...] == key_all_ref[0]
    mask = jnp.concatenate([same, same], 0)
    entry = x_ref[...]
    low_in = entry.astype(bf16)
    low_in_ref[...] = low_in
    qkv = dot_nn(low_in, attn_ref[:, : 3 * width]) + qkv_bias(vec_ref)
    qkv_ref[...] = qkv.astype(bf16)
    for pair in range(PAIRS):
        pair_forward(qkv_ref, mixed_ref, rows, pair, width, mask)
    first_sum = entry + dot_nn(mixed_ref[...], attn_ref[:, 3 * width :]) + vec_ref[2:3, :]
    unit_one, inverse_one = normalise(first_sum)
    normed = unit_one * vec_ref[3:4, :] + vec_ref[4:5, :]
    low = normed.astype(bf16)
    norm_ref[...] = low
    up_ref = ready(1)
    down_ref = ready(2)
    total = normed + vec_ref[5:6, :]
    for part in range(4):
        cols = pl.ds(part * width, width)
        inner = dot_nn(low, up_ref[:, cols]) + vec_ref[8 + part : 9 + part, :]
        act, rate = gelu_parts(inner)
        act = act.astype(bf16)
        act_ref[:, cols] = act
        slope[:, cols] = rate
        total = total + dot_nt(act, down_ref[:, cols])
    unit_two, inverse_two = normalise(total)
    out_ref[...] = (unit_two * vec_ref[6:7, :] + vec_ref[7:8, :]).astype(bf16)

    grad = cot_ref[...].astype(f32)
    sums_ref[6:7, :] += column_sum(grad * unit_two)
    sums_ref[7:8, :] += column_sum(grad)
    second_grad = norm_back(grad, unit_two, inverse_two, vec_ref[6:7, :])
    branch = second_grad.astype(bf16)
    branch_ref[...] = branch
    sums_ref[5:6, :] += column_sum(branch.astype(f32))
    total = second_grad
    for part in range(4):
        cols = pl.ds(part * width, width)
        inner = (dot_nn(branch, down_ref[:, cols]) * slope[:, cols]).astype(bf16)
        inner_ref[:, cols] = inner
        sums_ref[8 + part : 9 + part, :] += column_sum(inner.astype(f32))
        total = total + dot_nt(inner, up_ref[:, cols])
    sums_ref[3:4, :] += column_sum(total * unit_one)
    sums_ref[4:5, :] += column_sum(total)
    first = norm_back(total, unit_one, inverse_one, vec_ref[3:4, :])
    attn_low = first.astype(bf16)
    attn_low_ref[...] = attn_low
    sums_ref[2:3, :] += column_sum(attn_low.astype(f32))
    mixed_grad[...] = dot_nt(attn_low, attn_ref[:, 3 * width :]).astype(bf16)
    for pair in range(PAIRS):
        pair_backward(qkv_ref, mixed_grad, qkv_grad_ref, rows, pair, width, mask)
    qkv_grad = qkv_grad_ref[...]
    x_grad_ref[...] = first + dot_nt(qkv_grad, attn_ref[:, : 3 * width])
    sums_ref[0:1, :] += column_sum(qkv_grad[:, :width].astype(f32))
    sums_ref[1:2, :] += column_sum(qkv_grad[:, 2 * width :].astype(f32))


def row_spec(width, block=BLOCK):
    return pl.BlockSpec((block, width), lambda i: (i, 0))


def whole_spec(shape):
    return pl.BlockSpec(shape, lambda i: (0,) * len(shape), pipeline_mode=pl.Buffered(1))


def fixed_spec(shape):
    return pl.BlockSpec(shape, lambda i: (0,) * len(shape))


def params():
    return pltpu.CompilerParams(dimension_semantics=("arbitrary",), vmem_limit_bytes=VMEM_LIMIT)


def shaped(*dims, dtype=bf16):
    return jax.ShapeDtypeStruct(dims, dtype)


def cost(flops, nbytes, trans=0):
    return pl.CostEstimate(flops=int(flops), bytes_accessed=int(nbytes), transcendentals=int(trans))


def attn_forward(flat, place, attn, vec):
    rows, width = flat.shape
    weights = Weights(attn)
    return pl.pallas_call(
        weights.wrap(attn_fwd_kernel),
        grid=(rows // BLOCK,),
        in_specs=weights.specs() + [row_spec(width), whole_spec(vec.shape)],
        out_specs=[row_spec(3 * width), row_spec(width), row_spec(width)],
        out_shape=[shaped(rows, 3 * width), shaped(rows, width), shaped(rows, width, dtype=f32)],
        scratch_shapes=weights.scratch(),
        compiler_params=params(),
        cost_estimate=cost(2 * rows * width * (4 * width + 2 * SEG_LEN), rows * width * 14 + width * width * 8),
        name="seg_attn_fwd",
    )(*weights.arrays(place), flat, vec)


def ffn_forward(first_sum, place, up_proj, down_proj, vec):
    rows, width = first_sum.shape
    inner = up_proj.shape[1]
    per = BLOCK // SEG_LEN
    weights = Weights(up_proj, down_proj)
    cls_spec = pl.BlockSpec((1, per, width), lambda i: (i, 0, 0))
    return pl.pallas_call(
        weights.wrap(ffn_fwd_kernel),
        grid=(rows // BLOCK,),
        in_specs=weights.specs() + [row_spec(width), whole_spec(vec.shape)],
        out_specs=[row_spec(width), row_spec(inner), row_spec(inner), row_spec(width), row_spec(width), cls_spec],
        out_shape=[
            shaped(rows, width), shaped(rows, inner), shaped(rows, inner), shaped(rows, width, dtype=f32),
            shaped(rows, width), shaped(rows // BLOCK, per, width, dtype=f32),
        ],
        scratch_shapes=weights.scratch(),
        compiler_params=params(),
        cost_estimate=cost(4 * rows * width * inner, rows * (width * 12 + inner * 4) + width * inner * 4, 2 * rows * inner),
        name="seg_ffn_fwd",
    )(*weights.arrays(place), first_sum, vec)


def ffn_backward(cot, cls_grad, second_sum, first_sum, slope, place, up_proj, down_proj, vec):
    rows, width = first_sum.shape
    inner = up_proj.shape[1]
    per = BLOCK // SEG_LEN
    weights = Weights(up_proj, down_proj)
    cls_spec = pl.BlockSpec((1, per, width), lambda i: (i, 0, 0))
    return pl.pallas_call(
        weights.wrap(ffn_bwd_kernel),
        grid=(rows // BLOCK,),
        in_specs=weights.specs() + [
            row_spec(width), cls_spec, row_spec(width), row_spec(width), row_spec(inner), whole_spec(vec.shape),
        ],
        out_specs=[row_spec(width), row_spec(inner), row_spec(width), row_spec(width), fixed_spec(vec.shape)],
        out_shape=[
            shaped(rows, width), shaped(rows, inner), shaped(rows, width, dtype=f32), shaped(rows, width),
            shaped(*vec.shape, dtype=f32),
        ],
        scratch_shapes=weights.scratch(),
        compiler_params=params(),
        cost_estimate=cost(4 * rows * width * inner, rows * (width * 16 + inner * 4) + width * inner * 4),
        name="seg_ffn_bwd",
    )(*weights.arrays(place), cot, cls_grad, second_sum, first_sum, slope, vec)


def attn_backward(first_grad, attn_low, qkv, place, attn):
    rows, width = first_grad.shape
    weights = Weights(attn)
    return pl.pallas_call(
        weights.wrap(attn_bwd_kernel),
        grid=(rows // BLOCK,),
        in_specs=weights.specs() + [row_spec(width), row_spec(width), row_spec(3 * width)],
        out_specs=[row_spec(3 * width), row_spec(width), fixed_spec((8, width))],
        out_shape=[shaped(rows, 3 * width), shaped(rows, width, dtype=f32), shaped(8, width, dtype=f32)],
        scratch_shapes=[pltpu.VMEM((BLOCK, width), bf16)] + weights.scratch(),
        compiler_params=params(),
        cost_estimate=cost(2 * rows * width * (4 * width + 5 * SEG_LEN), rows * width * 22 + width * width * 8),
        name="seg_attn_bwd",
    )(*weights.arrays(place), first_grad, attn_low, qkv)


def cross_layer(entry, cot, row_key, blocks, place, attn, up_proj, down_proj, vec):
    rows, width = entry.shape
    inner = up_proj.shape[1]
    block = rows // blocks
    spec = partial(row_spec, block=block)
    weights = Weights(attn, up_proj, down_proj)
    return pl.pallas_call(
        weights.wrap(cross_kernel),
        grid=(blocks,),
        in_specs=weights.specs() + [
            spec(width), spec(width), spec(1), pl.BlockSpec((1, 1, block), lambda i: (i, 0, 0)), whole_spec(vec.shape),
        ],
        out_specs=[
            spec(width), spec(width), spec(width), spec(3 * width), spec(width), spec(width),
            spec(width), spec(inner), spec(width), spec(inner), fixed_spec(vec.shape),
        ],
        out_shape=[
            shaped(rows, width), shaped(rows, width, dtype=f32), shaped(rows, width), shaped(rows, 3 * width),
            shaped(rows, width), shaped(rows, width), shaped(rows, width), shaped(rows, inner),
            shaped(rows, width), shaped(rows, inner), shaped(*vec.shape, dtype=f32),
        ],
        scratch_shapes=[
            pltpu.VMEM((block, 3 * width), bf16), pltpu.VMEM((block, width), bf16), pltpu.VMEM((block, inner), f32),
        ] + weights.scratch(),
        compiler_params=params(),
        cost_estimate=cost(24 * rows * width * 4 * width, rows * width * 40 + width * inner * 6),
        name="cross_layer",
    )(*weights.arrays(place), entry, cot, row_key.reshape(rows, 1), row_key.reshape(blocks, 1, block), vec)


def spread_vec(columns):
    return jnp.concatenate([columns.astype(f32), jnp.zeros((4, columns.shape[1]), f32)], 0)


def hop_seg(value, hops):
    size = lax.axis_size("seg")
    return lax.ppermute(value, "seg", [(at, (at + 2 * hops) % size) for at in range(size)])


def swap_core(value):
    return lax.ppermute(value, "seg", [(at, at ^ 1) for at in range(lax.axis_size("seg"))])


def swap_batch(value, flip):
    return lax.ppermute(value, "batch", [(at, at ^ flip) for at in range(lax.axis_size("batch"))])


def fence(*values):
    return lax.optimization_barrier(values)


def by_links():
    return lax.axis_size("batch") == 4 and lax.axis_size("seg") == 8


class Gather:
    def __init__(self, *shards):
        self.many = len(shards)
        self.own, self.cols = shards[0].shape
        self.quarter = self.cols // 4
        self.mine = jnp.concatenate(shards, 0) if self.many > 1 else shards[0]
        self.part = lax.dynamic_slice_in_dim(self.mine, lax.axis_index("batch") * self.quarter, self.quarter, 1)

    def run_seg(self, direct):
        if direct:
            self.along = jnp.stack([hop_seg(self.part, hops) for hops in (3, 2, 1)])
        else:
            full = chips_exchange(jnp.broadcast_to(self.part, (4,) + self.part.shape))
            self.along = lax.dynamic_slice_in_dim(jnp.concatenate([full, full[:3]], 0), lax.axis_index("seg") // 2 + 1, 3)
        self.mine_too = swap_core(self.mine)

    def run_batch(self):
        self.over = [swap_batch(self.along, flip) for flip in (1, 2, 3)]

    def run_core(self):
        self.over = jnp.stack([self.along] + self.over)
        self.over_too = swap_core(self.over)

    def pieces(self):
        own, cols, quarter = self.own, self.cols, self.quarter
        arrays = [self.mine, self.over, self.mine_too, self.over_too]
        matrices = []
        for at in range(self.many):
            lines = slice(at * own, (at + 1) * own)
            blocks = []
            for core in (0, 1):
                target = lambda z, c, q, core=core: ((z * 2 + (c ^ core)) * own, 0)
                blocks.append((2 * core, (lines, slice(None)), (own, cols), target))
                for flip in range(4):
                    for later in range(3):
                        target = lambda z, c, q, core=core, flip=flip, later=later: (
                            (((z + 1 + later) & 3) * 2 + (c ^ core)) * own, (q ^ flip) * quarter
                        )
                        blocks.append((2 * core + 1, (flip, later, lines, slice(None)), (own, quarter), target))
            matrices.append(Pieces((own * lax.axis_size("seg"), cols), arrays, blocks))
        return matrices


def gather_plain(shard):
    full = lax.all_gather(shard, "seg", axis=0, tiled=True)
    block = (0, (slice(None), slice(None)), full.shape, lambda z, c, q: (0, 0))
    return Pieces(full.shape, [full], [block])


def swap_seg(value, flip):
    return lax.ppermute(value, "seg", [(at, at ^ flip) for at in range(lax.axis_size("seg"))])


def chips_exchange(value):
    groups = [[0, 2, 4, 6], [1, 3, 5, 7]]
    return lax.all_to_all(value, "seg", 0, 0, axis_index_groups=groups, tiled=True)


def gather_seg(value):
    if not by_links():
        return lax.all_gather(value, "seg", axis=0, tiled=False)
    copies = jnp.broadcast_to(value, (lax.axis_size("seg"),) + value.shape)
    return lax.all_to_all(copies, "seg", 0, 0, tiled=True)


def weight_grad_kernel(steps, place_ref, *refs):
    pairs, (keep_ref, send_ref, acc_ref) = refs[: 2 * len(steps)], refs[2 * len(steps) :]
    step = pl.program_id(0)
    begin = 0
    for at, many in enumerate(steps):

        @pl.when((step >= begin) & (step < begin + many))
        def _(at=at):
            acc_ref[...] = dot_tn(pairs[2 * at][...], pairs[2 * at + 1][...])

        begin += many
    c, q = place_ref[1], place_ref[2]
    size = keep_ref.shape[2]
    for flip in range(4):
        for chip in range(4):
            for core, out_ref in ((0, keep_ref), (1, send_ref)):
                row = (chip * 2 + (c ^ core)) * (4 * size) + (q ^ flip) * size
                rows = pl.ds(pl.multiple_of(row, size), size)
                out_ref[flip, chip] = acc_ref[rows, :].astype(bf16)


def weight_grads(place, *pairs):
    rows, width = pairs[0][0].shape
    steps = tuple(right.shape[1] // width for _, right in pairs)
    size = width // 32
    in_specs = [pl.BlockSpec(memory_space=pltpu.SMEM)]
    begin = 0
    for many in steps:
        in_specs.append(whole_spec((rows, width)))
        in_specs.append(pl.BlockSpec((rows, width), lambda i, begin=begin, many=many: (0, jnp.clip(i - begin, 0, many - 1))))
        begin += many
    out_spec = pl.BlockSpec((4, 4, size, width), lambda i: (0, 0, 0, i))
    out = shaped(4, 4, size, begin * width)
    return pl.pallas_call(
        partial(weight_grad_kernel, steps),
        grid=(begin,),
        in_specs=in_specs,
        out_specs=[out_spec, out_spec],
        out_shape=[out, out],
        scratch_shapes=[pltpu.VMEM((width, width), f32)],
        compiler_params=params(),
        cost_estimate=cost(2 * rows * width * width * begin, 2 * (rows + width) * width * begin),
        name="weight_grads",
    )(place, *[array for pair in pairs for array in pair])


def cross_grad_kernel(*refs):
    pairs, (out_ref,) = refs[:8], refs[8:]
    size = out_ref.shape[1]
    start = 0
    for at in range(4):
        cols = pairs[2 * at + 1].shape[1]
        grad = dot_tn(pairs[2 * at][...], pairs[2 * at + 1][...]).astype(bf16)
        for part in range(4):
            out_ref[part, :, start : start + cols] = grad[part * size : (part + 1) * size]
        start += cols


def cross_grads(*pairs):
    own = pairs[0][0].shape[1]
    cols = sum(right.shape[1] for _, right in pairs)
    vmem = pl.BlockSpec(memory_space=pltpu.VMEM)
    return pl.pallas_call(
        cross_grad_kernel,
        in_specs=[vmem] * 8,
        out_specs=vmem,
        out_shape=shaped(4, own // 4, cols),
        compiler_params=pltpu.CompilerParams(vmem_limit_bytes=VMEM_LIMIT),
        cost_estimate=cost(2 * pairs[0][0].size * cols, own * cols * 2),
        name="cross_weight_grads",
    )(*[array for pair in pairs for array in pair])


def wide_sum(first, *others):
    total = first.astype(f32)
    for other in others:
        total = total + other.astype(f32)
    return total


def batch_spread(value):
    value = value.astype(bf16)
    return [value] + [swap_batch(value, flip) for flip in (1, 2, 3)]


def core_sums(keep, got):
    sums = [wide_sum(keep[flip], got[flip]) for flip in range(4)]
    return sums[0], [part.astype(bf16) for part in sums[1:]]


def batch_swaps(parts):
    return [swap_batch(part, flip) for flip, part in zip((1, 2, 3), parts)]


def chip_sum(value):
    return jnp.sum(chips_exchange(value.astype(bf16)).astype(f32), 0)


def place_kernel(plan, place_ref, *refs):
    count = 4 * len(plan)
    blocks, outs = refs[:count], refs[count:]
    q = place_ref[2]
    for at, targets in enumerate(plan):
        for flip in range(4):
            block = blocks[4 * at + flip]
            size = block.shape[0]
            rows = pl.ds(pl.multiple_of((q ^ flip) * size, size), size)
            for source, index, target, cols in targets:
                outs[index][rows, target : target + cols] = block[:, source : source + cols].astype(f32)


def place_outputs(place, plan, groups, own, shape):
    vmem = pl.BlockSpec(memory_space=pltpu.VMEM)
    return pl.pallas_call(
        partial(place_kernel, plan),
        in_specs=[pl.BlockSpec(memory_space=pltpu.SMEM)] + [vmem] * (4 * len(groups)),
        out_specs=[vmem] * own,
        out_shape=[jax.ShapeDtypeStruct(shape, f32)] * own,
        compiler_params=pltpu.CompilerParams(vmem_limit_bytes=VMEM_LIMIT),
        cost_estimate=cost(0, own * shape[0] * shape[1] * 6),
        name="place_outputs",
    )(place, *[block for group in groups for block in group])


def scatter_sum(matrix):
    return lax.psum_scatter(matrix.astype(bf16), "seg", scatter_dimension=0, tiled=True)


def sum_everywhere(seg_sums, cross_sums):
    if not by_links():
        return lax.psum(seg_sums, ("batch", "seg")), lax.psum(cross_sums, "batch")
    for flip in (1, 2, 4):
        seg_sums = seg_sums + swap_seg(seg_sums, flip)
    both = jnp.concatenate([seg_sums, cross_sums], 0)
    for flip in (1, 2):
        both = both + swap_batch(both, flip)
    return both[: seg_sums.shape[0]], both[seg_sums.shape[0] :]


def local(
    hidden, seg_doc, seg_attn, seg_up, seg_down, seg_vec,
    cross_attn, cross_up, cross_down, cross_vec, tok_cot, cls_cot,
):
    micro, _, segments, _, length, width = hidden.shape
    own, cols = seg_attn.shape
    parts = lax.axis_size("seg")
    place = lax.axis_index("seg")
    count = micro * segments
    total = parts * count
    spot = jnp.stack([place // 2, place % 2, lax.axis_index("batch")]).astype(jnp.int32)

    flat = hidden.reshape(count * length, width)
    small = jnp.concatenate([cls_cot.reshape(count * width), seg_vec.T.reshape(-1), cross_vec.T.reshape(-1)])

    def spread_small(small):
        cot_all = small[:, : count * width].reshape(total, width)
        vecs = small[:, count * width :].reshape(parts, 24, own).transpose(1, 0, 2).reshape(24, width)
        return cot_all, spread_vec(vecs[:12]), spread_vec(vecs[12:])

    if by_links():
        one, two, three, four = Gather(seg_attn), Gather(seg_up, seg_down), Gather(cross_attn, cross_up), Gather(cross_down)
        one.run_seg(True)
        small = gather_seg(small)
        one.along, small, two.part, two.mine = fence(one.along, small, two.part, two.mine)
        cot_all, seg_vec_full, cross_vec_full = spread_small(small)
        one.run_batch()
        two.run_seg(False)
        one.over, two.along, three.part, three.mine = fence(one.over, two.along, three.part, three.mine)
        one.run_core()
        two.run_batch()
        three.run_seg(False)
        (attn_full,) = one.pieces()
        outs = attn_forward(flat, spot, attn_full, seg_vec_full)
        (qkv, mixed, first_sum), two.over, three.along, four.part, four.mine = fence(
            outs, two.over, three.along, four.part, four.mine
        )
        two.run_core()
        three.run_batch()
        four.run_seg(False)
        up_full, down_full = two.pieces()
        outs = ffn_forward(first_sum, spot, up_full, down_full, seg_vec_full)
        (normed, act, slope, second_sum, tok, cls), three.over, four.along = fence(outs, three.over, four.along)
        three.run_core()
        four.run_batch()
        entry = gather_seg(cls.reshape(count, width)).reshape(total, width)
        entry, four.over = fence(entry, four.over)
        four.run_core()
        cross_attn_full, cross_up_full = three.pieces()
        (cross_down_full,) = four.pieces()
    else:
        attn_full, up_full, down_full = [gather_plain(shard) for shard in (seg_attn, seg_up, seg_down)]
        cross_attn_full, cross_up_full, cross_down_full = [
            gather_plain(shard) for shard in (cross_attn, cross_up, cross_down)
        ]
        cot_all, seg_vec_full, cross_vec_full = spread_small(gather_seg(small))
        qkv, mixed, first_sum = attn_forward(flat, spot, attn_full, seg_vec_full)
        normed, act, slope, second_sum, tok, cls = ffn_forward(first_sum, spot, up_full, down_full, seg_vec_full)
        entry = gather_seg(cls.reshape(count, width)).reshape(total, width)

    docs = seg_doc[:, 0].reshape(micro, segments, parts) + (1 << 16) * jnp.arange(micro, dtype=jnp.int32)[:, None, None]
    docs = docs.transpose(2, 0, 1)
    blocks = micro if total > 256 else 1
    if blocks > 1:
        order = lambda rows: rows.reshape(parts, micro, segments, -1).transpose(1, 0, 2, 3).reshape(total, -1)
        back = lambda rows: rows.reshape(micro, parts, segments, -1).transpose(1, 0, 2, 3).reshape(total, -1)
        row_key = docs.transpose(1, 0, 2).reshape(total)
    else:
        order = back = lambda rows: rows
        row_key = docs.reshape(total)
    (
        cls_out, cls_grad, x_low, x_qkv_grad, x_mixed, x_attn_low, x_norm, x_inner, x_branch, x_act, x_sums,
    ) = cross_layer(
        order(entry), order(cot_all), row_key, blocks, spot,
        cross_attn_full, cross_up_full, cross_down_full, cross_vec_full,
    )
    own_cols = lambda rows: lax.dynamic_slice_in_dim(rows, place * own, own, 1)
    own_rows = lambda rows: lax.dynamic_slice_in_dim(back(rows), place * count, count, 0)
    cls_out = own_rows(cls_out)
    cls_grad = own_rows(cls_grad)

    branch, inner, first_grad, attn_low, ffn_sums = ffn_backward(
        tok_cot.reshape(count * length, width),
        cls_grad.reshape(cls.shape), second_sum, first_sum, slope, spot, up_full, down_full, seg_vec_full,
    )
    cross_pairs = (
        (own_cols(x_low), x_qkv_grad), (own_cols(x_mixed), x_attn_low),
        (own_cols(x_norm), x_inner), (own_cols(x_branch), x_act),
    )

    if by_links():
        keep, send = weight_grads(spot, (branch, act), (normed, inner), (mixed, attn_low))
        got = swap_core(send)
        x_grads = cross_grads(*cross_pairs)
        got, x_grads = fence(got, x_grads)
        stay, leave = core_sums(keep, got)
        stay, leave, attn_low = fence(stay, leave, attn_low)
        came = batch_swaps(leave)
        x_came = lax.all_to_all(x_grads, "batch", 0, 0, tiled=True)
        outs = attn_backward(first_grad, attn_low, qkv, spot, attn_full)
        (qkv_grad, hidden_grad, attn_sums), came, x_came = fence(outs, came, x_came)
        total_one = wide_sum(stay, *came)
        keep, send = weight_grads(spot, (flat, qkv_grad))
        set_one = batch_spread(chip_sum(total_one))
        set_cross = batch_spread(jnp.sum(x_came.astype(f32), 0))
        stay, leave = core_sums(keep, swap_core(send))
        set_two = batch_spread(chip_sum(wide_sum(stay, *batch_swaps(leave))))
        plan = (
            ((0, 2, 0, cols), (cols, 1, 0, cols), (2 * cols, 0, 3 * width, width)),
            ((0, 0, 0, 3 * width),),
            ((0, 3, 0, cols), (cols, 4, 0, cols), (2 * cols, 5, 0, cols)),
        )
        grads = place_outputs(spot, plan, (set_one, set_two, set_cross), 6, (own, cols))
    else:
        qkv_grad, hidden_grad, attn_sums = attn_backward(first_grad, attn_low, qkv, spot, attn_full)
        wide = [dot_tn(left, right) for left, right in cross_pairs]
        grads = [
            scatter_sum(jnp.concatenate([dot_tn(flat, qkv_grad), dot_tn(mixed, attn_low)], 1)),
            scatter_sum(dot_tn(normed, inner)), scatter_sum(dot_tn(branch, act)),
            jnp.concatenate(wide[:2], 1).astype(bf16), wide[2].astype(bf16), wide[3].astype(bf16),
        ]
        grads = [grad.astype(f32) for grad in lax.psum(tuple(grads), "batch")]
    sums = jnp.concatenate([attn_sums[:2], ffn_sums[2:12]], 0)
    seg_sums, x_sums = sum_everywhere(sums, x_sums[:12])
    seg_vec_grad = own_cols(seg_sums).T
    cross_vec_grad = own_cols(x_sums).T
    return (
        tok.reshape(hidden.shape), cls_out.reshape(cls_cot.shape), hidden_grad.reshape(hidden.shape),
        grads[0], grads[1], grads[2], seg_vec_grad, grads[3], grads[4], grads[5], cross_vec_grad,
    )


def solution(mesh):
    wide = P(None, "batch", None, "seg", None, None)
    rows = P("seg", None)
    cls = P(None, "batch", None, "seg", None)
    in_specs = (wide, P(None, "batch", None)) + (rows,) * 8 + (wide, cls)
    out_specs = (wide, cls, wide) + (rows,) * 8
    return jax.shard_map(local, mesh=mesh, in_specs=in_specs, out_specs=out_specs, check_vma=False)
```

```python
from functools import partial

import jax
import jax.numpy as jnp
from jax import lax
from jax.experimental import pallas as pl
from jax.experimental.pallas import tpu as pltpu
from jax.sharding import PartitionSpec as P

HEADS = 12
HEAD_DIM = 64
SEG_LEN = 128
PAIRS = HEADS // 2
PAIR = 2 * HEAD_DIM

NEG_FILL = -1e30
LN_EPS = 1e-05
SCALE = HEAD_DIM ** (-0.5)
ROOT_HALF = 0.7071067811865476
PDF_AT_ZERO = 0.3989422804014327
BLOCK = 256
CHIP_GROUPS = [[0, 2, 4, 6], [1, 3, 5, 7]]
VMEM_LIMIT = 60 * 1024 * 1024

f32 = jnp.float32
bf16 = jnp.bfloat16


def dot_nn(left, right):
    return lax.dot_general(left, right, (((1,), (0,)), ((), ())), preferred_element_type=f32)


def dot_nt(left, right):
    return lax.dot_general(left, right, (((1,), (1,)), ((), ())), preferred_element_type=f32)


def dot_tn(left, right):
    return lax.dot_general(left, right, (((0,), (0,)), ((), ())), preferred_element_type=f32)


def normalise(rows):
    centred = rows - jnp.mean(rows, -1, keepdims=True)
    spread = jnp.mean(centred * centred, -1, keepdims=True)
    inverse = lax.rsqrt(spread + LN_EPS)
    return centred * inverse, inverse


def norm_back(grad, unit, inverse, gain):
    scaled = grad * gain
    return inverse * (
        scaled
        - jnp.mean(scaled, -1, keepdims=True)
        - unit * jnp.mean(scaled * unit, -1, keepdims=True)
    )


def column_sum(rows):
    return jnp.sum(rows, 0, keepdims=True)


def gelu_parts(value):
    cdf = 0.5 * (1.0 + lax.erf(value * ROOT_HALF))
    pdf = PDF_AT_ZERO * jnp.exp(-0.5 * value * value)
    return value * cdf, cdf + value * pdf


def first_half(rows):
    return lax.broadcasted_iota(jnp.int32, (rows, PAIR), 1) < HEAD_DIM


def split_heads(rows, first):
    zero = jnp.zeros_like(rows)
    return jnp.concatenate([jnp.where(first, rows, zero), jnp.where(first, zero, rows)], 0)


def join_heads(stacked, first):
    rows = stacked.shape[0] // 2
    return jnp.where(first, stacked[:rows], stacked[rows:])


def pair_probs(query, keys, mask):
    scores = dot_nt(query, keys) * SCALE
    if mask is not None:
        scores = jnp.where(mask, scores, NEG_FILL)
    top = jnp.max(scores, -1, keepdims=True)
    expo = jnp.exp(scores - top)
    return expo * (1.0 / jnp.sum(expo, -1, keepdims=True))


def pair_forward(qkv_ref, out_ref, rows, pair, width, mask):
    first = first_half(rows.size)
    at = pair * PAIR
    query = split_heads(qkv_ref[rows, at : at + PAIR], first)
    keys = qkv_ref[rows, width + at : width + at + PAIR]
    values = qkv_ref[rows, 2 * width + at : 2 * width + at + PAIR]
    probs = pair_probs(query, keys, mask)
    mixed = join_heads(dot_nn(probs.astype(bf16), values), first)
    out_ref[rows, at : at + PAIR] = mixed.astype(bf16)


def pair_backward(qkv_ref, grad_ref, out_ref, rows, pair, width, mask):
    first = first_half(rows.size)
    at = pair * PAIR
    query = split_heads(qkv_ref[rows, at : at + PAIR], first)
    keys = qkv_ref[rows, width + at : width + at + PAIR]
    values = qkv_ref[rows, 2 * width + at : 2 * width + at + PAIR]
    out_grad = split_heads(grad_ref[rows, at : at + PAIR], first)
    probs = pair_probs(query, keys, mask)
    value_grad = dot_tn(probs.astype(bf16), out_grad)
    prob_grad = dot_nt(out_grad, values)
    score_grad = probs * (prob_grad - jnp.sum(prob_grad * probs, -1, keepdims=True))
    score_grad = score_grad.astype(bf16)
    query_grad = join_heads(dot_nn(score_grad, keys), first) * SCALE
    key_grad = dot_tn(score_grad, query) * SCALE
    out_ref[rows, at : at + PAIR] = query_grad.astype(bf16)
    out_ref[rows, width + at : width + at + PAIR] = key_grad.astype(bf16)
    out_ref[rows, 2 * width + at : 2 * width + at + PAIR] = value_grad.astype(bf16)


class Pieces:
    def __init__(self, shape, arrays, blocks):
        self.shape, self.arrays, self.blocks = shape, arrays, blocks

    def specs(self):
        return [pl.BlockSpec(memory_space=pl.ANY)] * len(self.arrays)

    def scratch(self):
        return [pltpu.VMEM(self.shape, bf16), pltpu.SemaphoreType.DMA((len(self.blocks),))]

    def copies(self, refs, place_ref, full_ref, sems):
        out = []
        for at, (index, source, size, target) in enumerate(self.blocks):
            row, col = target(place_ref[0], place_ref[1], place_ref[2])
            if not isinstance(row, int):
                row = pl.multiple_of(row, size[0])
            if not isinstance(col, int):
                col = pl.multiple_of(col, size[1])
            view = full_ref.at[pl.ds(row, size[0]), pl.ds(col, size[1])]
            out.append(pltpu.make_async_copy(refs[index].at[source], view, sems.at[at]))
        return out


class Weights:
    def __init__(self, *matrices):
        self.matrices = matrices

    def arrays(self, place):
        return [place] + [array for matrix in self.matrices for array in matrix.arrays]

    def specs(self):
        return [pl.BlockSpec(memory_space=pltpu.SMEM)] + [spec for matrix in self.matrices for spec in matrix.specs()]

    def scratch(self):
        return [item for matrix in self.matrices for item in matrix.scratch()]

    def wrap(self, body, with_place=False):
        many = sum(len(matrix.arrays) for matrix in self.matrices)

        def kernel(place_ref, *refs):
            given, rest = refs[:many], refs[many:]
            cut = len(rest) - 2 * len(self.matrices)
            rest, own = rest[:cut], rest[cut:]
            first = pl.program_id(0) == 0
            views, copies = [], []
            for at, matrix in enumerate(self.matrices):
                views.append(own[2 * at])
                copies.append(partial(matrix.copies, given[: len(matrix.arrays)], place_ref, own[2 * at], own[2 * at + 1]))
                given = given[len(matrix.arrays) :]

            @pl.when(first)
            def _():
                for group in copies:
                    for copy in group():
                        copy.start()

            def ready(at):
                @pl.when(first)
                def _():
                    for copy in copies[at]():
                        copy.wait()

                return views[at]

            body(ready, *([place_ref] if with_place else []), *rest)

        return kernel


def load_vec(small_ref, skip, own, vec_ref):
    @pl.when(pl.program_id(0) == 0)
    def _():
        for part in range(small_ref.shape[0]):
            vec_ref[0:12, part * own : (part + 1) * own] = small_ref[part, skip : skip + 12, :own].astype(f32)


def qkv_bias(vec_ref):
    query = vec_ref[0:1, :]
    return jnp.concatenate([query, jnp.zeros_like(query), vec_ref[1:2, :]], 1)


def attn_fwd_kernel(layout, ready, x_ref, small_ref, qkv_ref, mixed_ref, sum_ref, vec_ref):
    width = x_ref.shape[1]
    load_vec(small_ref, *layout, vec_ref)
    w_ref = ready(0)
    rows = x_ref[...]
    qkv = dot_nn(rows, w_ref[:, : 3 * width]) + qkv_bias(vec_ref)
    qkv_ref[...] = qkv.astype(bf16)
    for start in range(0, x_ref.shape[0], SEG_LEN):
        for pair in range(PAIRS):
            pair_forward(qkv_ref, mixed_ref, pl.ds(start, SEG_LEN), pair, width, None)
    branch = dot_nn(mixed_ref[...], w_ref[:, 3 * width :])
    sum_ref[...] = rows.astype(f32) + branch + vec_ref[2:3, :]


def ffn_fwd_kernel(layout, ready, sum_ref, small_ref, norm_ref, act_ref, slope_ref, second_ref, tok_ref, cls_ref, vec_ref):
    width = sum_ref.shape[1]
    load_vec(small_ref, *layout, vec_ref)
    up_ref = ready(0)
    down_ref = ready(1)
    unit, _ = normalise(sum_ref[...])
    normed = unit * vec_ref[3:4, :] + vec_ref[4:5, :]
    low = normed.astype(bf16)
    norm_ref[...] = low
    total = normed + vec_ref[5:6, :]
    for part in range(4):
        cols = pl.ds(part * width, width)
        inner = dot_nn(low, up_ref[:, cols]) + vec_ref[8 + part : 9 + part, :]
        act, slope = gelu_parts(inner)
        act = act.astype(bf16)
        act_ref[:, cols] = act
        slope_ref[:, cols] = slope.astype(bf16)
        total = total + dot_nt(act, down_ref[:, cols])
    second_ref[...] = total
    unit, _ = normalise(total)
    result = unit * vec_ref[6:7, :] + vec_ref[7:8, :]
    tok_ref[...] = result.astype(bf16)
    per = sum_ref.shape[0] // SEG_LEN
    for index in range(per):
        row = jnp.broadcast_to(result[index * SEG_LEN : index * SEG_LEN + 1, :][None], (cls_ref.shape[0], 1, width))
        cls_ref[:, pl.ds(pl.program_id(0) * per + index, 1), :] = row


def ffn_bwd_kernel(
    layout, ready, place_ref, cot_ref, cls_ref, second_ref, sum_ref, slope_ref, small_ref,
    branch_ref, inner_ref, first_ref, low_ref, sums_ref, vec_ref,
):
    width = sum_ref.shape[1]
    load_vec(small_ref, *layout, vec_ref)
    per = sum_ref.shape[0] // SEG_LEN
    begin = pl.program_id(0) * per
    if cls_ref.shape[0] > per * pl.num_programs(0):
        begin = begin + (place_ref[0] * 2 + place_ref[1]) * (per * pl.num_programs(0))

    @pl.when(pl.program_id(0) == 0)
    def _():
        sums_ref[...] = jnp.zeros_like(sums_ref)

    place = lax.broadcasted_iota(jnp.int32, (SEG_LEN, 1), 0) == 0
    parts = []
    for index in range(sum_ref.shape[0] // SEG_LEN):
        rows = cot_ref[index * SEG_LEN : (index + 1) * SEG_LEN, :].astype(f32)
        parts.append(rows + jnp.where(place, cls_ref[pl.ds(begin + index, 1), :], 0.0))
    grad = jnp.concatenate(parts, 0)
    unit, inverse = normalise(second_ref[...])
    sums_ref[6:7, :] += column_sum(grad * unit)
    sums_ref[7:8, :] += column_sum(grad)
    second_grad = norm_back(grad, unit, inverse, vec_ref[6:7, :])
    branch = second_grad.astype(bf16)
    branch_ref[...] = branch
    sums_ref[5:6, :] += column_sum(branch.astype(f32))
    up_ref = ready(0)
    down_ref = ready(1)
    total = second_grad
    for part in range(4):
        cols = pl.ds(part * width, width)
        act_grad = dot_nn(branch, down_ref[:, cols])
        inner = (act_grad * slope_ref[:, cols].astype(f32)).astype(bf16)
        inner_ref[:, cols] = inner
        sums_ref[8 + part : 9 + part, :] += column_sum(inner.astype(f32))
        total = total + dot_nt(inner, up_ref[:, cols])
    unit, inverse = normalise(sum_ref[...])
    sums_ref[3:4, :] += column_sum(total * unit)
    sums_ref[4:5, :] += column_sum(total)
    first = norm_back(total, unit, inverse, vec_ref[3:4, :])
    first_ref[...] = first
    low = first.astype(bf16)
    low_ref[...] = low
    sums_ref[2:3, :] += column_sum(low.astype(f32))


def attn_bwd_kernel(ready, first_ref, low_ref, qkv_ref, qkv_grad_ref, x_grad_ref, sums_ref, mixed_grad):
    width = first_ref.shape[1]

    @pl.when(pl.program_id(0) == 0)
    def _():
        sums_ref[...] = jnp.zeros_like(sums_ref)

    w_ref = ready(0)
    mixed_grad[...] = dot_nt(low_ref[...], w_ref[:, 3 * width :]).astype(bf16)
    for start in range(0, first_ref.shape[0], SEG_LEN):
        for pair in range(PAIRS):
            pair_backward(qkv_ref, mixed_grad, qkv_grad_ref, pl.ds(start, SEG_LEN), pair, width, None)
    qkv_grad = qkv_grad_ref[...]
    x_grad_ref[...] = first_ref[...] + dot_nt(qkv_grad, w_ref[:, : 3 * width])
    sums_ref[0:1, :] += column_sum(qkv_grad[:, :width].astype(f32))
    sums_ref[1:2, :] += column_sum(qkv_grad[:, 2 * width :].astype(f32))


def cross_kernel(
    single, layout, ready, place_ref, x_ref, cot_ref, key_own_ref, key_all_ref, small_ref,
    out_ref, x_grad_ref, grads_ref, sums_ref,
    qkv_ref, qkv_grad_ref, mixed_ref, mixed_grad, slope, act_ref, inner_ref, vec_ref, grad_ref,
):
    own = layout[1]
    load_vec(small_ref, *layout, vec_ref)
    width = x_ref.shape[1]
    count = x_ref.shape[0]
    rows = pl.ds(0, count)

    @pl.when(pl.program_id(0) == 0)
    def _():
        sums_ref[...] = jnp.zeros_like(sums_ref)

    attn_ref = ready(0)
    same = key_own_ref[...] == key_all_ref[0]
    mask = jnp.concatenate([same, same], 0)
    entry = x_ref[...]
    low_in = entry.astype(bf16)
    qkv = dot_nn(low_in, attn_ref[:, : 3 * width]) + qkv_bias(vec_ref)
    qkv_ref[...] = qkv.astype(bf16)
    for pair in range(PAIRS):
        pair_forward(qkv_ref, mixed_ref, rows, pair, width, mask)
    first_sum = entry + dot_nn(mixed_ref[...], attn_ref[:, 3 * width :]) + vec_ref[2:3, :]
    unit_one, inverse_one = normalise(first_sum)
    normed = unit_one * vec_ref[3:4, :] + vec_ref[4:5, :]
    low = normed.astype(bf16)
    up_ref = ready(1)
    down_ref = ready(2)
    total = normed + vec_ref[5:6, :]
    for part in range(4):
        cols = pl.ds(part * width, width)
        inner = dot_nn(low, up_ref[:, cols]) + vec_ref[8 + part : 9 + part, :]
        act, rate = gelu_parts(inner)
        act = act.astype(bf16)
        act_ref[:, cols] = act
        slope[:, cols] = rate
        total = total + dot_nt(act, down_ref[:, cols])
    unit_two, inverse_two = normalise(total)
    out_ref[...] = (unit_two * vec_ref[6:7, :] + vec_ref[7:8, :]).astype(bf16)

    if single:
        for part in range(small_ref.shape[0]):
            for at in range(width // 128):
                tile = small_ref[part, at * 8 : (at + 1) * 8, :]
                grad_ref[part * 8 : (part + 1) * 8, at * 128 : (at + 1) * 128] = tile.astype(f32)
        grad = grad_ref[...]
    else:
        grad = cot_ref[...].astype(f32)
    sums_ref[6:7, :] += column_sum(grad * unit_two)
    sums_ref[7:8, :] += column_sum(grad)
    second_grad = norm_back(grad, unit_two, inverse_two, vec_ref[6:7, :])
    branch = second_grad.astype(bf16)
    sums_ref[5:6, :] += column_sum(branch.astype(f32))
    total = second_grad
    for part in range(4):
        cols = pl.ds(part * width, width)
        inner = (dot_nn(branch, down_ref[:, cols]) * slope[:, cols]).astype(bf16)
        inner_ref[:, cols] = inner
        sums_ref[8 + part : 9 + part, :] += column_sum(inner.astype(f32))
        total = total + dot_nt(inner, up_ref[:, cols])
    sums_ref[3:4, :] += column_sum(total * unit_one)
    sums_ref[4:5, :] += column_sum(total)
    first = norm_back(total, unit_one, inverse_one, vec_ref[3:4, :])
    attn_low = first.astype(bf16)
    sums_ref[2:3, :] += column_sum(attn_low.astype(f32))
    mixed_grad[...] = dot_nt(attn_low, attn_ref[:, 3 * width :]).astype(bf16)
    for pair in range(PAIRS):
        pair_backward(qkv_ref, mixed_grad, qkv_grad_ref, rows, pair, width, mask)
    qkv_grad = qkv_grad_ref[...]
    x_grad_ref[...] = first + dot_nt(qkv_grad, attn_ref[:, : 3 * width])
    sums_ref[0:1, :] += column_sum(qkv_grad[:, :width].astype(f32))
    sums_ref[1:2, :] += column_sum(qkv_grad[:, 2 * width :].astype(f32))

    begin = (place_ref[0] * 2 + place_ref[1]) * own
    spot = lax.broadcasted_iota(jnp.int32, (width, own), 0) - lax.broadcasted_iota(jnp.int32, (width, own), 1)
    chosen = (spot == begin).astype(f32).astype(bf16)
    start = 0
    for left, right in ((low_in, qkv_grad), (mixed_ref[...], attn_low), (low, inner_ref[...]), (branch, act_ref[...])):
        cols = right.shape[1]
        grad = dot_tn(dot_nn(left, chosen).astype(bf16), right)
        if single:
            grads_ref[:, start : start + cols] = grad.astype(bf16)
        else:

            @pl.when(pl.program_id(0) == 0)
            def _(start=start, cols=cols):
                grads_ref[:, start : start + cols] = jnp.zeros((own, cols), f32)

            grads_ref[:, start : start + cols] += grad
        start += cols
    if single:
        sums = sums_ref[0:12, :]
        sums = jnp.concatenate([sums[:, : width // 2], sums[:, width // 2 :]], 0).astype(bf16)
        grads_ref[:, start:] = jnp.concatenate([sums] * (own // 24), 0)


def row_spec(width, block=BLOCK):
    return pl.BlockSpec((block, width), lambda i: (i, 0))


def whole_spec(shape):
    return pl.BlockSpec(shape, lambda i: (0,) * len(shape), pipeline_mode=pl.Buffered(1))


def fixed_spec(shape):
    return pl.BlockSpec(shape, lambda i: (0,) * len(shape))


def params():
    return pltpu.CompilerParams(dimension_semantics=("arbitrary",), vmem_limit_bytes=VMEM_LIMIT)


def shaped(*dims, dtype=bf16):
    return jax.ShapeDtypeStruct(dims, dtype)


def cost(flops, nbytes, trans=0):
    return pl.CostEstimate(flops=int(flops), bytes_accessed=int(nbytes), transcendentals=int(trans))


def attn_forward(flat, place, attn, small, layout):
    rows, width = flat.shape
    weights = Weights(attn)
    return pl.pallas_call(
        weights.wrap(partial(attn_fwd_kernel, layout)),
        grid=(rows // BLOCK,),
        in_specs=weights.specs() + [row_spec(width), whole_spec(small.shape)],
        out_specs=[row_spec(3 * width), row_spec(width), row_spec(width)],
        out_shape=[shaped(rows, 3 * width), shaped(rows, width), shaped(rows, width, dtype=f32)],
        scratch_shapes=[pltpu.VMEM((16, width), f32)] + weights.scratch(),
        compiler_params=params(),
        cost_estimate=cost(2 * rows * width * (4 * width + 2 * SEG_LEN), rows * width * 14 + width * width * 8),
        name="seg_attn_fwd",
    )(*weights.arrays(place), flat, small)


def ffn_forward(first_sum, place, up_proj, down_proj, small, layout, parts):
    rows, width = first_sum.shape
    inner = up_proj.shape[1]
    weights = Weights(up_proj, down_proj)
    cls_shape = (parts, rows // SEG_LEN, width)
    cls_spec = fixed_spec(cls_shape)
    return pl.pallas_call(
        weights.wrap(partial(ffn_fwd_kernel, layout)),
        grid=(rows // BLOCK,),
        in_specs=weights.specs() + [row_spec(width), whole_spec(small.shape)],
        out_specs=[row_spec(width), row_spec(inner), row_spec(inner), row_spec(width), row_spec(width), cls_spec],
        out_shape=[
            shaped(rows, width), shaped(rows, inner), shaped(rows, inner), shaped(rows, width, dtype=f32),
            shaped(rows, width), shaped(*cls_shape, dtype=f32),
        ],
        scratch_shapes=[pltpu.VMEM((16, width), f32)] + weights.scratch(),
        compiler_params=params(),
        cost_estimate=cost(4 * rows * width * inner, rows * (width * 12 + inner * 4) + width * inner * 4, 2 * rows * inner),
        name="seg_ffn_fwd",
    )(*weights.arrays(place), first_sum, small)


def ffn_backward(cot, cls_grad, second_sum, first_sum, slope, place, up_proj, down_proj, small, layout):
    rows, width = first_sum.shape
    inner = up_proj.shape[1]
    weights = Weights(up_proj, down_proj)
    cls_spec = whole_spec(cls_grad.shape)
    return pl.pallas_call(
        weights.wrap(partial(ffn_bwd_kernel, layout), with_place=True),
        grid=(rows // BLOCK,),
        in_specs=weights.specs() + [
            row_spec(width), cls_spec, row_spec(width), row_spec(width), row_spec(inner), whole_spec(small.shape),
        ],
        out_specs=[row_spec(width), row_spec(inner), row_spec(width), row_spec(width), fixed_spec((16, width))],
        out_shape=[
            shaped(rows, width), shaped(rows, inner), shaped(rows, width, dtype=f32), shaped(rows, width),
            shaped(16, width, dtype=f32),
        ],
        scratch_shapes=[pltpu.VMEM((16, width), f32)] + weights.scratch(),
        compiler_params=params(),
        cost_estimate=cost(4 * rows * width * inner, rows * (width * 16 + inner * 4) + width * inner * 4),
        name="seg_ffn_bwd",
    )(*weights.arrays(place), cot, cls_grad, second_sum, first_sum, slope, small)


def attn_backward(first_grad, attn_low, qkv, place, attn, share, shares, before=()):
    rows, width = first_grad.shape
    weights = Weights(attn)
    steps = rows // BLOCK // shares
    spec = lambda cols: pl.BlockSpec((BLOCK, cols), lambda i: (i + share * steps, 0))
    kept = len(before)
    args = weights.arrays(place) + [first_grad, attn_low, qkv]

    def body(ready, *refs):
        attn_bwd_kernel(ready, *refs[:3], *refs[3 + kept :])

    return pl.pallas_call(
        weights.wrap(body),
        grid=(steps,),
        in_specs=weights.specs() + [spec(width), spec(width), spec(3 * width)] + [pl.BlockSpec(memory_space=pl.ANY)] * kept,
        out_specs=[spec(3 * width), spec(width), fixed_spec((8, width))],
        out_shape=[shaped(rows, 3 * width), shaped(rows, width, dtype=f32), shaped(8, width, dtype=f32)],
        input_output_aliases={len(args) + at: at for at in range(kept)},
        scratch_shapes=[pltpu.VMEM((BLOCK, width), bf16)] + weights.scratch(),
        compiler_params=params(),
        cost_estimate=cost(
            2 * rows * width * (4 * width + 5 * SEG_LEN) // shares, rows * width * 22 // shares + width * width * 8
        ),
        name="seg_attn_bwd",
    )(*args, *before)


def cross_layer(entry, cot, row_key, blocks, place, attn, up_proj, down_proj, small, layout):
    rows, width = entry.shape
    inner = up_proj.shape[1]
    block = rows // blocks
    spec = partial(row_spec, block=block)
    weights = Weights(attn, up_proj, down_proj)
    own = layout[1]
    wide = (own, 3 * inner + (width // 2 if by_links() else 0))
    return pl.pallas_call(
        weights.wrap(partial(cross_kernel, by_links(), layout), with_place=True),
        grid=(blocks,),
        in_specs=weights.specs() + [
            spec(width), spec(width), spec(1), pl.BlockSpec((1, 1, block), lambda i: (i, 0, 0)), whole_spec(small.shape),
        ],
        out_specs=[spec(width), spec(width), fixed_spec(wide), fixed_spec((16, width))],
        out_shape=[
            shaped(rows, width), shaped(rows, width, dtype=f32), shaped(*wide, dtype=bf16 if by_links() else f32),
            shaped(16, width, dtype=f32),
        ],
        scratch_shapes=[
            pltpu.VMEM((block, 3 * width), bf16), pltpu.VMEM((block, 3 * width), bf16), pltpu.VMEM((block, width), bf16),
            pltpu.VMEM((block, width), bf16), pltpu.VMEM((block, inner), f32), pltpu.VMEM((block, inner), bf16),
            pltpu.VMEM((block, inner), bf16), pltpu.VMEM((16, width), f32), pltpu.VMEM((block, width), f32),
        ] + weights.scratch(),
        compiler_params=params(),
        cost_estimate=cost(24 * rows * width * 4 * width, rows * width * 40 + width * inner * 6),
        name="cross_layer",
    )(*weights.arrays(place), entry, cot, row_key.reshape(rows, 1), row_key.reshape(blocks, 1, block), small)


def hop_seg(value, hops):
    size = lax.axis_size("seg")
    return lax.ppermute(value, "seg", [(at, (at + 2 * hops) % size) for at in range(size)])


def swap_core(value):
    return lax.ppermute(value, "seg", [(at, at ^ 1) for at in range(lax.axis_size("seg"))])


def swap_batch(value, flip):
    return lax.ppermute(value, "batch", [(at, at ^ flip) for at in range(lax.axis_size("batch"))])


def fence(*values):
    return lax.optimization_barrier(values)


def by_links():
    return lax.axis_size("batch") == 4 and lax.axis_size("seg") == 8


class Gather:
    def __init__(self, *shards):
        self.many = len(shards)
        self.own, self.cols = shards[0].shape
        self.quarter = self.cols // 4
        self.mine = jnp.concatenate(shards, 0) if self.many > 1 else shards[0]
        self.part = lax.dynamic_slice_in_dim(self.mine, lax.axis_index("batch") * self.quarter, self.quarter, 1)

    def run_seg(self, how):
        if how == "permute":
            self.raw = [hop_seg(self.part, hops) for hops in (3, 2, 1)]
        else:
            self.raw = [chips_exchange(jnp.broadcast_to(self.part, (4,) + self.part.shape))]

    def run_own(self):
        self.mine_too = swap_core(self.mine)

    def sort_seg(self):
        if len(self.raw) == 3:
            self.along = jnp.stack(self.raw)
        else:
            full = jnp.concatenate([self.raw[0], self.raw[0][:3]], 0)
            self.along = lax.dynamic_slice_in_dim(full, lax.axis_index("seg") // 2 + 1, 3)

    def run_near(self):
        self.near = [swap_batch(self.along, flip) for flip in (1, 2)]

    def run_far(self):
        half = self.mine.shape[0] // 2
        self.far = [swap_batch(self.near[1][:, :half], 1), swap_batch(self.near[0][:, half:], 2)]

    def run_core_near(self):
        self.near = jnp.stack([self.along] + self.near)
        self.near_too = swap_core(self.near)

    def run_core_far(self):
        self.far_too = [swap_core(array) for array in self.far]

    def pieces(self):
        own, cols, quarter = self.own, self.cols, self.quarter
        half = self.mine.shape[0] // 2
        arrays = [self.mine, self.near] + self.far + [self.mine_too, self.near_too] + self.far_too
        matrices = []
        for at in range(self.many):
            first, last = at * own, (at + 1) * own
            blocks = []
            for core in (0, 1):

                def chip(later, core=core):
                    return lambda z, c: (((z + 1 + later) & 3) * 2 + (c ^ core)) * own

                target = lambda z, c, q, core=core: ((z * 2 + (c ^ core)) * own, 0)
                blocks.append((4 * core, (slice(first, last), slice(None)), (own, cols), target))
                for later in range(3):
                    row = chip(later)
                    for flip in range(3):
                        target = lambda z, c, q, row=row, flip=flip: (row(z, c), (q ^ flip) * quarter)
                        source = (flip, later, slice(first, last), slice(None))
                        blocks.append((4 * core + 1, source, (own, quarter), target))
                    for side in (0, 1):
                        lo, hi = max(first, side * half), min(last, (side + 1) * half)
                        if lo >= hi:
                            continue
                        target = lambda z, c, q, row=row, skip=lo - first: (row(z, c) + skip, (q ^ 3) * quarter)
                        source = (later, slice(lo - side * half, hi - side * half), slice(None))
                        blocks.append((4 * core + 2 + side, source, (hi - lo, quarter), target))
            matrices.append(Pieces((own * lax.axis_size("seg"), cols), arrays, blocks))
        return matrices


def gather_plain(shard):
    full = lax.all_gather(shard, "seg", axis=0, tiled=True)
    block = (0, (slice(None), slice(None)), full.shape, lambda z, c, q: (0, 0))
    return Pieces(full.shape, [full], [block])


def chips_exchange(value):
    return lax.all_to_all(value, "seg", 0, 0, axis_index_groups=CHIP_GROUPS, tiled=True)


def gather_seg(value):
    if not by_links():
        return lax.all_gather(value, "seg", axis=0, tiled=False)
    copies = jnp.broadcast_to(value, (lax.axis_size("seg"),) + value.shape)
    return lax.all_to_all(copies, "seg", 0, 0, tiled=True)


def weight_grad_kernel(steps, place_ref, *refs):
    pairs, (keep_ref, send_ref, acc_ref) = refs[: 2 * len(steps)], refs[2 * len(steps) :]
    step = pl.program_id(0)
    begin = 0
    for at, many in enumerate(steps):

        @pl.when((step >= begin) & (step < begin + many))
        def _(at=at):
            acc_ref[...] = dot_tn(pairs[2 * at][...], pairs[2 * at + 1][...])

        begin += many
    c, q = place_ref[1], place_ref[2]
    size = keep_ref.shape[2]
    for flip in range(4):
        for chip in range(4):
            for core, out_ref in ((0, keep_ref), (1, send_ref)):
                row = (chip * 2 + (c ^ core)) * (4 * size) + (q ^ flip) * size
                rows = pl.ds(pl.multiple_of(row, size), size)
                out_ref[flip, chip] = acc_ref[rows, :].astype(bf16)


def weight_grads(place, *pairs):
    rows, width = pairs[0][0].shape
    steps = tuple(right.shape[1] // width for _, right in pairs)
    size = width // 32
    in_specs = [pl.BlockSpec(memory_space=pltpu.SMEM)]
    begin = 0
    for many in steps:
        in_specs.append(whole_spec((rows, width)))
        in_specs.append(pl.BlockSpec((rows, width), lambda i, begin=begin, many=many: (0, jnp.clip(i - begin, 0, many - 1))))
        begin += many
    out_spec = pl.BlockSpec((4, 4, size, width), lambda i: (0, 0, 0, i))
    out = shaped(4, 4, size, begin * width)
    return pl.pallas_call(
        partial(weight_grad_kernel, steps),
        grid=(begin,),
        in_specs=in_specs,
        out_specs=[out_spec, out_spec],
        out_shape=[out, out],
        scratch_shapes=[pltpu.VMEM((width, width), f32)],
        compiler_params=params(),
        cost_estimate=cost(2 * rows * width * width * begin, 2 * (rows + width) * width * begin),
        name="weight_grads",
    )(place, *[array for pair in pairs for array in pair])


def wide_sum(first, *others):
    total = first.astype(f32)
    for other in others:
        total = total + other.astype(f32)
    return total


def batch_spread(value):
    value = value.astype(bf16)
    return [value] + [swap_batch(value, flip) for flip in (1, 2, 3)]


def core_sums(keep, got):
    sums = [wide_sum(keep[flip], got[flip]) for flip in range(4)]
    return sums[0], [part.astype(bf16) for part in sums[1:]]


def batch_swaps(parts):
    return [swap_batch(part, flip) for flip, part in zip((1, 2, 3), parts)]


def place_kernel(plan, place_ref, *refs):
    count = 4 * len(plan)
    blocks, outs = refs[:count], refs[count:]
    q = place_ref[2]
    for at, targets in enumerate(plan):
        for flip in range(4):
            block = blocks[4 * at + flip]
            size = block.shape[0]
            rows = pl.ds(pl.multiple_of((q ^ flip) * size, size), size)
            for source, index, target, cols in targets:
                outs[index][rows, target : target + cols] = block[:, source : source + cols].astype(f32)


def place_outputs(place, plan, groups, own, shape):
    vmem = pl.BlockSpec(memory_space=pltpu.VMEM)
    return pl.pallas_call(
        partial(place_kernel, plan),
        in_specs=[pl.BlockSpec(memory_space=pltpu.SMEM)] + [vmem] * (4 * len(groups)),
        out_specs=[vmem] * own,
        out_shape=[jax.ShapeDtypeStruct(shape, f32)] * own,
        compiler_params=pltpu.CompilerParams(vmem_limit_bytes=VMEM_LIMIT),
        cost_estimate=cost(0, own * shape[0] * shape[1] * 6),
        name="place_outputs",
    )(place, *[block for group in groups for block in group])


def scatter_sum(matrix):
    return lax.psum_scatter(matrix.astype(bf16), "seg", scatter_dimension=0, tiled=True)


def local(
    hidden, seg_doc, seg_attn, seg_up, seg_down, seg_vec,
    cross_attn, cross_up, cross_down, cross_vec, tok_cot, cls_cot,
):
    micro, _, segments, _, length, width = hidden.shape
    own, cols = seg_attn.shape
    parts = lax.axis_size("seg")
    place = lax.axis_index("seg")
    count = micro * segments
    total = parts * count
    spot = jnp.stack([place // 2, place % 2, lax.axis_index("batch")]).astype(jnp.int32)

    flat = hidden.reshape(count * length, width)
    tiles = width // 128
    vecs = jnp.pad(jnp.concatenate([seg_vec.T, cross_vec.T], 0), ((0, 0), (0, 128 - own)))
    small = cls_cot.reshape(count, tiles, 128).transpose(1, 0, 2).reshape(count * tiles, 128)
    small = jnp.concatenate([small, vecs], 0)
    seg_layout, cross_layout = (count * tiles, own), (count * tiles + 12, own)

    if by_links():
        one, two, three, four = Gather(seg_attn), Gather(seg_up, seg_down), Gather(cross_attn, cross_up), Gather(cross_down)
        one.run_seg("permute")
        small = gather_seg(small)
        one.run_own()
        one.raw, small, two.part, two.mine = fence(one.raw, small, two.part, two.mine)
        one.sort_seg()
        one.run_near()
        two.run_seg("permute")
        (one.near,) = fence(one.near)
        one.run_far()
        one.far, one.near, two.raw, three.part, three.mine = fence(one.far, one.near, two.raw, three.part, three.mine)
        two.sort_seg()
        one.run_core_near()
        one.run_core_far()
        two.run_near()
        three.run_seg("exchange")
        (attn_full,) = one.pieces()
        outs = attn_forward(flat, spot, attn_full, small, seg_layout)
        (qkv, mixed, first_sum), two.near, two.mine, four.part, three.raw = fence(
            outs, two.near, two.mine, four.part, three.raw
        )
        two.run_far()
        two.run_core_near()
        two.run_own()
        two.far, three.raw, three.mine, four.mine = fence(two.far, three.raw, three.mine, four.mine)
        three.sort_seg()
        two.run_core_far()
        three.run_near()
        four.run_seg("exchange")
        up_full, down_full = two.pieces()
        outs = ffn_forward(first_sum, spot, up_full, down_full, small, seg_layout, parts)
        (normed, act, slope, second_sum, tok, cls), three.near, four.raw, three.mine, four.mine = fence(
            outs, three.near, four.raw, three.mine, four.mine
        )
        four.sort_seg()
        three.run_far()
        entry = lax.all_to_all(cls, "seg", 0, 0, tiled=True).reshape(total, width)
        cot_all = entry
        three.run_core_near()
        three.run_own()
        four.run_near()
        entry, three.far, four.near = fence(entry, three.far, four.near)
        three.run_core_far()
        four.run_far()
        four.run_core_near()
        four.run_own()
        (four.far,) = fence(four.far)
        four.run_core_far()
        cross_attn_full, cross_up_full = three.pieces()
        (cross_down_full,) = four.pieces()
    else:
        attn_full, up_full, down_full = [gather_plain(shard) for shard in (seg_attn, seg_up, seg_down)]
        cross_attn_full, cross_up_full, cross_down_full = [
            gather_plain(shard) for shard in (cross_attn, cross_up, cross_down)
        ]
        small = gather_seg(small)
        cot_all = small[:, : count * tiles].reshape(parts, tiles, count, 128).transpose(0, 2, 1, 3).reshape(total, width)
        qkv, mixed, first_sum = attn_forward(flat, spot, attn_full, small, seg_layout)
        normed, act, slope, second_sum, tok, cls = ffn_forward(first_sum, spot, up_full, down_full, small, seg_layout, parts)
        entry = gather_seg(cls[0]).reshape(total, width)

    docs = seg_doc[:, 0].reshape(micro, segments, parts) + (1 << 16) * jnp.arange(micro, dtype=jnp.int32)[:, None, None]
    docs = docs.transpose(2, 0, 1)
    blocks = micro if total > 256 else 1
    if blocks > 1:
        order = lambda rows: rows.reshape(parts, micro, segments, -1).transpose(1, 0, 2, 3).reshape(total, -1)
        back = lambda rows: rows.reshape(micro, parts, segments, -1).transpose(1, 0, 2, 3).reshape(total, -1)
        row_key = docs.transpose(1, 0, 2).reshape(total)
    else:
        order = back = lambda rows: rows
        row_key = docs.reshape(total)
    cls_out, cls_grad, x_grads, x_sums = cross_layer(
        order(entry), order(cot_all), row_key, blocks, spot,
        cross_attn_full, cross_up_full, cross_down_full, small, cross_layout,
    )
    own_cols = lambda rows: lax.dynamic_slice_in_dim(rows, place * own, own, 1)
    own_rows = lambda rows: lax.dynamic_slice_in_dim(back(rows), place * count, count, 0)
    cls_out = own_rows(cls_out)
    if not by_links():
        cls_grad = own_rows(cls_grad)
    outs = ffn_backward(
        tok_cot.reshape(count * length, width),
        cls_grad, second_sum, first_sum, slope, spot, up_full, down_full, small, seg_layout,
    )

    if by_links():
        folded = lambda rows: jnp.concatenate([rows[:, : width // 2], rows[:, width // 2 :]], 0)
        unfolded = lambda rows: jnp.concatenate([rows[:12], rows[12:]], 1)
        x_came = lax.all_to_all(x_grads.reshape(4, own // 4, 3 * cols + width // 2), "batch", 0, 0, tiled=True)
        (branch, inner, first_grad, attn_low, ffn_sums), x_came = fence(outs, x_came)
        x_sum = jnp.sum(x_came.astype(f32), 0)
        cross_sums = unfolded(x_sum[:, 3 * cols :])
        keep_down, send = weight_grads(spot, (branch, act))
        send, inner = fence(send, inner)
        got_down = swap_core(send)
        set_cross = batch_spread(x_sum[:, : 3 * cols])
        keep_up, send_up = weight_grads(spot, (normed, inner), (mixed, attn_low))
        got_down, keep_up, send_up = fence(got_down, keep_up, send_up)
        stay_down, leave = core_sums(keep_down, got_down)
        leave, send_up, attn_low = fence(leave, send_up, attn_low)
        came_down = batch_swaps(leave)
        got_up = swap_core(send_up)
        outs = attn_backward(first_grad, attn_low, qkv, spot, attn_full, 0, 2)
        outs, came_down, got_up = fence(outs, came_down, got_up)
        total_down = wide_sum(stay_down, *came_down).astype(bf16)
        stay_up, leave = core_sums(keep_up, got_up)
        (qkv_grad, hidden_grad, sums_one), total_down, leave = fence(outs, total_down, leave)
        raw_down = chips_exchange(total_down)
        came_up = batch_swaps(leave)
        outs = attn_backward(first_grad, attn_low, qkv, spot, attn_full, 1, 2, (qkv_grad, hidden_grad))
        (qkv_grad, hidden_grad, sums_two), raw_down = fence(outs, raw_down)
        sums = folded(jnp.concatenate([(sums_one + sums_two)[:2], ffn_sums[2:12]], 0))
        sums_too = swap_core(sums)
        keep, send = weight_grads(spot, (flat, qkv_grad))
        keep, send, sums, sums_too, came_up = fence(keep, send, sums, sums_too, came_up)
        got = swap_core(send)
        total_up = wide_sum(stay_up, *came_up).astype(bf16)
        sums = jnp.broadcast_to(sums + sums_too, (4, 24, width // 2))
        stay, leave = core_sums(keep, got)
        stay = jnp.concatenate([stay, sums], 2)
        leave = [jnp.concatenate([part, sums.astype(bf16)], 2) for part in leave]
        total_up, leave = fence(total_up, leave)
        came = batch_swaps(leave)
        raw_up = chips_exchange(total_up)
        set_down = batch_spread(jnp.sum(raw_down.astype(f32), 0))
        came, raw_up = fence(came, raw_up)
        raw = chips_exchange(wide_sum(stay, *came).astype(bf16))
        set_up = batch_spread(jnp.sum(raw_up.astype(f32), 0))
        last = jnp.sum(raw.astype(f32), 0)
        set_qkv = batch_spread(last[:, : 3 * width])
        seg_sums = unfolded(last[:, 3 * width :])
        shape = (own, cols)
        x_plan = (((0, 0, 0, cols), (cols, 1, 0, cols), (2 * cols, 2, 0, cols)),)
        x_placed = place_outputs(spot, x_plan, (set_cross,), 3, shape)
        (down_placed,) = place_outputs(spot, (((0, 0, 0, cols),),), (set_down,), 1, shape)
        (up_placed,) = place_outputs(spot, (((0, 0, 0, cols),),), (set_up,), 1, shape)
        attn_plan = (((0, 0, 0, 3 * width),), ((cols, 0, 3 * width, width),))
        (attn_placed,) = place_outputs(spot, attn_plan, (set_qkv, set_up), 1, shape)
        grads = [attn_placed, up_placed, down_placed] + list(x_placed)
    else:
        branch, inner, first_grad, attn_low, ffn_sums = outs
        qkv_grad, hidden_grad, attn_sums = attn_backward(first_grad, attn_low, qkv, spot, attn_full, 0, 1)
        x_grads = x_grads.astype(bf16)
        grads = [
            scatter_sum(jnp.concatenate([dot_tn(flat, qkv_grad), dot_tn(mixed, attn_low)], 1)),
            scatter_sum(dot_tn(normed, inner)), scatter_sum(dot_tn(branch, act)),
            x_grads[:, :cols], x_grads[:, cols : 2 * cols], x_grads[:, 2 * cols :],
        ]
        grads = [grad.astype(f32) for grad in lax.psum(tuple(grads), "batch")]
        seg_sums = lax.psum(jnp.concatenate([attn_sums[:2], ffn_sums[2:12]], 0), ("batch", "seg"))
        cross_sums = lax.psum(x_sums[:12], "batch")
    seg_vec_grad = own_cols(seg_sums).T
    cross_vec_grad = own_cols(cross_sums).T
    return (
        tok.reshape(hidden.shape), cls_out.reshape(cls_cot.shape), hidden_grad.reshape(hidden.shape),
        grads[0], grads[1], grads[2], seg_vec_grad, grads[3], grads[4], grads[5], cross_vec_grad,
    )


def solution(mesh):
    wide = P(None, "batch", None, "seg", None, None)
    rows = P("seg", None)
    cls = P(None, "batch", None, "seg", None)
    in_specs = (wide, P(None, "batch", None)) + (rows,) * 8 + (wide, cls)
    out_specs = (wide, cls, wide) + (rows,) * 8
    return jax.shard_map(local, mesh=mesh, in_specs=in_specs, out_specs=out_specs, check_vma=False)
```

```python
from functools import partial

import jax
import jax.numpy as jnp
from jax import lax
from jax.experimental import pallas as pl
from jax.experimental.pallas import tpu as pltpu
from jax.sharding import PartitionSpec as P

HEADS = 12
HEAD_DIM = 64
SEG_LEN = 128
PAIRS = HEADS // 2
PAIR = 2 * HEAD_DIM
GROUP = 6

NEG_FILL = -1e30
LN_EPS = 1e-05
SCALE = HEAD_DIM ** (-0.5)
ROOT_HALF = 0.7071067811865476
PDF_AT_ZERO = 0.3989422804014327
BLOCK = 256
CHIP_GROUPS = [[0, 2, 4, 6], [1, 3, 5, 7]]
VMEM_LIMIT = 60 * 1024 * 1024

f32 = jnp.float32
bf16 = jnp.bfloat16


def dot_nn(left, right):
    return lax.dot_general(left, right, (((1,), (0,)), ((), ())), preferred_element_type=f32)


def dot_nt(left, right):
    return lax.dot_general(left, right, (((1,), (1,)), ((), ())), preferred_element_type=f32)


def dot_tn(left, right):
    return lax.dot_general(left, right, (((0,), (0,)), ((), ())), preferred_element_type=f32)


def normalise(rows):
    centred = rows - jnp.mean(rows, -1, keepdims=True)
    spread = jnp.mean(centred * centred, -1, keepdims=True)
    inverse = lax.rsqrt(spread + LN_EPS)
    return centred * inverse, inverse


def norm_back(grad, unit, inverse, gain):
    scaled = grad * gain
    return inverse * (
        scaled
        - jnp.mean(scaled, -1, keepdims=True)
        - unit * jnp.mean(scaled * unit, -1, keepdims=True)
    )


def column_sum(rows):
    return jnp.sum(rows, 0, keepdims=True)


def gelu_parts(value):
    cdf = 0.5 * (1.0 + lax.erf(value * ROOT_HALF))
    pdf = PDF_AT_ZERO * jnp.exp(-0.5 * value * value)
    return value * cdf, cdf + value * pdf


def first_half(rows):
    return lax.broadcasted_iota(jnp.int32, (rows, PAIR), 1) < HEAD_DIM


def split_heads(rows, first):
    zero = jnp.zeros_like(rows)
    return jnp.concatenate([jnp.where(first, rows, zero), jnp.where(first, zero, rows)], 0)


def join_heads(stacked, first):
    rows = stacked.shape[0] // 2
    return jnp.where(first, stacked[:rows], stacked[rows:])


def pair_probs(query, keys, mask):
    scores = dot_nt(keys, query) * SCALE
    if mask is not None:
        scores = jnp.where(mask, scores, NEG_FILL)
    top = jnp.max(scores, 0, keepdims=True)
    expo = jnp.exp(scores - top)
    return expo * (1.0 / jnp.sum(expo, 0, keepdims=True))


def pair_parts(qkv_ref, rows, pair, width, first):
    at = pair * PAIR
    query = split_heads(qkv_ref[rows, at : at + PAIR], first)
    return query, qkv_ref[rows, width + at : width + at + PAIR], qkv_ref[rows, 2 * width + at : 2 * width + at + PAIR]


def heads_forward(qkv_ref, out_ref, rows, width, mask):
    first = first_half(rows.size)
    for start in range(0, PAIRS, GROUP):
        pairs = range(start, start + GROUP)
        parts = [pair_parts(qkv_ref, rows, pair, width, first) for pair in pairs]
        probs = [pair_probs(query, keys, mask).astype(bf16) for query, keys, _ in parts]
        mixed = [join_heads(dot_tn(prob, values), first) for prob, (_, _, values) in zip(probs, parts)]
        for pair, value in zip(pairs, mixed):
            out_ref[rows, pair * PAIR : (pair + 1) * PAIR] = value.astype(bf16)


def heads_backward(qkv_ref, grad_ref, out_ref, rows, width, mask):
    first = first_half(rows.size)
    for start in range(0, PAIRS, GROUP):
        pairs = range(start, start + GROUP)
        parts = [pair_parts(qkv_ref, rows, pair, width, first) for pair in pairs]
        grads = [split_heads(grad_ref[rows, pair * PAIR : (pair + 1) * PAIR], first) for pair in pairs]
        probs = [pair_probs(query, keys, mask) for query, keys, _ in parts]
        prob_grads = [dot_nt(values, grad) for (_, _, values), grad in zip(parts, grads)]
        value_grads = [dot_nn(prob.astype(bf16), grad) for prob, grad in zip(probs, grads)]
        score_grads = [
            (prob * (grad - jnp.sum(grad * prob, 0, keepdims=True))).astype(bf16) for prob, grad in zip(probs, prob_grads)
        ]
        key_grads = [dot_nn(grad, query) * SCALE for grad, (query, _, _) in zip(score_grads, parts)]
        query_grads = [join_heads(dot_tn(grad, keys), first) * SCALE for grad, (_, keys, _) in zip(score_grads, parts)]
        for at, values in ((0, query_grads), (width, key_grads), (2 * width, value_grads)):
            for pair, value in zip(pairs, values):
                out_ref[rows, at + pair * PAIR : at + (pair + 1) * PAIR] = value.astype(bf16)


class Pieces:
    def __init__(self, shape, arrays, blocks):
        self.shape, self.arrays, self.blocks = shape, arrays, blocks

    def specs(self):
        return [pl.BlockSpec(memory_space=pl.ANY)] * len(self.arrays)

    def scratch(self):
        return [pltpu.VMEM(self.shape, bf16), pltpu.SemaphoreType.DMA((len(self.blocks),))]

    def copies(self, refs, place_ref, full_ref, sems):
        out = []
        for at, (index, source, size, target) in enumerate(self.blocks):
            row, col = target(place_ref[0], place_ref[1], place_ref[2])
            if not isinstance(row, int):
                row = pl.multiple_of(row, size[0])
            if not isinstance(col, int):
                col = pl.multiple_of(col, size[1])
            view = full_ref.at[pl.ds(row, size[0]), pl.ds(col, size[1])]
            out.append(pltpu.make_async_copy(refs[index].at[source], view, sems.at[at]))
        return out


class Weights:
    def __init__(self, *matrices):
        self.matrices = matrices

    def arrays(self, place):
        return [place] + [array for matrix in self.matrices for array in matrix.arrays]

    def specs(self):
        return [pl.BlockSpec(memory_space=pltpu.SMEM)] + [spec for matrix in self.matrices for spec in matrix.specs()]

    def scratch(self):
        return [item for matrix in self.matrices for item in matrix.scratch()]

    def wrap(self, body, with_place=False):
        many = sum(len(matrix.arrays) for matrix in self.matrices)

        def kernel(place_ref, *refs):
            given, rest = refs[:many], refs[many:]
            cut = len(rest) - 2 * len(self.matrices)
            rest, own = rest[:cut], rest[cut:]
            first = pl.program_id(0) == 0
            views, copies = [], []
            for at, matrix in enumerate(self.matrices):
                views.append(own[2 * at])
                copies.append(partial(matrix.copies, given[: len(matrix.arrays)], place_ref, own[2 * at], own[2 * at + 1]))
                given = given[len(matrix.arrays) :]

            @pl.when(first)
            def _():
                for group in copies:
                    for copy in group():
                        copy.start()

            def ready(at):
                @pl.when(first)
                def _():
                    for copy in copies[at]():
                        copy.wait()

                return views[at]

            body(ready, *([place_ref] if with_place else []), *rest)

        return kernel


def load_vec(small_ref, skip, own, vec_ref):
    @pl.when(pl.program_id(0) == 0)
    def _():
        for part in range(small_ref.shape[0]):
            vec_ref[0:12, part * own : (part + 1) * own] = small_ref[part, skip : skip + 12, :own].astype(f32)


def qkv_bias(vec_ref):
    query = vec_ref[0:1, :]
    return jnp.concatenate([query, jnp.zeros_like(query), vec_ref[1:2, :]], 1)


def attn_fwd_kernel(layout, ready, x_ref, small_ref, qkv_ref, mixed_ref, sum_ref, vec_ref):
    width = x_ref.shape[1]
    load_vec(small_ref, *layout, vec_ref)
    w_ref = ready(0)
    rows = x_ref[...]
    qkv = dot_nn(rows, w_ref[:, : 3 * width]) + qkv_bias(vec_ref)
    qkv_ref[...] = qkv.astype(bf16)
    for start in range(0, x_ref.shape[0], SEG_LEN):
        heads_forward(qkv_ref, mixed_ref, pl.ds(start, SEG_LEN), width, None)
    branch = dot_nn(mixed_ref[...], w_ref[:, 3 * width :])
    sum_ref[...] = rows.astype(f32) + branch + vec_ref[2:3, :]


def ffn_fwd_kernel(layout, ready, sum_ref, small_ref, norm_ref, act_ref, slope_ref, second_ref, tok_ref, cls_ref, vec_ref):
    width = sum_ref.shape[1]
    load_vec(small_ref, *layout, vec_ref)
    up_ref = ready(0)
    down_ref = ready(1)
    unit, _ = normalise(sum_ref[...])
    normed = unit * vec_ref[3:4, :] + vec_ref[4:5, :]
    low = normed.astype(bf16)
    norm_ref[...] = low
    total = normed + vec_ref[5:6, :]
    for part in range(4):
        cols = pl.ds(part * width, width)
        inner = dot_nn(low, up_ref[:, cols]) + vec_ref[8 + part : 9 + part, :]
        act, slope = gelu_parts(inner)
        act = act.astype(bf16)
        act_ref[:, cols] = act
        slope_ref[:, cols] = slope.astype(bf16)
        total = total + dot_nt(act, down_ref[:, cols])
    second_ref[...] = total
    unit, _ = normalise(total)
    result = unit * vec_ref[6:7, :] + vec_ref[7:8, :]
    tok_ref[...] = result.astype(bf16)
    per = sum_ref.shape[0] // SEG_LEN
    for index in range(per):
        row = jnp.broadcast_to(result[index * SEG_LEN : index * SEG_LEN + 1, :][None], (cls_ref.shape[0], 1, width))
        cls_ref[:, pl.ds(pl.program_id(0) * per + index, 1), :] = row


def ffn_bwd_kernel(
    layout, ready, place_ref, cot_ref, cls_ref, second_ref, sum_ref, slope_ref, small_ref,
    branch_ref, inner_ref, first_ref, low_ref, sums_ref, vec_ref,
):
    width = sum_ref.shape[1]
    load_vec(small_ref, *layout, vec_ref)
    per = sum_ref.shape[0] // SEG_LEN
    begin = pl.program_id(0) * per
    if cls_ref.shape[0] > per * pl.num_programs(0):
        begin = begin + (place_ref[0] * 2 + place_ref[1]) * (per * pl.num_programs(0))

    @pl.when(pl.program_id(0) == 0)
    def _():
        sums_ref[...] = jnp.zeros_like(sums_ref)

    place = lax.broadcasted_iota(jnp.int32, (SEG_LEN, 1), 0) == 0
    parts = []
    for index in range(sum_ref.shape[0] // SEG_LEN):
        rows = cot_ref[index * SEG_LEN : (index + 1) * SEG_LEN, :].astype(f32)
        parts.append(rows + jnp.where(place, cls_ref[pl.ds(begin + index, 1), :], 0.0))
    grad = jnp.concatenate(parts, 0)
    unit, inverse = normalise(second_ref[...])
    sums_ref[6:7, :] += column_sum(grad * unit)
    sums_ref[7:8, :] += column_sum(grad)
    second_grad = norm_back(grad, unit, inverse, vec_ref[6:7, :])
    branch = second_grad.astype(bf16)
    branch_ref[...] = branch
    sums_ref[5:6, :] += column_sum(branch.astype(f32))
    up_ref = ready(0)
    down_ref = ready(1)
    total = second_grad
    for part in range(4):
        cols = pl.ds(part * width, width)
        act_grad = dot_nn(branch, down_ref[:, cols])
        inner = (act_grad * slope_ref[:, cols].astype(f32)).astype(bf16)
        inner_ref[:, cols] = inner
        sums_ref[8 + part : 9 + part, :] += column_sum(inner.astype(f32))
        total = total + dot_nt(inner, up_ref[:, cols])
    unit, inverse = normalise(sum_ref[...])
    sums_ref[3:4, :] += column_sum(total * unit)
    sums_ref[4:5, :] += column_sum(total)
    first = norm_back(total, unit, inverse, vec_ref[3:4, :])
    first_ref[...] = first
    low = first.astype(bf16)
    low_ref[...] = low
    sums_ref[2:3, :] += column_sum(low.astype(f32))


def attn_bwd_kernel(ready, first_ref, low_ref, qkv_ref, qkv_grad_ref, x_grad_ref, sums_ref, mixed_grad):
    width = first_ref.shape[1]

    @pl.when(pl.program_id(0) == 0)
    def _():
        sums_ref[...] = jnp.zeros_like(sums_ref)

    w_ref = ready(0)
    mixed_grad[...] = dot_nt(low_ref[...], w_ref[:, 3 * width :]).astype(bf16)
    for start in range(0, first_ref.shape[0], SEG_LEN):
        heads_backward(qkv_ref, mixed_grad, qkv_grad_ref, pl.ds(start, SEG_LEN), width, None)
    qkv_grad = qkv_grad_ref[...]
    x_grad_ref[...] = first_ref[...] + dot_nt(qkv_grad, w_ref[:, : 3 * width])
    sums_ref[0:1, :] += column_sum(qkv_grad[:, :width].astype(f32))
    sums_ref[1:2, :] += column_sum(qkv_grad[:, 2 * width :].astype(f32))


def cross_kernel(
    single, layout, ready, place_ref, x_ref, cot_ref, key_own_ref, key_all_ref, small_ref,
    out_ref, x_grad_ref, grads_ref, sums_ref,
    qkv_ref, qkv_grad_ref, mixed_ref, mixed_grad, slope, act_ref, inner_ref, vec_ref, grad_ref,
):
    own = layout[1]
    load_vec(small_ref, *layout, vec_ref)
    width = x_ref.shape[1]
    count = x_ref.shape[0]
    rows = pl.ds(0, count)

    @pl.when(pl.program_id(0) == 0)
    def _():
        sums_ref[...] = jnp.zeros_like(sums_ref)

    attn_ref = ready(0)
    mask = key_own_ref[...] == key_all_ref[0]
    entry = x_ref[...]
    low_in = entry.astype(bf16)
    qkv = dot_nn(low_in, attn_ref[:, : 3 * width]) + qkv_bias(vec_ref)
    qkv_ref[...] = qkv.astype(bf16)
    heads_forward(qkv_ref, mixed_ref, rows, width, mask)
    first_sum = entry + dot_nn(mixed_ref[...], attn_ref[:, 3 * width :]) + vec_ref[2:3, :]
    unit_one, inverse_one = normalise(first_sum)
    normed = unit_one * vec_ref[3:4, :] + vec_ref[4:5, :]
    low = normed.astype(bf16)
    up_ref = ready(1)
    down_ref = ready(2)
    total = normed + vec_ref[5:6, :]
    for part in range(4):
        cols = pl.ds(part * width, width)
        inner = dot_nn(low, up_ref[:, cols]) + vec_ref[8 + part : 9 + part, :]
        act, rate = gelu_parts(inner)
        act = act.astype(bf16)
        act_ref[:, cols] = act
        slope[:, cols] = rate
        total = total + dot_nt(act, down_ref[:, cols])
    unit_two, inverse_two = normalise(total)
    out_ref[...] = (unit_two * vec_ref[6:7, :] + vec_ref[7:8, :]).astype(bf16)

    if single:
        for part in range(small_ref.shape[0]):
            for at in range(width // 128):
                tile = small_ref[part, at * 8 : (at + 1) * 8, :]
                grad_ref[part * 8 : (part + 1) * 8, at * 128 : (at + 1) * 128] = tile.astype(f32)
        grad = grad_ref[...]
    else:
        grad = cot_ref[...].astype(f32)
    sums_ref[6:7, :] += column_sum(grad * unit_two)
    sums_ref[7:8, :] += column_sum(grad)
    second_grad = norm_back(grad, unit_two, inverse_two, vec_ref[6:7, :])
    branch = second_grad.astype(bf16)
    sums_ref[5:6, :] += column_sum(branch.astype(f32))
    total = second_grad
    for part in range(4):
        cols = pl.ds(part * width, width)
        inner = (dot_nn(branch, down_ref[:, cols]) * slope[:, cols]).astype(bf16)
        inner_ref[:, cols] = inner
        sums_ref[8 + part : 9 + part, :] += column_sum(inner.astype(f32))
        total = total + dot_nt(inner, up_ref[:, cols])
    sums_ref[3:4, :] += column_sum(total * unit_one)
    sums_ref[4:5, :] += column_sum(total)
    first = norm_back(total, unit_one, inverse_one, vec_ref[3:4, :])
    attn_low = first.astype(bf16)
    sums_ref[2:3, :] += column_sum(attn_low.astype(f32))
    mixed_grad[...] = dot_nt(attn_low, attn_ref[:, 3 * width :]).astype(bf16)
    heads_backward(qkv_ref, mixed_grad, qkv_grad_ref, rows, width, mask)
    qkv_grad = qkv_grad_ref[...]
    x_grad_ref[...] = first + dot_nt(qkv_grad, attn_ref[:, : 3 * width])
    sums_ref[0:1, :] += column_sum(qkv_grad[:, :width].astype(f32))
    sums_ref[1:2, :] += column_sum(qkv_grad[:, 2 * width :].astype(f32))

    begin = (place_ref[0] * 2 + place_ref[1]) * own
    spot = lax.broadcasted_iota(jnp.int32, (width, own), 0) - lax.broadcasted_iota(jnp.int32, (width, own), 1)
    chosen = (spot == begin).astype(f32).astype(bf16)
    start = 0
    for left, right in ((low_in, qkv_grad), (mixed_ref[...], attn_low), (low, inner_ref[...]), (branch, act_ref[...])):
        cols = right.shape[1]
        grad = dot_tn(dot_nn(left, chosen).astype(bf16), right)
        if single:
            grads_ref[:, start : start + cols] = grad.astype(bf16)
        else:

            @pl.when(pl.program_id(0) == 0)
            def _(start=start, cols=cols):
                grads_ref[:, start : start + cols] = jnp.zeros((own, cols), f32)

            grads_ref[:, start : start + cols] += grad
        start += cols
    if single:
        sums = sums_ref[0:12, :]
        sums = jnp.concatenate([sums[:, : width // 2], sums[:, width // 2 :]], 0).astype(bf16)
        grads_ref[:, start:] = jnp.concatenate([sums] * (own // 24), 0)


def row_spec(width, block=BLOCK):
    return pl.BlockSpec((block, width), lambda i: (i, 0))


def whole_spec(shape):
    return pl.BlockSpec(shape, lambda i: (0,) * len(shape), pipeline_mode=pl.Buffered(1))


def fixed_spec(shape):
    return pl.BlockSpec(shape, lambda i: (0,) * len(shape))


def params():
    return pltpu.CompilerParams(dimension_semantics=("arbitrary",), vmem_limit_bytes=VMEM_LIMIT)


def shaped(*dims, dtype=bf16):
    return jax.ShapeDtypeStruct(dims, dtype)


def cost(flops, nbytes, trans=0):
    return pl.CostEstimate(flops=int(flops), bytes_accessed=int(nbytes), transcendentals=int(trans))


def attn_forward(flat, place, attn, small, layout):
    rows, width = flat.shape
    weights = Weights(attn)
    return pl.pallas_call(
        weights.wrap(partial(attn_fwd_kernel, layout)),
        grid=(rows // BLOCK,),
        in_specs=weights.specs() + [row_spec(width), whole_spec(small.shape)],
        out_specs=[row_spec(3 * width), row_spec(width), row_spec(width)],
        out_shape=[shaped(rows, 3 * width), shaped(rows, width), shaped(rows, width, dtype=f32)],
        scratch_shapes=[pltpu.VMEM((16, width), f32)] + weights.scratch(),
        compiler_params=params(),
        cost_estimate=cost(2 * rows * width * (4 * width + 2 * SEG_LEN), rows * width * 14 + width * width * 8),
        name="seg_attn_fwd",
    )(*weights.arrays(place), flat, small)


def ffn_forward(first_sum, place, up_proj, down_proj, small, layout, parts):
    rows, width = first_sum.shape
    inner = up_proj.shape[1]
    weights = Weights(up_proj, down_proj)
    cls_shape = (parts, rows // SEG_LEN, width)
    cls_spec = fixed_spec(cls_shape)
    return pl.pallas_call(
        weights.wrap(partial(ffn_fwd_kernel, layout)),
        grid=(rows // BLOCK,),
        in_specs=weights.specs() + [row_spec(width), whole_spec(small.shape)],
        out_specs=[row_spec(width), row_spec(inner), row_spec(inner), row_spec(width), row_spec(width), cls_spec],
        out_shape=[
            shaped(rows, width), shaped(rows, inner), shaped(rows, inner), shaped(rows, width, dtype=f32),
            shaped(rows, width), shaped(*cls_shape, dtype=f32),
        ],
        scratch_shapes=[pltpu.VMEM((16, width), f32)] + weights.scratch(),
        compiler_params=params(),
        cost_estimate=cost(4 * rows * width * inner, rows * (width * 12 + inner * 4) + width * inner * 4, 2 * rows * inner),
        name="seg_ffn_fwd",
    )(*weights.arrays(place), first_sum, small)


def ffn_backward(cot, cls_grad, second_sum, first_sum, slope, place, up_proj, down_proj, small, layout):
    rows, width = first_sum.shape
    inner = up_proj.shape[1]
    weights = Weights(up_proj, down_proj)
    cls_spec = whole_spec(cls_grad.shape)
    return pl.pallas_call(
        weights.wrap(partial(ffn_bwd_kernel, layout), with_place=True),
        grid=(rows // BLOCK,),
        in_specs=weights.specs() + [
            row_spec(width), cls_spec, row_spec(width), row_spec(width), row_spec(inner), whole_spec(small.shape),
        ],
        out_specs=[row_spec(width), row_spec(inner), row_spec(width), row_spec(width), fixed_spec((16, width))],
        out_shape=[
            shaped(rows, width), shaped(rows, inner), shaped(rows, width, dtype=f32), shaped(rows, width),
            shaped(16, width, dtype=f32),
        ],
        scratch_shapes=[pltpu.VMEM((16, width), f32)] + weights.scratch(),
        compiler_params=params(),
        cost_estimate=cost(4 * rows * width * inner, rows * (width * 16 + inner * 4) + width * inner * 4),
        name="seg_ffn_bwd",
    )(*weights.arrays(place), cot, cls_grad, second_sum, first_sum, slope, small)


def attn_backward(first_grad, attn_low, qkv, place, attn, share, shares, before=()):
    rows, width = first_grad.shape
    weights = Weights(attn)
    steps = rows // BLOCK // shares
    spec = lambda cols: pl.BlockSpec((BLOCK, cols), lambda i: (i + share * steps, 0))
    kept = len(before)
    args = weights.arrays(place) + [first_grad, attn_low, qkv]

    def body(ready, *refs):
        attn_bwd_kernel(ready, *refs[:3], *refs[3 + kept :])

    return pl.pallas_call(
        weights.wrap(body),
        grid=(steps,),
        in_specs=weights.specs() + [spec(width), spec(width), spec(3 * width)] + [pl.BlockSpec(memory_space=pl.ANY)] * kept,
        out_specs=[spec(3 * width), spec(width), fixed_spec((8, width))],
        out_shape=[shaped(rows, 3 * width), shaped(rows, width, dtype=f32), shaped(8, width, dtype=f32)],
        input_output_aliases={len(args) + at: at for at in range(kept)},
        scratch_shapes=[pltpu.VMEM((BLOCK, width), bf16)] + weights.scratch(),
        compiler_params=params(),
        cost_estimate=cost(
            2 * rows * width * (4 * width + 5 * SEG_LEN) // shares, rows * width * 22 // shares + width * width * 8
        ),
        name="seg_attn_bwd",
    )(*args, *before)


def cross_layer(entry, cot, row_key, blocks, place, attn, up_proj, down_proj, small, layout):
    rows, width = entry.shape
    inner = up_proj.shape[1]
    block = rows // blocks
    spec = partial(row_spec, block=block)
    weights = Weights(attn, up_proj, down_proj)
    own = layout[1]
    both = jnp.tile(row_key.reshape(blocks, 1, block), (1, 1, 2))
    wide = (own, 3 * inner + (width // 2 if by_links() else 0))
    return pl.pallas_call(
        weights.wrap(partial(cross_kernel, by_links(), layout), with_place=True),
        grid=(blocks,),
        in_specs=weights.specs() + [
            spec(width), spec(width), spec(1), pl.BlockSpec((1, 1, 2 * block), lambda i: (i, 0, 0)), whole_spec(small.shape),
        ],
        out_specs=[spec(width), spec(width), fixed_spec(wide), fixed_spec((16, width))],
        out_shape=[
            shaped(rows, width), shaped(rows, width, dtype=f32), shaped(*wide, dtype=bf16 if by_links() else f32),
            shaped(16, width, dtype=f32),
        ],
        scratch_shapes=[
            pltpu.VMEM((block, 3 * width), bf16), pltpu.VMEM((block, 3 * width), bf16), pltpu.VMEM((block, width), bf16),
            pltpu.VMEM((block, width), bf16), pltpu.VMEM((block, inner), f32), pltpu.VMEM((block, inner), bf16),
            pltpu.VMEM((block, inner), bf16), pltpu.VMEM((16, width), f32), pltpu.VMEM((block, width), f32),
        ] + weights.scratch(),
        compiler_params=params(),
        cost_estimate=cost(24 * rows * width * 4 * width, rows * width * 40 + width * inner * 6),
        name="cross_layer",
    )(*weights.arrays(place), entry, cot, row_key.reshape(rows, 1), both, small)


def hop_seg(value, hops):
    size = lax.axis_size("seg")
    return lax.ppermute(value, "seg", [(at, (at + 2 * hops) % size) for at in range(size)])


def swap_core(value):
    return lax.ppermute(value, "seg", [(at, at ^ 1) for at in range(lax.axis_size("seg"))])


def swap_batch(value, flip):
    return lax.ppermute(value, "batch", [(at, at ^ flip) for at in range(lax.axis_size("batch"))])


def fence(*values):
    return lax.optimization_barrier(values)


def by_links():
    return lax.axis_size("batch") == 4 and lax.axis_size("seg") == 8


class Gather:
    def __init__(self, *shards):
        self.many = len(shards)
        self.own, self.cols = shards[0].shape
        self.quarter = self.cols // 4
        self.mine = jnp.concatenate(shards, 0) if self.many > 1 else shards[0]
        self.part = lax.dynamic_slice_in_dim(self.mine, lax.axis_index("batch") * self.quarter, self.quarter, 1)

    def run_seg(self):
        self.raw = [hop_seg(self.part, hops) for hops in (3, 2, 1)]

    def sort_wide(self, full):
        first = lax.axis_index("seg") // 2 + 1
        self.along = lax.dynamic_slice_in_dim(jnp.concatenate([full, full[:3]], 0), first, 3)

    def run_own(self):
        self.mine_too = swap_core(self.mine)

    def sort_seg(self):
        self.along = jnp.stack(self.raw)

    def run_near(self):
        self.near = [swap_batch(self.along, flip) for flip in (1, 2)]

    def run_far(self):
        half = self.mine.shape[0] // 2
        self.far = [swap_batch(self.near[1][:, :half], 1), swap_batch(self.near[0][:, half:], 2)]

    def run_core_along(self):
        self.along_too = swap_core(self.along)

    def run_core_near(self, joined):
        self.joined = joined
        if joined:
            self.near = [jnp.stack([self.along] + self.near)]
            self.near_too = [swap_core(array) for array in self.near]
        else:
            self.near_too = [self.along_too] + [swap_core(array) for array in self.near]
            self.near = [self.along] + self.near

    def run_core_far(self):
        self.far_too = [swap_core(array) for array in self.far]

    def pieces(self):
        own, cols, quarter = self.own, self.cols, self.quarter
        half = self.mine.shape[0] // 2
        arrays = [self.mine] + self.near + self.far + [self.mine_too] + self.near_too + self.far_too
        many = len(self.near)
        matrices = []
        for at in range(self.many):
            first, last = at * own, (at + 1) * own
            blocks = []
            for core in (0, 1):

                def chip(later, core=core):
                    return lambda z, c: (((z + 1 + later) & 3) * 2 + (c ^ core)) * own

                target = lambda z, c, q, core=core: ((z * 2 + (c ^ core)) * own, 0)
                blocks.append(((many + 3) * core, (slice(first, last), slice(None)), (own, cols), target))
                for later in range(3):
                    row = chip(later)
                    for flip in range(3):
                        target = lambda z, c, q, row=row, flip=flip: (row(z, c), (q ^ flip) * quarter)
                        source = (later, slice(first, last), slice(None))
                        where = (many + 3) * core + 1
                        source, where = ((flip,) + source, where) if self.joined else (source, where + flip)
                        blocks.append((where, source, (own, quarter), target))
                    for side in (0, 1):
                        lo, hi = max(first, side * half), min(last, (side + 1) * half)
                        if lo >= hi:
                            continue
                        target = lambda z, c, q, row=row, skip=lo - first: (row(z, c) + skip, (q ^ 3) * quarter)
                        source = (later, slice(lo - side * half, hi - side * half), slice(None))
                        blocks.append(((many + 3) * core + many + 1 + side, source, (hi - lo, quarter), target))
            matrices.append(Pieces((own * lax.axis_size("seg"), cols), arrays, blocks))
        return matrices


def gather_plain(shard):
    full = lax.all_gather(shard, "seg", axis=0, tiled=True)
    block = (0, (slice(None), slice(None)), full.shape, lambda z, c, q: (0, 0))
    return Pieces(full.shape, [full], [block])


def chips_exchange(value):
    return lax.all_to_all(value, "seg", 0, 0, axis_index_groups=CHIP_GROUPS, tiled=True)


def gather_seg(value):
    if not by_links():
        return lax.all_gather(value, "seg", axis=0, tiled=False)
    copies = jnp.broadcast_to(value, (lax.axis_size("seg"),) + value.shape)
    return lax.all_to_all(copies, "seg", 0, 0, tiled=True)


def plain_grad_kernel(steps, *refs):
    pairs, (out_ref,) = refs[: 2 * len(steps)], refs[2 * len(steps) :]
    begin = 0
    for at, many in enumerate(steps):

        @pl.when((pl.program_id(0) >= begin) & (pl.program_id(0) < begin + many))
        def _(at=at):
            out_ref[...] = dot_tn(pairs[2 * at][...], pairs[2 * at + 1][...]).astype(bf16)

        begin += many


def plain_grads(*pairs):
    rows, width = pairs[0][0].shape
    steps = tuple(right.shape[1] // width for _, right in pairs)
    in_specs = []
    begin = 0
    for many in steps:
        in_specs.append(whole_spec((rows, width)))
        in_specs.append(pl.BlockSpec((rows, width), lambda i, begin=begin, many=many: (0, jnp.clip(i - begin, 0, many - 1))))
        begin += many
    return pl.pallas_call(
        partial(plain_grad_kernel, steps),
        grid=(begin,),
        in_specs=in_specs,
        out_specs=pl.BlockSpec((width, width), lambda i: (0, i)),
        out_shape=shaped(width, begin * width),
        compiler_params=params(),
        cost_estimate=cost(2 * rows * width * width * begin, 2 * (rows + width) * width * begin),
        name="plain_weight_grads",
    )(*[array for pair in pairs for array in pair])


def weight_grad_kernel(steps, place_ref, *refs):
    pairs, (keep_ref, send_ref, acc_ref) = refs[: 2 * len(steps)], refs[2 * len(steps) :]
    step = pl.program_id(0)
    begin = 0
    for at, many in enumerate(steps):

        @pl.when((step >= begin) & (step < begin + many))
        def _(at=at):
            acc_ref[...] = dot_tn(pairs[2 * at][...], pairs[2 * at + 1][...])

        begin += many
    c, q = place_ref[1], place_ref[2]
    size = keep_ref.shape[2]
    for flip in range(4):
        for chip in range(4):
            for core, out_ref in ((0, keep_ref), (1, send_ref)):
                row = (chip * 2 + (c ^ core)) * (4 * size) + (q ^ flip) * size
                rows = pl.ds(pl.multiple_of(row, size), size)
                out_ref[flip, chip] = acc_ref[rows, :].astype(bf16)


def weight_grads(place, *pairs):
    rows, width = pairs[0][0].shape
    steps = tuple(right.shape[1] // width for _, right in pairs)
    size = width // 32
    in_specs = [pl.BlockSpec(memory_space=pltpu.SMEM)]
    begin = 0
    for many in steps:
        in_specs.append(whole_spec((rows, width)))
        in_specs.append(pl.BlockSpec((rows, width), lambda i, begin=begin, many=many: (0, jnp.clip(i - begin, 0, many - 1))))
        begin += many
    out_spec = pl.BlockSpec((4, 4, size, width), lambda i: (0, 0, 0, i))
    out = shaped(4, 4, size, begin * width)
    return pl.pallas_call(
        partial(weight_grad_kernel, steps),
        grid=(begin,),
        in_specs=in_specs,
        out_specs=[out_spec, out_spec],
        out_shape=[out, out],
        scratch_shapes=[pltpu.VMEM((width, width), f32)],
        compiler_params=params(),
        cost_estimate=cost(2 * rows * width * width * begin, 2 * (rows + width) * width * begin),
        name="weight_grads",
    )(place, *[array for pair in pairs for array in pair])


def wide_sum(first, *others):
    total = first.astype(f32)
    for other in others:
        total = total + other.astype(f32)
    return total


def batch_spread(value):
    value = value.astype(bf16)
    return [value] + [swap_batch(value, flip) for flip in (1, 2, 3)]


def core_sums(keep, got):
    sums = [wide_sum(keep[flip], got[flip]) for flip in range(4)]
    return sums[0], [part.astype(bf16) for part in sums[1:]]


def batch_swaps(parts):
    return [swap_batch(part, flip) for flip, part in zip((1, 2, 3), parts)]


def place_kernel(plan, place_ref, *refs):
    count = 4 * len(plan)
    blocks, outs = refs[:count], refs[count:]
    q = place_ref[2]
    for at, targets in enumerate(plan):
        for flip in range(4):
            block = blocks[4 * at + flip]
            size = block.shape[0]
            rows = pl.ds(pl.multiple_of((q ^ flip) * size, size), size)
            for source, index, target, cols in targets:
                outs[index][rows, target : target + cols] = block[:, source : source + cols].astype(f32)


def place_outputs(place, plan, groups, own, shape):
    vmem = pl.BlockSpec(memory_space=pltpu.VMEM)
    return pl.pallas_call(
        partial(place_kernel, plan),
        in_specs=[pl.BlockSpec(memory_space=pltpu.SMEM)] + [vmem] * (4 * len(groups)),
        out_specs=[vmem] * own,
        out_shape=[jax.ShapeDtypeStruct(shape, f32)] * own,
        compiler_params=pltpu.CompilerParams(vmem_limit_bytes=VMEM_LIMIT),
        cost_estimate=cost(0, own * shape[0] * shape[1] * 6),
        name="place_outputs",
    )(place, *[block for group in groups for block in group])


def scatter_sum(matrix):
    return lax.psum_scatter(matrix.astype(bf16), "seg", scatter_dimension=0, tiled=True)


def local(
    hidden, seg_doc, seg_attn, seg_up, seg_down, seg_vec,
    cross_attn, cross_up, cross_down, cross_vec, tok_cot, cls_cot,
):
    micro, _, segments, _, length, width = hidden.shape
    own, cols = seg_attn.shape
    parts = lax.axis_size("seg")
    place = lax.axis_index("seg")
    count = micro * segments
    total = parts * count
    spot = jnp.stack([place // 2, place % 2, lax.axis_index("batch")]).astype(jnp.int32)

    flat = hidden.reshape(count * length, width)
    tiles = width // 128
    vecs = jnp.pad(jnp.concatenate([seg_vec.T, cross_vec.T], 0), ((0, 0), (0, 128 - own)))
    small = cls_cot.reshape(count, tiles, 128).transpose(1, 0, 2).reshape(count * tiles, 128)
    small = jnp.concatenate([small, vecs], 0)
    seg_layout, cross_layout = (count * tiles, own), (count * tiles + 12, own)

    docs = seg_doc[:, 0].reshape(micro, segments, parts) + (1 << 16) * jnp.arange(micro, dtype=jnp.int32)[:, None, None]
    docs = docs.transpose(2, 0, 1)
    blocks = micro if total > 256 else 1
    if blocks > 1:
        order = lambda rows: rows.reshape(parts, micro, segments, -1).transpose(1, 0, 2, 3).reshape(total, -1)
        back = lambda rows: rows.reshape(micro, parts, segments, -1).transpose(1, 0, 2, 3).reshape(total, -1)
        row_key = docs.transpose(1, 0, 2).reshape(total)
    else:
        order = back = lambda rows: rows
        row_key = docs.reshape(total)
    if by_links():
        one, two, three = Gather(seg_attn), Gather(seg_up, seg_down), Gather(cross_up, cross_down)
        one.run_seg()
        small = gather_seg(small)
        one.run_own()
        one.raw, small, two.part, two.mine = fence(one.raw, small, two.part, two.mine)
        one.sort_seg()
        one.run_near()
        two.run_seg()
        (one.near,) = fence(one.near)
        one.run_far()
        wide = jnp.broadcast_to(three.part, (4,) + three.part.shape)
        one.far, one.near, two.raw, wide, two.mine, three.mine, row_key = fence(
            one.far, one.near, two.raw, wide, two.mine, three.mine, row_key
        )
        two.sort_seg()
        two.run_near()
        two.run_core_along()
        full = chips_exchange(wide)
        one.run_core_near(True)
        one.run_core_far()
        (attn_full,) = one.pieces()
        outs = attn_forward(flat, spot, attn_full, small, seg_layout)
        two.run_own()
        three.run_own()
        (qkv, mixed, first_sum), two.near, two.along_too, full, cross_attn, two.mine_too, three.mine_too = fence(
            outs, two.near, two.along_too, full, cross_attn, two.mine_too, three.mine_too
        )
        cross_attn_full = gather_plain(cross_attn)
        two.run_far()
        two.run_core_near(False)
        (two.far, full) = fence(two.far, full)
        three.sort_wide(full)
        three.run_near()
        two.run_core_far()
        three.run_core_along()
        up_full, down_full = two.pieces()
        outs = ffn_forward(first_sum, spot, up_full, down_full, small, seg_layout, parts)
        (normed, act, slope, second_sum, tok, cls), three.near, three.along_too = fence(outs, three.near, three.along_too)
        three.run_far()
        entry = lax.all_to_all(cls, "seg", 0, 0, tiled=True).reshape(total, width)
        cot_all = entry
        three.run_core_near(False)
        entry, three.far = fence(entry, three.far)
        three.run_core_far()
        cross_up_full, cross_down_full = three.pieces()
    else:
        attn_full, up_full, down_full = [gather_plain(shard) for shard in (seg_attn, seg_up, seg_down)]
        cross_attn_full, cross_up_full, cross_down_full = [
            gather_plain(shard) for shard in (cross_attn, cross_up, cross_down)
        ]
        small = gather_seg(small)
        cot_all = small[:, : count * tiles].reshape(parts, tiles, count, 128).transpose(0, 2, 1, 3).reshape(total, width)
        qkv, mixed, first_sum = attn_forward(flat, spot, attn_full, small, seg_layout)
        normed, act, slope, second_sum, tok, cls = ffn_forward(first_sum, spot, up_full, down_full, small, seg_layout, parts)
        entry = gather_seg(cls[0]).reshape(total, width)

    cls_out, cls_grad, x_grads, x_sums = cross_layer(
        order(entry), order(cot_all), row_key, blocks, spot,
        cross_attn_full, cross_up_full, cross_down_full, small, cross_layout,
    )
    own_cols = lambda rows: lax.dynamic_slice_in_dim(rows, place * own, own, 1)
    own_rows = lambda rows: lax.dynamic_slice_in_dim(back(rows), place * count, count, 0)
    cls_out = own_rows(cls_out)
    if not by_links():
        cls_grad = own_rows(cls_grad)
    outs = ffn_backward(
        tok_cot.reshape(count * length, width),
        cls_grad, second_sum, first_sum, slope, spot, up_full, down_full, small, seg_layout,
    )

    if by_links():
        folded = lambda rows: jnp.concatenate([rows[:, : width // 2], rows[:, width // 2 :]], 0)
        unfolded = lambda rows: jnp.concatenate([rows[:12], rows[12:]], 1)
        x_came = lax.all_to_all(x_grads.reshape(4, own // 4, 3 * cols + width // 2), "batch", 0, 0, tiled=True)
        (branch, inner, first_grad, attn_low, ffn_sums), x_came = fence(outs, x_came)
        x_sum = jnp.sum(x_came.astype(f32), 0)
        cross_sums = unfolded(x_sum[:, 3 * cols :])
        x_low = x_sum[:, : 3 * cols].astype(bf16)
        x_low, branch = fence(x_low, branch)
        x_near = [swap_batch(x_low, flip) for flip in (1, 2)]
        down_grad = plain_grads((branch, act))
        down_grad, x_near, x_low, inner = fence(down_grad, x_near, x_low, inner)
        down_part = lax.psum_scatter(down_grad, "seg", scatter_dimension=0, tiled=True)
        x_far = swap_batch(x_low, 3)
        keep_up, send = weight_grads(spot, (normed, inner), (mixed, attn_low))
        keep_up, send, x_far, attn_low = fence(keep_up, send, x_far, attn_low)
        set_cross = [x_low] + x_near + [x_far]
        stay_up, leave = core_sums(keep_up, swap_core(send))
        leave, attn_low = fence(leave, attn_low)
        near_up = [swap_batch(leave[0], 1), swap_batch(leave[1], 2)]
        outs = attn_backward(first_grad, attn_low, qkv, spot, attn_full, 0, 1)
        (qkv_grad, hidden_grad, attn_sums), near_up, last = fence(outs, near_up, leave[2])
        far_up = swap_batch(last, 3)
        sums = folded(jnp.concatenate([attn_sums[:2], ffn_sums[2:12]], 0))
        sums_too = swap_core(sums)
        keep, send = weight_grads(spot, (flat, qkv_grad))
        keep, send, sums, sums_too, far_up = fence(keep, send, sums, sums_too, far_up)
        got = swap_core(send)
        total_up = wide_sum(stay_up, *near_up, far_up).astype(bf16)
        raw_up = chips_exchange(total_up)
        sums = jnp.broadcast_to(sums + sums_too, (4, 24, width // 2))
        stay, leave = core_sums(keep, got)
        stay = jnp.concatenate([stay, sums], 2)
        leave = [jnp.concatenate([part, sums.astype(bf16)], 2) for part in leave]
        came = [swap_batch(part, flip) for flip, part in zip((1, 2, 3), leave)]
        came, raw_up, down_part = fence(came, raw_up, down_part)
        total_qkv = wide_sum(stay, *came).astype(bf16)
        raw = chips_exchange(total_qkv)
        batch_place = lax.axis_index("batch")
        shares = [lax.dynamic_slice_in_dim(down_part, (batch_place ^ flip) * (own // 4), own // 4, 0) for flip in range(4)]
        down_came = [swap_batch(shares[flip], flip) for flip in (1, 2, 3)]
        up_low = jnp.sum(raw_up.astype(f32), 0).astype(bf16)
        set_up = batch_spread(up_low)
        raw, down_came = fence(raw, down_came)
        last = jnp.sum(raw.astype(f32), 0)
        seg_sums = unfolded(last[:, 3 * width :])
        set_qkv = batch_spread(last[:, : 3 * width])
        set_down = batch_spread(wide_sum(shares[0], *down_came))
        shape = (own, cols)
        x_plan = (((0, 0, 0, cols), (cols, 1, 0, cols), (2 * cols, 2, 0, cols)),)
        x_placed = place_outputs(spot, x_plan, (set_cross,), 3, shape)
        (down_placed,) = place_outputs(spot, (((0, 0, 0, cols),),), (set_down,), 1, shape)
        (up_placed,) = place_outputs(spot, (((0, 0, 0, cols),),), (set_up,), 1, shape)
        attn_plan = (((0, 0, 0, 3 * width),), ((cols, 0, 3 * width, width),))
        (attn_placed,) = place_outputs(spot, attn_plan, (set_qkv, set_up), 1, shape)
        grads = [attn_placed, up_placed, down_placed] + list(x_placed)
    else:
        branch, inner, first_grad, attn_low, ffn_sums = outs
        qkv_grad, hidden_grad, attn_sums = attn_backward(first_grad, attn_low, qkv, spot, attn_full, 0, 1)
        x_grads = x_grads.astype(bf16)
        grads = [
            scatter_sum(jnp.concatenate([dot_tn(flat, qkv_grad), dot_tn(mixed, attn_low)], 1)),
            scatter_sum(dot_tn(normed, inner)), scatter_sum(dot_tn(branch, act)),
            x_grads[:, :cols], x_grads[:, cols : 2 * cols], x_grads[:, 2 * cols :],
        ]
        grads = [grad.astype(f32) for grad in lax.psum(tuple(grads), "batch")]
        seg_sums = lax.psum(jnp.concatenate([attn_sums[:2], ffn_sums[2:12]], 0), ("batch", "seg"))
        cross_sums = lax.psum(x_sums[:12], "batch")
    seg_vec_grad = own_cols(seg_sums).T
    cross_vec_grad = own_cols(cross_sums).T
    return (
        tok.reshape(hidden.shape), cls_out.reshape(cls_cot.shape), hidden_grad.reshape(hidden.shape),
        grads[0], grads[1], grads[2], seg_vec_grad, grads[3], grads[4], grads[5], cross_vec_grad,
    )


def solution(mesh):
    wide = P(None, "batch", None, "seg", None, None)
    rows = P("seg", None)
    cls = P(None, "batch", None, "seg", None)
    in_specs = (wide, P(None, "batch", None)) + (rows,) * 8 + (wide, cls)
    out_specs = (wide, cls, wide) + (rows,) * 8
    return jax.shard_map(local, mesh=mesh, in_specs=in_specs, out_specs=out_specs, check_vma=False)
```

```python
from functools import partial

import jax
import jax.numpy as jnp
from jax import lax
from jax.experimental import pallas as pl
from jax.experimental.pallas import tpu as pltpu
from jax.sharding import PartitionSpec as P

HEADS = 12
HEAD_DIM = 64
SEG_LEN = 128
PAIRS = HEADS // 2
PAIR = 2 * HEAD_DIM
GROUP = 6

NEG_FILL = -1e30
LN_EPS = 1e-05
SCALE = HEAD_DIM ** (-0.5)
ROOT_HALF = 0.7071067811865476
PDF_AT_ZERO = 0.3989422804014327
BLOCK = 256
CHIP_GROUPS = [[0, 2, 4, 6], [1, 3, 5, 7]]
VMEM_LIMIT = 60 * 1024 * 1024

f32 = jnp.float32
bf16 = jnp.bfloat16


def dot_nn(left, right):
    return lax.dot_general(left, right, (((1,), (0,)), ((), ())), preferred_element_type=f32)


def dot_nt(left, right):
    return lax.dot_general(left, right, (((1,), (1,)), ((), ())), preferred_element_type=f32)


def dot_tn(left, right):
    return lax.dot_general(left, right, (((0,), (0,)), ((), ())), preferred_element_type=f32)


def normalise(rows):
    centred = rows - jnp.mean(rows, -1, keepdims=True)
    spread = jnp.mean(centred * centred, -1, keepdims=True)
    inverse = lax.rsqrt(spread + LN_EPS)
    return centred * inverse, inverse


def norm_back(grad, unit, inverse, gain):
    scaled = grad * gain
    return inverse * (
        scaled
        - jnp.mean(scaled, -1, keepdims=True)
        - unit * jnp.mean(scaled * unit, -1, keepdims=True)
    )


def column_sum(rows):
    return jnp.sum(rows, 0, keepdims=True)


def gelu_parts(value):
    cdf = 0.5 * (1.0 + lax.erf(value * ROOT_HALF))
    pdf = PDF_AT_ZERO * jnp.exp(-0.5 * value * value)
    return value * cdf, cdf + value * pdf


def first_half(rows):
    return lax.broadcasted_iota(jnp.int32, (rows, PAIR), 1) < HEAD_DIM


def split_heads(rows, first):
    zero = jnp.zeros_like(rows)
    return jnp.concatenate([jnp.where(first, rows, zero), jnp.where(first, zero, rows)], 0)


def join_heads(stacked, first):
    rows = stacked.shape[0] // 2
    return jnp.where(first, stacked[:rows], stacked[rows:])


def pair_probs(query, keys, mask):
    scores = dot_nt(keys, query) * SCALE
    if mask is not None:
        scores = jnp.where(mask, scores, NEG_FILL)
    top = jnp.max(scores, 0, keepdims=True)
    expo = jnp.exp(scores - top)
    return expo * (1.0 / jnp.sum(expo, 0, keepdims=True))


def pair_parts(qkv_ref, rows, pair, width, first):
    at = pair * PAIR
    query = split_heads(qkv_ref[rows, at : at + PAIR], first)
    return query, qkv_ref[rows, width + at : width + at + PAIR], qkv_ref[rows, 2 * width + at : 2 * width + at + PAIR]


def heads_forward(qkv_ref, out_ref, rows, width, mask):
    first = first_half(rows.size)
    for start in range(0, PAIRS, GROUP):
        pairs = range(start, start + GROUP)
        parts = [pair_parts(qkv_ref, rows, pair, width, first) for pair in pairs]
        probs = [pair_probs(query, keys, mask).astype(bf16) for query, keys, _ in parts]
        mixed = [join_heads(dot_tn(prob, values), first) for prob, (_, _, values) in zip(probs, parts)]
        for pair, value in zip(pairs, mixed):
            out_ref[rows, pair * PAIR : (pair + 1) * PAIR] = value.astype(bf16)


def heads_backward(qkv_ref, grad_ref, out_ref, rows, width, mask):
    first = first_half(rows.size)
    for start in range(0, PAIRS, GROUP):
        pairs = range(start, start + GROUP)
        parts = [pair_parts(qkv_ref, rows, pair, width, first) for pair in pairs]
        grads = [split_heads(grad_ref[rows, pair * PAIR : (pair + 1) * PAIR], first) for pair in pairs]
        probs = [pair_probs(query, keys, mask) for query, keys, _ in parts]
        prob_grads = [dot_nt(values, grad) for (_, _, values), grad in zip(parts, grads)]
        value_grads = [dot_nn(prob.astype(bf16), grad) for prob, grad in zip(probs, grads)]
        score_grads = [
            (prob * (grad - jnp.sum(grad * prob, 0, keepdims=True))).astype(bf16) for prob, grad in zip(probs, prob_grads)
        ]
        key_grads = [dot_nn(grad, query) * SCALE for grad, (query, _, _) in zip(score_grads, parts)]
        query_grads = [join_heads(dot_tn(grad, keys), first) * SCALE for grad, (_, keys, _) in zip(score_grads, parts)]
        for at, values in ((0, query_grads), (width, key_grads), (2 * width, value_grads)):
            for pair, value in zip(pairs, values):
                out_ref[rows, at + pair * PAIR : at + (pair + 1) * PAIR] = value.astype(bf16)


class Pieces:
    def __init__(self, shape, arrays, blocks):
        self.shape, self.arrays, self.blocks = shape, arrays, blocks

    def specs(self):
        return [pl.BlockSpec(memory_space=pl.ANY)] * len(self.arrays)

    def scratch(self):
        return [pltpu.VMEM(self.shape, bf16), pltpu.SemaphoreType.DMA((len(self.blocks),))]

    def copies(self, refs, place_ref, full_ref, sems):
        out = []
        for at, (index, source, size, target) in enumerate(self.blocks):
            row, col = target(place_ref[0], place_ref[1], place_ref[2])
            if not isinstance(row, int):
                row = pl.multiple_of(row, size[0])
            if not isinstance(col, int):
                col = pl.multiple_of(col, size[1])
            view = full_ref.at[pl.ds(row, size[0]), pl.ds(col, size[1])]
            out.append(pltpu.make_async_copy(refs[index].at[source], view, sems.at[at]))
        return out


class Weights:
    def __init__(self, *matrices):
        self.matrices = matrices

    def arrays(self, place):
        return [place] + [array for matrix in self.matrices for array in matrix.arrays]

    def specs(self):
        return [pl.BlockSpec(memory_space=pltpu.SMEM)] + [spec for matrix in self.matrices for spec in matrix.specs()]

    def scratch(self):
        return [item for matrix in self.matrices for item in matrix.scratch()]

    def wrap(self, body, with_place=False):
        many = sum(len(matrix.arrays) for matrix in self.matrices)

        def kernel(place_ref, *refs):
            given, rest = refs[:many], refs[many:]
            cut = len(rest) - 2 * len(self.matrices)
            rest, own = rest[:cut], rest[cut:]
            first = pl.program_id(0) == 0
            views, copies = [], []
            for at, matrix in enumerate(self.matrices):
                views.append(own[2 * at])
                copies.append(partial(matrix.copies, given[: len(matrix.arrays)], place_ref, own[2 * at], own[2 * at + 1]))
                given = given[len(matrix.arrays) :]

            @pl.when(first)
            def _():
                for group in copies:
                    for copy in group():
                        copy.start()

            def ready(at):
                @pl.when(first)
                def _():
                    for copy in copies[at]():
                        copy.wait()

                return views[at]

            body(ready, *([place_ref] if with_place else []), *rest)

        return kernel


def load_vec(small_ref, skip, own, vec_ref):
    @pl.when(pl.program_id(0) == 0)
    def _():
        for part in range(small_ref.shape[0]):
            vec_ref[0:12, part * own : (part + 1) * own] = small_ref[part, skip : skip + 12, :own].astype(f32)


def qkv_bias(vec_ref):
    query = vec_ref[0:1, :]
    return jnp.concatenate([query, jnp.zeros_like(query), vec_ref[1:2, :]], 1)


def attn_fwd_kernel(layout, ready, x_ref, small_ref, qkv_ref, mixed_ref, sum_ref, vec_ref):
    width = x_ref.shape[1]
    load_vec(small_ref, *layout, vec_ref)
    w_ref = ready(0)
    rows = x_ref[...]
    qkv = dot_nn(rows, w_ref[:, : 3 * width]) + qkv_bias(vec_ref)
    qkv_ref[...] = qkv.astype(bf16)
    for start in range(0, x_ref.shape[0], SEG_LEN):
        heads_forward(qkv_ref, mixed_ref, pl.ds(start, SEG_LEN), width, None)
    branch = dot_nn(mixed_ref[...], w_ref[:, 3 * width :])
    sum_ref[...] = rows.astype(f32) + branch + vec_ref[2:3, :]


def ffn_fwd_kernel(layout, ready, sum_ref, small_ref, norm_ref, act_ref, slope_ref, second_ref, tok_ref, cls_ref, vec_ref):
    width = sum_ref.shape[1]
    load_vec(small_ref, *layout, vec_ref)
    up_ref = ready(0)
    down_ref = ready(1)
    unit, _ = normalise(sum_ref[...])
    normed = unit * vec_ref[3:4, :] + vec_ref[4:5, :]
    low = normed.astype(bf16)
    norm_ref[...] = low
    total = normed + vec_ref[5:6, :]
    for part in range(4):
        cols = pl.ds(part * width, width)
        inner = dot_nn(low, up_ref[:, cols]) + vec_ref[8 + part : 9 + part, :]
        act, slope = gelu_parts(inner)
        act = act.astype(bf16)
        act_ref[:, cols] = act
        slope_ref[:, cols] = slope.astype(bf16)
        total = total + dot_nt(act, down_ref[:, cols])
    second_ref[...] = total
    unit, _ = normalise(total)
    result = unit * vec_ref[6:7, :] + vec_ref[7:8, :]
    tok_ref[...] = result.astype(bf16)
    per = sum_ref.shape[0] // SEG_LEN
    for index in range(per):
        row = jnp.broadcast_to(result[index * SEG_LEN : index * SEG_LEN + 1, :][None], (cls_ref.shape[0], 1, width))
        cls_ref[:, pl.ds(pl.program_id(0) * per + index, 1), :] = row


def ffn_bwd_kernel(
    layout, ready, place_ref, cot_ref, cls_ref, second_ref, sum_ref, slope_ref, small_ref,
    branch_ref, inner_ref, first_ref, low_ref, sums_ref, vec_ref,
):
    width = sum_ref.shape[1]
    load_vec(small_ref, *layout, vec_ref)
    per = sum_ref.shape[0] // SEG_LEN
    begin = pl.program_id(0) * per
    if cls_ref.shape[0] > per * pl.num_programs(0):
        begin = begin + (place_ref[0] * 2 + place_ref[1]) * (per * pl.num_programs(0))

    @pl.when(pl.program_id(0) == 0)
    def _():
        sums_ref[...] = jnp.zeros_like(sums_ref)

    place = lax.broadcasted_iota(jnp.int32, (SEG_LEN, 1), 0) == 0
    parts = []
    for index in range(sum_ref.shape[0] // SEG_LEN):
        rows = cot_ref[index * SEG_LEN : (index + 1) * SEG_LEN, :].astype(f32)
        parts.append(rows + jnp.where(place, cls_ref[pl.ds(begin + index, 1), :], 0.0))
    grad = jnp.concatenate(parts, 0)
    unit, inverse = normalise(second_ref[...])
    sums_ref[6:7, :] += column_sum(grad * unit)
    sums_ref[7:8, :] += column_sum(grad)
    second_grad = norm_back(grad, unit, inverse, vec_ref[6:7, :])
    branch = second_grad.astype(bf16)
    branch_ref[...] = branch
    sums_ref[5:6, :] += column_sum(branch.astype(f32))
    up_ref = ready(0)
    down_ref = ready(1)
    total = second_grad
    for part in range(4):
        cols = pl.ds(part * width, width)
        act_grad = dot_nn(branch, down_ref[:, cols])
        inner = (act_grad * slope_ref[:, cols].astype(f32)).astype(bf16)
        inner_ref[:, cols] = inner
        sums_ref[8 + part : 9 + part, :] += column_sum(inner.astype(f32))
        total = total + dot_nt(inner, up_ref[:, cols])
    unit, inverse = normalise(sum_ref[...])
    sums_ref[3:4, :] += column_sum(total * unit)
    sums_ref[4:5, :] += column_sum(total)
    first = norm_back(total, unit, inverse, vec_ref[3:4, :])
    first_ref[...] = first
    low = first.astype(bf16)
    low_ref[...] = low
    sums_ref[2:3, :] += column_sum(low.astype(f32))


def attn_bwd_kernel(ready, first_ref, low_ref, qkv_ref, qkv_grad_ref, x_grad_ref, sums_ref, mixed_grad):
    width = first_ref.shape[1]

    @pl.when(pl.program_id(0) == 0)
    def _():
        sums_ref[...] = jnp.zeros_like(sums_ref)

    w_ref = ready(0)
    mixed_grad[...] = dot_nt(low_ref[...], w_ref[:, 3 * width :]).astype(bf16)
    for start in range(0, first_ref.shape[0], SEG_LEN):
        heads_backward(qkv_ref, mixed_grad, qkv_grad_ref, pl.ds(start, SEG_LEN), width, None)
    qkv_grad = qkv_grad_ref[...]
    x_grad_ref[...] = first_ref[...] + dot_nt(qkv_grad, w_ref[:, : 3 * width])
    sums_ref[0:1, :] += column_sum(qkv_grad[:, :width].astype(f32))
    sums_ref[1:2, :] += column_sum(qkv_grad[:, 2 * width :].astype(f32))


def cross_kernel(
    single, layout, ready, place_ref, x_ref, cot_ref, key_own_ref, key_all_ref, small_ref,
    out_ref, x_grad_ref, grads_ref, sums_ref,
    qkv_ref, qkv_grad_ref, mixed_ref, mixed_grad, slope, act_ref, inner_ref, vec_ref, grad_ref,
):
    own = layout[1]
    load_vec(small_ref, *layout, vec_ref)
    width = x_ref.shape[1]
    count = x_ref.shape[0]
    rows = pl.ds(0, count)

    @pl.when(pl.program_id(0) == 0)
    def _():
        sums_ref[...] = jnp.zeros_like(sums_ref)

    attn_ref = ready(0)
    mask = key_own_ref[...] == key_all_ref[0]
    entry = x_ref[...]
    low_in = entry.astype(bf16)
    qkv = dot_nn(low_in, attn_ref[:, : 3 * width]) + qkv_bias(vec_ref)
    qkv_ref[...] = qkv.astype(bf16)
    heads_forward(qkv_ref, mixed_ref, rows, width, mask)
    first_sum = entry + dot_nn(mixed_ref[...], attn_ref[:, 3 * width :]) + vec_ref[2:3, :]
    unit_one, inverse_one = normalise(first_sum)
    normed = unit_one * vec_ref[3:4, :] + vec_ref[4:5, :]
    low = normed.astype(bf16)
    up_ref = ready(1)
    down_ref = ready(2)
    total = normed + vec_ref[5:6, :]
    for part in range(4):
        cols = pl.ds(part * width, width)
        inner = dot_nn(low, up_ref[:, cols]) + vec_ref[8 + part : 9 + part, :]
        act, rate = gelu_parts(inner)
        act = act.astype(bf16)
        act_ref[:, cols] = act
        slope[:, cols] = rate
        total = total + dot_nt(act, down_ref[:, cols])
    unit_two, inverse_two = normalise(total)
    out_ref[...] = (unit_two * vec_ref[6:7, :] + vec_ref[7:8, :]).astype(bf16)

    if single:
        for part in range(small_ref.shape[0]):
            for at in range(width // 128):
                tile = small_ref[part, at * 8 : (at + 1) * 8, :]
                grad_ref[part * 8 : (part + 1) * 8, at * 128 : (at + 1) * 128] = tile.astype(f32)
        grad = grad_ref[...]
    else:
        grad = cot_ref[...].astype(f32)
    sums_ref[6:7, :] += column_sum(grad * unit_two)
    sums_ref[7:8, :] += column_sum(grad)
    second_grad = norm_back(grad, unit_two, inverse_two, vec_ref[6:7, :])
    branch = second_grad.astype(bf16)
    sums_ref[5:6, :] += column_sum(branch.astype(f32))
    total = second_grad
    for part in range(4):
        cols = pl.ds(part * width, width)
        inner = (dot_nn(branch, down_ref[:, cols]) * slope[:, cols]).astype(bf16)
        inner_ref[:, cols] = inner
        sums_ref[8 + part : 9 + part, :] += column_sum(inner.astype(f32))
        total = total + dot_nt(inner, up_ref[:, cols])
    sums_ref[3:4, :] += column_sum(total * unit_one)
    sums_ref[4:5, :] += column_sum(total)
    first = norm_back(total, unit_one, inverse_one, vec_ref[3:4, :])
    attn_low = first.astype(bf16)
    sums_ref[2:3, :] += column_sum(attn_low.astype(f32))
    mixed_grad[...] = dot_nt(attn_low, attn_ref[:, 3 * width :]).astype(bf16)
    heads_backward(qkv_ref, mixed_grad, qkv_grad_ref, rows, width, mask)
    qkv_grad = qkv_grad_ref[...]
    x_grad_ref[...] = first + dot_nt(qkv_grad, attn_ref[:, : 3 * width])
    sums_ref[0:1, :] += column_sum(qkv_grad[:, :width].astype(f32))
    sums_ref[1:2, :] += column_sum(qkv_grad[:, 2 * width :].astype(f32))

    begin = (place_ref[0] * 2 + place_ref[1]) * own
    spot = lax.broadcasted_iota(jnp.int32, (width, own), 0) - lax.broadcasted_iota(jnp.int32, (width, own), 1)
    chosen = (spot == begin).astype(f32).astype(bf16)
    start = 0
    for left, right in ((low_in, qkv_grad), (mixed_ref[...], attn_low), (low, inner_ref[...]), (branch, act_ref[...])):
        cols = right.shape[1]
        grad = dot_tn(dot_nn(left, chosen).astype(bf16), right)
        if single:
            grads_ref[:, start : start + cols] = grad.astype(bf16)
        else:

            @pl.when(pl.program_id(0) == 0)
            def _(start=start, cols=cols):
                grads_ref[:, start : start + cols] = jnp.zeros((own, cols), f32)

            grads_ref[:, start : start + cols] += grad
        start += cols
    if single:
        sums = sums_ref[0:12, :]
        sums = jnp.concatenate([sums[:, : width // 2], sums[:, width // 2 :]], 0).astype(bf16)
        grads_ref[:, start:] = jnp.concatenate([sums] * (own // 24), 0)


def row_spec(width, block=BLOCK):
    return pl.BlockSpec((block, width), lambda i: (i, 0))


def whole_spec(shape):
    return pl.BlockSpec(shape, lambda i: (0,) * len(shape), pipeline_mode=pl.Buffered(1))


def fixed_spec(shape):
    return pl.BlockSpec(shape, lambda i: (0,) * len(shape))


def params():
    return pltpu.CompilerParams(dimension_semantics=("arbitrary",), vmem_limit_bytes=VMEM_LIMIT)


def shaped(*dims, dtype=bf16):
    return jax.ShapeDtypeStruct(dims, dtype)


def cost(flops, nbytes, trans=0):
    return pl.CostEstimate(flops=int(flops), bytes_accessed=int(nbytes), transcendentals=int(trans))


def attn_forward(flat, place, attn, small, layout):
    rows, width = flat.shape
    weights = Weights(attn)
    return pl.pallas_call(
        weights.wrap(partial(attn_fwd_kernel, layout)),
        grid=(rows // BLOCK,),
        in_specs=weights.specs() + [row_spec(width), whole_spec(small.shape)],
        out_specs=[row_spec(3 * width), row_spec(width), row_spec(width)],
        out_shape=[shaped(rows, 3 * width), shaped(rows, width), shaped(rows, width, dtype=f32)],
        scratch_shapes=[pltpu.VMEM((16, width), f32)] + weights.scratch(),
        compiler_params=params(),
        cost_estimate=cost(2 * rows * width * (4 * width + 2 * SEG_LEN), rows * width * 14 + width * width * 8),
        name="seg_attn_fwd",
    )(*weights.arrays(place), flat, small)


def ffn_forward(first_sum, place, up_proj, down_proj, small, layout, parts):
    rows, width = first_sum.shape
    inner = up_proj.shape[1]
    weights = Weights(up_proj, down_proj)
    cls_shape = (parts, rows // SEG_LEN, width)
    cls_spec = fixed_spec(cls_shape)
    return pl.pallas_call(
        weights.wrap(partial(ffn_fwd_kernel, layout)),
        grid=(rows // BLOCK,),
        in_specs=weights.specs() + [row_spec(width), whole_spec(small.shape)],
        out_specs=[row_spec(width), row_spec(inner), row_spec(inner), row_spec(width), row_spec(width), cls_spec],
        out_shape=[
            shaped(rows, width), shaped(rows, inner), shaped(rows, inner), shaped(rows, width, dtype=f32),
            shaped(rows, width), shaped(*cls_shape, dtype=f32),
        ],
        scratch_shapes=[pltpu.VMEM((16, width), f32)] + weights.scratch(),
        compiler_params=params(),
        cost_estimate=cost(4 * rows * width * inner, rows * (width * 12 + inner * 4) + width * inner * 4, 2 * rows * inner),
        name="seg_ffn_fwd",
    )(*weights.arrays(place), first_sum, small)


def ffn_backward(cot, cls_grad, second_sum, first_sum, slope, place, up_proj, down_proj, small, layout):
    rows, width = first_sum.shape
    inner = up_proj.shape[1]
    weights = Weights(up_proj, down_proj)
    cls_spec = whole_spec(cls_grad.shape)
    return pl.pallas_call(
        weights.wrap(partial(ffn_bwd_kernel, layout), with_place=True),
        grid=(rows // BLOCK,),
        in_specs=weights.specs() + [
            row_spec(width), cls_spec, row_spec(width), row_spec(width), row_spec(inner), whole_spec(small.shape),
        ],
        out_specs=[row_spec(width), row_spec(inner), row_spec(width), row_spec(width), fixed_spec((16, width))],
        out_shape=[
            shaped(rows, width), shaped(rows, inner), shaped(rows, width, dtype=f32), shaped(rows, width),
            shaped(16, width, dtype=f32),
        ],
        scratch_shapes=[pltpu.VMEM((16, width), f32)] + weights.scratch(),
        compiler_params=params(),
        cost_estimate=cost(4 * rows * width * inner, rows * (width * 16 + inner * 4) + width * inner * 4),
        name="seg_ffn_bwd",
    )(*weights.arrays(place), cot, cls_grad, second_sum, first_sum, slope, small)


def attn_backward(first_grad, attn_low, qkv, place, attn, share, shares, before=()):
    rows, width = first_grad.shape
    weights = Weights(attn)
    steps = rows // BLOCK // shares
    spec = lambda cols: pl.BlockSpec((BLOCK, cols), lambda i: (i + share * steps, 0))
    kept = len(before)
    args = weights.arrays(place) + [first_grad, attn_low, qkv]

    def body(ready, *refs):
        attn_bwd_kernel(ready, *refs[:3], *refs[3 + kept :])

    return pl.pallas_call(
        weights.wrap(body),
        grid=(steps,),
        in_specs=weights.specs() + [spec(width), spec(width), spec(3 * width)] + [pl.BlockSpec(memory_space=pl.ANY)] * kept,
        out_specs=[spec(3 * width), spec(width), fixed_spec((8, width))],
        out_shape=[shaped(rows, 3 * width), shaped(rows, width, dtype=f32), shaped(8, width, dtype=f32)],
        input_output_aliases={len(args) + at: at for at in range(kept)},
        scratch_shapes=[pltpu.VMEM((BLOCK, width), bf16)] + weights.scratch(),
        compiler_params=params(),
        cost_estimate=cost(
            2 * rows * width * (4 * width + 5 * SEG_LEN) // shares, rows * width * 22 // shares + width * width * 8
        ),
        name="seg_attn_bwd",
    )(*args, *before)


def cross_layer(entry, cot, row_key, blocks, place, attn, up_proj, down_proj, small, layout):
    rows, width = entry.shape
    inner = up_proj.shape[1]
    block = rows // blocks
    spec = partial(row_spec, block=block)
    weights = Weights(attn, up_proj, down_proj)
    own = layout[1]
    both = jnp.tile(row_key.reshape(blocks, 1, block), (1, 1, 2))
    wide = (own, 3 * inner + (width // 2 if by_links() else 0))
    return pl.pallas_call(
        weights.wrap(partial(cross_kernel, by_links(), layout), with_place=True),
        grid=(blocks,),
        in_specs=weights.specs() + [
            spec(width), spec(width), spec(1), pl.BlockSpec((1, 1, 2 * block), lambda i: (i, 0, 0)), whole_spec(small.shape),
        ],
        out_specs=[spec(width), spec(width), fixed_spec(wide), fixed_spec((16, width))],
        out_shape=[
            shaped(rows, width), shaped(rows, width, dtype=f32), shaped(*wide, dtype=bf16 if by_links() else f32),
            shaped(16, width, dtype=f32),
        ],
        scratch_shapes=[
            pltpu.VMEM((block, 3 * width), bf16), pltpu.VMEM((block, 3 * width), bf16), pltpu.VMEM((block, width), bf16),
            pltpu.VMEM((block, width), bf16), pltpu.VMEM((block, inner), f32), pltpu.VMEM((block, inner), bf16),
            pltpu.VMEM((block, inner), bf16), pltpu.VMEM((16, width), f32), pltpu.VMEM((block, width), f32),
        ] + weights.scratch(),
        compiler_params=params(),
        cost_estimate=cost(24 * rows * width * 4 * width, rows * width * 40 + width * inner * 6),
        name="cross_layer",
    )(*weights.arrays(place), entry, cot, row_key.reshape(rows, 1), both, small)


def hop_seg(value, hops):
    size = lax.axis_size("seg")
    return lax.ppermute(value, "seg", [(at, (at + 2 * hops) % size) for at in range(size)])


def swap_core(value):
    return lax.ppermute(value, "seg", [(at, at ^ 1) for at in range(lax.axis_size("seg"))])


def swap_batch(value, flip):
    return lax.ppermute(value, "batch", [(at, at ^ flip) for at in range(lax.axis_size("batch"))])


def fence(*values):
    return lax.optimization_barrier(values)


def by_links():
    return lax.axis_size("batch") == 4 and lax.axis_size("seg") == 8


class Gather:
    def __init__(self, *shards):
        self.many = len(shards)
        self.own, self.cols = shards[0].shape
        self.quarter = self.cols // 4
        self.mine = jnp.concatenate(shards, 0) if self.many > 1 else shards[0]
        self.part = lax.dynamic_slice_in_dim(self.mine, lax.axis_index("batch") * self.quarter, self.quarter, 1)

    def run_seg(self):
        self.raw = [hop_seg(self.part, hops) for hops in (3, 2, 1)]

    def sort_wide(self, full):
        first = lax.axis_index("seg") // 2 + 1
        self.along = lax.dynamic_slice_in_dim(jnp.concatenate([full, full[:3]], 0), first, 3)

    def run_own(self):
        self.mine_too = swap_core(self.mine)

    def sort_seg(self):
        self.along = jnp.stack(self.raw)

    def run_near(self):
        self.near = [swap_batch(self.along, flip) for flip in (1, 2)]

    def run_far(self):
        half = self.mine.shape[0] // 2
        self.far = [swap_batch(self.near[1][:, :half], 1), swap_batch(self.near[0][:, half:], 2)]

    def run_core_along(self):
        self.along_too = swap_core(self.along)

    def run_core_near(self, joined):
        self.joined = joined
        if joined:
            self.near = [jnp.stack([self.along] + self.near)]
            self.near_too = [swap_core(array) for array in self.near]
        else:
            self.near_too = [self.along_too] + [swap_core(array) for array in self.near]
            self.near = [self.along] + self.near

    def run_core_far(self):
        self.far_too = [swap_core(array) for array in self.far]

    def pieces(self):
        own, cols, quarter = self.own, self.cols, self.quarter
        half = self.mine.shape[0] // 2
        arrays = [self.mine] + self.near + self.far + [self.mine_too] + self.near_too + self.far_too
        many = len(self.near)
        matrices = []
        for at in range(self.many):
            first, last = at * own, (at + 1) * own
            blocks = []
            for core in (0, 1):

                def chip(later, core=core):
                    return lambda z, c: (((z + 1 + later) & 3) * 2 + (c ^ core)) * own

                target = lambda z, c, q, core=core: ((z * 2 + (c ^ core)) * own, 0)
                blocks.append(((many + 3) * core, (slice(first, last), slice(None)), (own, cols), target))
                for later in range(3):
                    row = chip(later)
                    for flip in range(3):
                        target = lambda z, c, q, row=row, flip=flip: (row(z, c), (q ^ flip) * quarter)
                        source = (later, slice(first, last), slice(None))
                        where = (many + 3) * core + 1
                        source, where = ((flip,) + source, where) if self.joined else (source, where + flip)
                        blocks.append((where, source, (own, quarter), target))
                    for side in (0, 1):
                        lo, hi = max(first, side * half), min(last, (side + 1) * half)
                        if lo >= hi:
                            continue
                        target = lambda z, c, q, row=row, skip=lo - first: (row(z, c) + skip, (q ^ 3) * quarter)
                        source = (later, slice(lo - side * half, hi - side * half), slice(None))
                        blocks.append(((many + 3) * core + many + 1 + side, source, (hi - lo, quarter), target))
            matrices.append(Pieces((own * lax.axis_size("seg"), cols), arrays, blocks))
        return matrices


def gather_plain(shard):
    full = lax.all_gather(shard, "seg", axis=0, tiled=True)
    block = (0, (slice(None), slice(None)), full.shape, lambda z, c, q: (0, 0))
    return Pieces(full.shape, [full], [block])


def chips_exchange(value):
    return lax.all_to_all(value, "seg", 0, 0, axis_index_groups=CHIP_GROUPS, tiled=True)


def gather_seg(value):
    if not by_links():
        return lax.all_gather(value, "seg", axis=0, tiled=False)
    copies = jnp.broadcast_to(value, (lax.axis_size("seg"),) + value.shape)
    return lax.all_to_all(copies, "seg", 0, 0, tiled=True)


def plain_grad_kernel(steps, *refs):
    pairs, (out_ref,) = refs[: 2 * len(steps)], refs[2 * len(steps) :]
    begin = 0
    for at, many in enumerate(steps):

        @pl.when((pl.program_id(0) >= begin) & (pl.program_id(0) < begin + many))
        def _(at=at):
            out_ref[...] = dot_tn(pairs[2 * at][...], pairs[2 * at + 1][...]).astype(bf16)

        begin += many


def plain_grads(*pairs):
    rows, width = pairs[0][0].shape
    steps = tuple(right.shape[1] // width for _, right in pairs)
    in_specs = []
    begin = 0
    for many in steps:
        in_specs.append(whole_spec((rows, width)))
        in_specs.append(pl.BlockSpec((rows, width), lambda i, begin=begin, many=many: (0, jnp.clip(i - begin, 0, many - 1))))
        begin += many
    return pl.pallas_call(
        partial(plain_grad_kernel, steps),
        grid=(begin,),
        in_specs=in_specs,
        out_specs=pl.BlockSpec((width, width), lambda i: (0, i)),
        out_shape=shaped(width, begin * width),
        compiler_params=params(),
        cost_estimate=cost(2 * rows * width * width * begin, 2 * (rows + width) * width * begin),
        name="plain_weight_grads",
    )(*[array for pair in pairs for array in pair])


def weight_grad_kernel(steps, place_ref, *refs):
    pairs, (keep_ref, send_ref, acc_ref) = refs[: 2 * len(steps)], refs[2 * len(steps) :]
    step = pl.program_id(0)
    begin = 0
    for at, many in enumerate(steps):

        @pl.when((step >= begin) & (step < begin + many))
        def _(at=at):
            acc_ref[...] = dot_tn(pairs[2 * at][...], pairs[2 * at + 1][...])

        begin += many
    c, q = place_ref[1], place_ref[2]
    size = keep_ref.shape[2]
    for flip in range(4):
        for chip in range(4):
            for core, out_ref in ((0, keep_ref), (1, send_ref)):
                row = (chip * 2 + (c ^ core)) * (4 * size) + (q ^ flip) * size
                rows = pl.ds(pl.multiple_of(row, size), size)
                out_ref[flip, chip] = acc_ref[rows, :].astype(bf16)


def weight_grads(place, *pairs):
    rows, width = pairs[0][0].shape
    steps = tuple(right.shape[1] // width for _, right in pairs)
    size = width // 32
    in_specs = [pl.BlockSpec(memory_space=pltpu.SMEM)]
    begin = 0
    for many in steps:
        in_specs.append(whole_spec((rows, width)))
        in_specs.append(pl.BlockSpec((rows, width), lambda i, begin=begin, many=many: (0, jnp.clip(i - begin, 0, many - 1))))
        begin += many
    out_spec = pl.BlockSpec((4, 4, size, width), lambda i: (0, 0, 0, i))
    out = shaped(4, 4, size, begin * width)
    return pl.pallas_call(
        partial(weight_grad_kernel, steps),
        grid=(begin,),
        in_specs=in_specs,
        out_specs=[out_spec, out_spec],
        out_shape=[out, out],
        scratch_shapes=[pltpu.VMEM((width, width), f32)],
        compiler_params=params(),
        cost_estimate=cost(2 * rows * width * width * begin, 2 * (rows + width) * width * begin),
        name="weight_grads",
    )(place, *[array for pair in pairs for array in pair])


def wide_sum(first, *others):
    total = first.astype(f32)
    for other in others:
        total = total + other.astype(f32)
    return total


def batch_spread(value):
    value = value.astype(bf16)
    return [value] + [swap_batch(value, flip) for flip in (1, 2, 3)]


def core_sums(keep, got):
    sums = [wide_sum(keep[flip], got[flip]) for flip in range(4)]
    return sums[0], [part.astype(bf16) for part in sums[1:]]


def batch_swaps(parts):
    return [swap_batch(part, flip) for flip, part in zip((1, 2, 3), parts)]


def place_kernel(plan, place_ref, *refs):
    count = 4 * len(plan)
    blocks, outs = refs[:count], refs[count:]
    q = place_ref[2]
    for at, targets in enumerate(plan):
        for flip in range(4):
            block = blocks[4 * at + flip]
            size = block.shape[0]
            rows = pl.ds(pl.multiple_of((q ^ flip) * size, size), size)
            for source, index, target, cols in targets:
                outs[index][rows, target : target + cols] = block[:, source : source + cols].astype(f32)


def place_outputs(place, plan, groups, own, shape):
    vmem = pl.BlockSpec(memory_space=pltpu.VMEM)
    return pl.pallas_call(
        partial(place_kernel, plan),
        in_specs=[pl.BlockSpec(memory_space=pltpu.SMEM)] + [vmem] * (4 * len(groups)),
        out_specs=[vmem] * own,
        out_shape=[jax.ShapeDtypeStruct(shape, f32)] * own,
        compiler_params=pltpu.CompilerParams(vmem_limit_bytes=VMEM_LIMIT),
        cost_estimate=cost(0, own * shape[0] * shape[1] * 6),
        name="place_outputs",
    )(place, *[block for group in groups for block in group])


def scatter_sum(matrix):
    return lax.psum_scatter(matrix.astype(bf16), "seg", scatter_dimension=0, tiled=True)


def local(
    hidden, seg_doc, seg_attn, seg_up, seg_down, seg_vec,
    cross_attn, cross_up, cross_down, cross_vec, tok_cot, cls_cot,
):
    micro, _, segments, _, length, width = hidden.shape
    own, cols = seg_attn.shape
    parts = lax.axis_size("seg")
    place = lax.axis_index("seg")
    count = micro * segments
    total = parts * count
    spot = jnp.stack([place // 2, place % 2, lax.axis_index("batch")]).astype(jnp.int32)

    flat = hidden.reshape(count * length, width)
    tiles = width // 128
    vecs = jnp.pad(jnp.concatenate([seg_vec.T, cross_vec.T], 0), ((0, 0), (0, 128 - own)))
    small = cls_cot.reshape(count, tiles, 128).transpose(1, 0, 2).reshape(count * tiles, 128)
    small = jnp.concatenate([small, vecs], 0)
    seg_layout, cross_layout = (count * tiles, own), (count * tiles + 12, own)

    docs = seg_doc[:, 0].reshape(micro, segments, parts) + (1 << 16) * jnp.arange(micro, dtype=jnp.int32)[:, None, None]
    docs = docs.transpose(2, 0, 1)
    blocks = micro if total > 256 else 1
    if blocks > 1:
        order = lambda rows: rows.reshape(parts, micro, segments, -1).transpose(1, 0, 2, 3).reshape(total, -1)
        back = lambda rows: rows.reshape(micro, parts, segments, -1).transpose(1, 0, 2, 3).reshape(total, -1)
        row_key = docs.transpose(1, 0, 2).reshape(total)
    else:
        order = back = lambda rows: rows
        row_key = docs.reshape(total)
    if by_links():
        one, two, three = Gather(seg_attn), Gather(seg_up, seg_down), Gather(cross_up, cross_down)
        one.run_seg()
        small = gather_seg(small)
        one.run_own()
        one.raw, small, two.part, two.mine = fence(one.raw, small, two.part, two.mine)
        one.sort_seg()
        one.run_near()
        two.run_seg()
        (one.near,) = fence(one.near)
        one.run_far()
        wide = jnp.broadcast_to(three.part, (4,) + three.part.shape)
        one.far, one.near, two.raw, wide, two.mine, three.mine, row_key = fence(
            one.far, one.near, two.raw, wide, two.mine, three.mine, row_key
        )
        two.sort_seg()
        two.run_near()
        two.run_core_along()
        full = chips_exchange(wide)
        one.run_core_near(True)
        one.run_core_far()
        (attn_full,) = one.pieces()
        outs = attn_forward(flat, spot, attn_full, small, seg_layout)
        two.run_own()
        three.run_own()
        (qkv, mixed, first_sum), two.near, two.along_too, full, cross_attn, two.mine_too, three.mine_too = fence(
            outs, two.near, two.along_too, full, cross_attn, two.mine_too, three.mine_too
        )
        cross_attn_full = gather_plain(cross_attn)
        two.run_far()
        two.run_core_near(False)
        (two.far, full) = fence(two.far, full)
        three.sort_wide(full)
        three.run_near()
        two.run_core_far()
        three.run_core_along()
        up_full, down_full = two.pieces()
        outs = ffn_forward(first_sum, spot, up_full, down_full, small, seg_layout, parts)
        (normed, act, slope, second_sum, tok, cls), three.near, three.along_too = fence(outs, three.near, three.along_too)
        three.run_far()
        entry = lax.all_to_all(cls, "seg", 0, 0, tiled=True).reshape(total, width)
        cot_all = entry
        three.run_core_near(False)
        entry, three.far = fence(entry, three.far)
        three.run_core_far()
        cross_up_full, cross_down_full = three.pieces()
    else:
        attn_full, up_full, down_full = [gather_plain(shard) for shard in (seg_attn, seg_up, seg_down)]
        cross_attn_full, cross_up_full, cross_down_full = [
            gather_plain(shard) for shard in (cross_attn, cross_up, cross_down)
        ]
        small = gather_seg(small)
        cot_all = small[:, : count * tiles].reshape(parts, tiles, count, 128).transpose(0, 2, 1, 3).reshape(total, width)
        qkv, mixed, first_sum = attn_forward(flat, spot, attn_full, small, seg_layout)
        normed, act, slope, second_sum, tok, cls = ffn_forward(first_sum, spot, up_full, down_full, small, seg_layout, parts)
        entry = gather_seg(cls[0]).reshape(total, width)

    cls_out, cls_grad, x_grads, x_sums = cross_layer(
        order(entry), order(cot_all), row_key, blocks, spot,
        cross_attn_full, cross_up_full, cross_down_full, small, cross_layout,
    )
    own_cols = lambda rows: lax.dynamic_slice_in_dim(rows, place * own, own, 1)
    own_rows = lambda rows: lax.dynamic_slice_in_dim(back(rows), place * count, count, 0)
    cls_out = own_rows(cls_out)
    if not by_links():
        cls_grad = own_rows(cls_grad)
    outs = ffn_backward(
        tok_cot.reshape(count * length, width),
        cls_grad, second_sum, first_sum, slope, spot, up_full, down_full, small, seg_layout,
    )

    if by_links():
        folded = lambda rows: jnp.concatenate([rows[:, : width // 2], rows[:, width // 2 :]], 0)
        unfolded = lambda rows: jnp.concatenate([rows[:12], rows[12:]], 1)
        x_came = lax.all_to_all(x_grads.reshape(4, own // 4, 3 * cols + width // 2), "batch", 0, 0, tiled=True)
        (branch, inner, first_grad, attn_low, ffn_sums), x_came = fence(outs, x_came)
        x_sum = jnp.sum(x_came.astype(f32), 0)
        cross_sums = unfolded(x_sum[:, 3 * cols :])
        x_low = x_sum[:, : 3 * cols].astype(bf16)
        x_low, branch = fence(x_low, branch)
        x_low, inner = fence(x_low, inner)
        x_near = [swap_batch(x_low, flip) for flip in (1, 2)]
        keep_up, send = weight_grads(spot, (normed, inner))
        keep_up, send, act, x_near, x_low = fence(keep_up, send, act, x_near, x_low)
        got_up = swap_core(send)
        x_far = swap_batch(x_low, 3)
        down_grad = plain_grads((branch, act), (mixed, attn_low))
        down_grad, got_up, x_far, attn_low = fence(down_grad, got_up, x_far, attn_low)
        down_part = lax.psum_scatter(down_grad, "seg", scatter_dimension=0, tiled=True)
        set_cross = [x_low] + x_near + [x_far]
        stay_up, leave = core_sums(keep_up, got_up)
        leave, attn_low = fence(leave, attn_low)
        near_up = [swap_batch(leave[0], 1), swap_batch(leave[1], 2)]
        outs = attn_backward(first_grad, attn_low, qkv, spot, attn_full, 0, 1)
        (qkv_grad, hidden_grad, attn_sums), near_up, last = fence(outs, near_up, leave[2])
        far_up = swap_batch(last, 3)
        sums = folded(jnp.concatenate([attn_sums[:2], ffn_sums[2:12]], 0))
        sums_too = swap_core(sums)
        keep, send = weight_grads(spot, (flat, qkv_grad))
        keep, send, sums, sums_too, far_up = fence(keep, send, sums, sums_too, far_up)
        got = swap_core(send)
        total_up = wide_sum(stay_up, *near_up, far_up).astype(bf16)
        raw_up = chips_exchange(total_up)
        sums = jnp.broadcast_to(sums + sums_too, (4, 24, width // 2))
        stay, leave = core_sums(keep, got)
        stay = jnp.concatenate([stay, sums], 2)
        leave = [jnp.concatenate([part, sums.astype(bf16)], 2) for part in leave]
        came = [swap_batch(part, flip) for flip, part in zip((1, 2, 3), leave)]
        shape = (own, cols)
        x_plan = (((0, 0, 0, cols), (cols, 1, 0, cols), (2 * cols, 2, 0, cols)),)
        x_placed = place_outputs(spot, x_plan, (set_cross,), 3, shape)
        came, raw_up, down_part, x_placed = fence(came, raw_up, down_part, x_placed)
        total_qkv = wide_sum(stay, *came).astype(bf16)
        raw = chips_exchange(total_qkv)
        batch_place = lax.axis_index("batch")
        shares = [lax.dynamic_slice_in_dim(down_part, (batch_place ^ flip) * (own // 4), own // 4, 0) for flip in range(4)]
        down_came = [swap_batch(shares[flip], flip) for flip in (1, 2, 3)]
        up_low = jnp.sum(raw_up.astype(f32), 0).astype(bf16)
        set_up = batch_spread(up_low)
        set_down = batch_spread(wide_sum(shares[0], *down_came))
        raw, set_down, set_up = fence(raw, set_down, set_up)
        last = jnp.sum(raw.astype(f32), 0)
        seg_sums = unfolded(last[:, 3 * width :])
        set_qkv = batch_spread(last[:, : 3 * width])
        (down_placed,) = place_outputs(spot, (((0, 0, 0, cols),),), (set_down,), 1, shape)
        (up_placed,) = place_outputs(spot, (((0, 0, 0, cols),),), (set_up,), 1, shape)
        attn_plan = (((0, 0, 0, 3 * width),), ((cols, 0, 3 * width, width),))
        (attn_placed,) = place_outputs(spot, attn_plan, (set_qkv, set_down), 1, shape)
        grads = [attn_placed, up_placed, down_placed] + list(x_placed)
    else:
        branch, inner, first_grad, attn_low, ffn_sums = outs
        qkv_grad, hidden_grad, attn_sums = attn_backward(first_grad, attn_low, qkv, spot, attn_full, 0, 1)
        x_grads = x_grads.astype(bf16)
        grads = [
            scatter_sum(jnp.concatenate([dot_tn(flat, qkv_grad), dot_tn(mixed, attn_low)], 1)),
            scatter_sum(dot_tn(normed, inner)), scatter_sum(dot_tn(branch, act)),
            x_grads[:, :cols], x_grads[:, cols : 2 * cols], x_grads[:, 2 * cols :],
        ]
        grads = [grad.astype(f32) for grad in lax.psum(tuple(grads), "batch")]
        seg_sums = lax.psum(jnp.concatenate([attn_sums[:2], ffn_sums[2:12]], 0), ("batch", "seg"))
        cross_sums = lax.psum(x_sums[:12], "batch")
    seg_vec_grad = own_cols(seg_sums).T
    cross_vec_grad = own_cols(cross_sums).T
    return (
        tok.reshape(hidden.shape), cls_out.reshape(cls_cot.shape), hidden_grad.reshape(hidden.shape),
        grads[0], grads[1], grads[2], seg_vec_grad, grads[3], grads[4], grads[5], cross_vec_grad,
    )


def solution(mesh):
    wide = P(None, "batch", None, "seg", None, None)
    rows = P("seg", None)
    cls = P(None, "batch", None, "seg", None)
    in_specs = (wide, P(None, "batch", None)) + (rows,) * 8 + (wide, cls)
    out_specs = (wide, cls, wide) + (rows,) * 8
    return jax.shard_map(local, mesh=mesh, in_specs=in_specs, out_specs=out_specs, check_vma=False)
```

```python
from functools import partial

import jax
import jax.numpy as jnp
from jax import lax
from jax.experimental import pallas as pl
from jax.experimental.pallas import tpu as pltpu
from jax.sharding import PartitionSpec as P

HEADS = 12
HEAD_DIM = 64
SEG_LEN = 128
PAIRS = HEADS // 2
PAIR = 2 * HEAD_DIM
GROUP = 6

NEG_FILL = -1e30
LN_EPS = 1e-05
SCALE = HEAD_DIM ** (-0.5)
ROOT_HALF = 0.7071067811865476
PDF_AT_ZERO = 0.3989422804014327
BLOCK = 256
CHIP_GROUPS = [[0, 2, 4, 6], [1, 3, 5, 7]]
VMEM_LIMIT = 60 * 1024 * 1024

f32 = jnp.float32
bf16 = jnp.bfloat16


def dot_nn(left, right):
    return lax.dot_general(left, right, (((1,), (0,)), ((), ())), preferred_element_type=f32)


def dot_nt(left, right):
    return lax.dot_general(left, right, (((1,), (1,)), ((), ())), preferred_element_type=f32)


def dot_tn(left, right):
    return lax.dot_general(left, right, (((0,), (0,)), ((), ())), preferred_element_type=f32)


def normalise(rows):
    centred = rows - jnp.mean(rows, -1, keepdims=True)
    spread = jnp.mean(centred * centred, -1, keepdims=True)
    inverse = lax.rsqrt(spread + LN_EPS)
    return centred * inverse, inverse


def norm_back(grad, unit, inverse, gain):
    scaled = grad * gain
    return inverse * (
        scaled
        - jnp.mean(scaled, -1, keepdims=True)
        - unit * jnp.mean(scaled * unit, -1, keepdims=True)
    )


def column_sum(rows):
    return jnp.sum(rows, 0, keepdims=True)


def gelu_parts(value):
    cdf = 0.5 * (1.0 + lax.erf(value * ROOT_HALF))
    pdf = PDF_AT_ZERO * jnp.exp(-0.5 * value * value)
    return value * cdf, cdf + value * pdf


def first_half(rows):
    return lax.broadcasted_iota(jnp.int32, (rows, PAIR), 1) < HEAD_DIM


def split_heads(rows, first):
    zero = jnp.zeros_like(rows)
    return jnp.concatenate([jnp.where(first, rows, zero), jnp.where(first, zero, rows)], 0)


def join_heads(stacked, first):
    rows = stacked.shape[0] // 2
    return jnp.where(first, stacked[:rows], stacked[rows:])


def pair_probs(query, keys, mask):
    scores = dot_nt(keys, query) * SCALE
    if mask is not None:
        scores = jnp.where(mask, scores, NEG_FILL)
    top = jnp.max(scores, 0, keepdims=True)
    expo = jnp.exp(scores - top)
    return expo * (1.0 / jnp.sum(expo, 0, keepdims=True))


def pair_parts(qkv_ref, rows, pair, width, first):
    at = pair * PAIR
    query = split_heads(qkv_ref[rows, at : at + PAIR], first)
    return query, qkv_ref[rows, width + at : width + at + PAIR], qkv_ref[rows, 2 * width + at : 2 * width + at + PAIR]


def heads_forward(qkv_ref, out_ref, spans, width, mask):
    first = first_half(spans[0].size)
    every = [(rows, pair) for rows in spans for pair in range(PAIRS)]
    parts = [pair_parts(qkv_ref, rows, pair, width, first) for rows, pair in every]
    probs = [pair_probs(query, keys, mask).astype(bf16) for query, keys, _ in parts]
    mixed = [join_heads(dot_tn(prob, values), first) for prob, (_, _, values) in zip(probs, parts)]
    for (rows, pair), value in zip(every, mixed):
        out_ref[rows, pair * PAIR : (pair + 1) * PAIR] = value.astype(bf16)


def heads_backward(qkv_ref, grad_ref, out_ref, rows, width, mask):
    first = first_half(rows.size)
    for start in range(0, PAIRS, GROUP):
        pairs = range(start, start + GROUP)
        parts = [pair_parts(qkv_ref, rows, pair, width, first) for pair in pairs]
        grads = [split_heads(grad_ref[rows, pair * PAIR : (pair + 1) * PAIR], first) for pair in pairs]
        probs = [pair_probs(query, keys, mask) for query, keys, _ in parts]
        prob_grads = [dot_nt(values, grad) for (_, _, values), grad in zip(parts, grads)]
        value_grads = [dot_nn(prob.astype(bf16), grad) for prob, grad in zip(probs, grads)]
        score_grads = [
            (prob * (grad - jnp.sum(grad * prob, 0, keepdims=True))).astype(bf16) for prob, grad in zip(probs, prob_grads)
        ]
        key_grads = [dot_nn(grad, query) * SCALE for grad, (query, _, _) in zip(score_grads, parts)]
        query_grads = [join_heads(dot_tn(grad, keys), first) * SCALE for grad, (_, keys, _) in zip(score_grads, parts)]
        for at, values in ((0, query_grads), (width, key_grads), (2 * width, value_grads)):
            for pair, value in zip(pairs, values):
                out_ref[rows, at + pair * PAIR : at + (pair + 1) * PAIR] = value.astype(bf16)


class Pieces:
    def __init__(self, shape, arrays, blocks):
        self.shape, self.arrays, self.blocks = shape, arrays, blocks

    def specs(self):
        return [pl.BlockSpec(memory_space=pl.ANY)] * len(self.arrays)

    def scratch(self):
        return [pltpu.VMEM(self.shape, bf16), pltpu.SemaphoreType.DMA((len(self.blocks),))]

    def copies(self, refs, place_ref, full_ref, sems):
        out = []
        for at, (index, source, size, target) in enumerate(self.blocks):
            row, col = target(place_ref[0], place_ref[1], place_ref[2])
            if not isinstance(row, int):
                row = pl.multiple_of(row, size[0])
            if not isinstance(col, int):
                col = pl.multiple_of(col, size[1])
            view = full_ref.at[pl.ds(row, size[0]), pl.ds(col, size[1])]
            out.append(pltpu.make_async_copy(refs[index].at[source], view, sems.at[at]))
        return out


class Weights:
    def __init__(self, *matrices):
        self.matrices = matrices

    def arrays(self, place):
        return [place] + [array for matrix in self.matrices for array in matrix.arrays]

    def specs(self):
        return [pl.BlockSpec(memory_space=pltpu.SMEM)] + [spec for matrix in self.matrices for spec in matrix.specs()]

    def scratch(self):
        return [item for matrix in self.matrices for item in matrix.scratch()]

    def wrap(self, body, with_place=False, split=None):
        many = sum(len(matrix.arrays) for matrix in self.matrices)

        def kernel(place_ref, *refs):
            given, rest = refs[:many], refs[many:]
            cut = len(rest) - 2 * len(self.matrices)
            rest, own = rest[:cut], rest[cut:]
            first = pl.program_id(0) == 0
            views, copies = [], []
            for at, matrix in enumerate(self.matrices):
                views.append(own[2 * at])
                copies.append(partial(matrix.copies, given[: len(matrix.arrays)], place_ref, own[2 * at], own[2 * at + 1]))
                given = given[len(matrix.arrays) :]

            def start():
                for group in copies:
                    for copy in group():
                        copy.start()

            def wait(at):
                for copy in copies[at]():
                    copy.wait()
                return views[at]

            def ready(at):
                pl.when(first)(lambda: (wait(at), None)[1])
                return views[at]

            call = lambda how: body(how, *([place_ref] if with_place else []), *rest)
            if split is None:
                pl.when(first)(start)
                call(ready)
            elif not split:
                start()
                call(wait)
            else:

                @pl.when(first)
                def _():
                    start()
                    call(wait)

                @pl.when(jnp.logical_not(first))
                def _():
                    call(lambda at: views[at])

        return kernel


def load_vec(small_ref, skip, own, vec_ref):
    @pl.when(pl.program_id(0) == 0)
    def _():
        for part in range(small_ref.shape[0]):
            vec_ref[0:12, part * own : (part + 1) * own] = small_ref[part, skip : skip + 12, :own].astype(f32)


def qkv_bias(vec_ref):
    query = vec_ref[0:1, :]
    return jnp.concatenate([query, jnp.zeros_like(query), vec_ref[1:2, :]], 1)


def attn_fwd_kernel(layout, ready, x_ref, small_ref, qkv_ref, mixed_ref, sum_ref, vec_ref):
    width = x_ref.shape[1]
    load_vec(small_ref, *layout, vec_ref)
    w_ref = ready(0)
    rows = x_ref[...]
    qkv = dot_nn(rows, w_ref[:, : 3 * width]) + qkv_bias(vec_ref)
    qkv_ref[...] = qkv.astype(bf16)
    spans = [pl.ds(start, SEG_LEN) for start in range(0, x_ref.shape[0], SEG_LEN)]
    heads_forward(qkv_ref, mixed_ref, spans, width, None)
    branch = dot_nn(mixed_ref[...], w_ref[:, 3 * width :])
    sum_ref[...] = rows.astype(f32) + branch + vec_ref[2:3, :]


def ffn_fwd_kernel(layout, ready, sum_ref, small_ref, norm_ref, act_ref, slope_ref, second_ref, tok_ref, cls_ref, vec_ref):
    width = sum_ref.shape[1]
    load_vec(small_ref, *layout, vec_ref)
    up_ref = ready(0)
    down_ref = ready(1)
    unit, _ = normalise(sum_ref[...])
    normed = unit * vec_ref[3:4, :] + vec_ref[4:5, :]
    low = normed.astype(bf16)
    norm_ref[...] = low
    total = normed + vec_ref[5:6, :]
    ahead = dot_nn(low, up_ref[:, :width])
    for part in range(4):
        cols = pl.ds(part * width, width)
        inner = ahead + vec_ref[8 + part : 9 + part, :]
        if part < 3:
            ahead = dot_nn(low, up_ref[:, (part + 1) * width : (part + 2) * width])
        act, slope = gelu_parts(inner)
        act = act.astype(bf16)
        act_ref[:, cols] = act
        slope_ref[:, cols] = slope.astype(bf16)
        total = total + dot_nt(act, down_ref[:, cols])
    second_ref[...] = total
    unit, _ = normalise(total)
    result = unit * vec_ref[6:7, :] + vec_ref[7:8, :]
    tok_ref[...] = result.astype(bf16)
    per = sum_ref.shape[0] // SEG_LEN
    for index in range(per):
        row = jnp.broadcast_to(result[index * SEG_LEN : index * SEG_LEN + 1, :][None], (cls_ref.shape[0], 1, width))
        cls_ref[:, pl.ds(pl.program_id(0) * per + index, 1), :] = row


def ffn_bwd_kernel(
    layout, ready, place_ref, cot_ref, cls_ref, second_ref, sum_ref, slope_ref, small_ref,
    branch_ref, inner_ref, first_ref, low_ref, sums_ref, vec_ref,
):
    width = sum_ref.shape[1]
    load_vec(small_ref, *layout, vec_ref)
    per = sum_ref.shape[0] // SEG_LEN
    begin = pl.program_id(0) * per
    if cls_ref.shape[0] > per * pl.num_programs(0):
        begin = begin + (place_ref[0] * 2 + place_ref[1]) * (per * pl.num_programs(0))

    @pl.when(pl.program_id(0) == 0)
    def _():
        sums_ref[...] = jnp.zeros_like(sums_ref)

    place = lax.broadcasted_iota(jnp.int32, (SEG_LEN, 1), 0) == 0
    parts = []
    for index in range(sum_ref.shape[0] // SEG_LEN):
        rows = cot_ref[index * SEG_LEN : (index + 1) * SEG_LEN, :].astype(f32)
        parts.append(rows + jnp.where(place, cls_ref[pl.ds(begin + index, 1), :], 0.0))
    grad = jnp.concatenate(parts, 0)
    unit, inverse = normalise(second_ref[...])
    sums_ref[6:7, :] += column_sum(grad * unit)
    sums_ref[7:8, :] += column_sum(grad)
    second_grad = norm_back(grad, unit, inverse, vec_ref[6:7, :])
    branch = second_grad.astype(bf16)
    branch_ref[...] = branch
    sums_ref[5:6, :] += column_sum(branch.astype(f32))
    up_ref = ready(0)
    down_ref = ready(1)
    total = second_grad
    ahead = dot_nn(branch, down_ref[:, :width])
    for part in range(4):
        cols = pl.ds(part * width, width)
        act_grad = ahead
        if part < 3:
            ahead = dot_nn(branch, down_ref[:, (part + 1) * width : (part + 2) * width])
        inner = (act_grad * slope_ref[:, cols].astype(f32)).astype(bf16)
        inner_ref[:, cols] = inner
        sums_ref[8 + part : 9 + part, :] += column_sum(inner.astype(f32))
        total = total + dot_nt(inner, up_ref[:, cols])
    unit, inverse = normalise(sum_ref[...])
    sums_ref[3:4, :] += column_sum(total * unit)
    sums_ref[4:5, :] += column_sum(total)
    first = norm_back(total, unit, inverse, vec_ref[3:4, :])
    first_ref[...] = first
    low = first.astype(bf16)
    low_ref[...] = low
    sums_ref[2:3, :] += column_sum(low.astype(f32))


def attn_bwd_kernel(ready, first_ref, low_ref, qkv_ref, qkv_grad_ref, x_grad_ref, sums_ref, mixed_grad):
    width = first_ref.shape[1]

    @pl.when(pl.program_id(0) == 0)
    def _():
        sums_ref[...] = jnp.zeros_like(sums_ref)

    w_ref = ready(0)
    mixed_grad[...] = dot_nt(low_ref[...], w_ref[:, 3 * width :]).astype(bf16)
    for start in range(0, first_ref.shape[0], SEG_LEN):
        heads_backward(qkv_ref, mixed_grad, qkv_grad_ref, pl.ds(start, SEG_LEN), width, None)
    qkv_grad = qkv_grad_ref[...]
    x_grad_ref[...] = first_ref[...] + dot_nt(qkv_grad, w_ref[:, : 3 * width])
    sums_ref[0:1, :] += column_sum(qkv_grad[:, :width].astype(f32))
    sums_ref[1:2, :] += column_sum(qkv_grad[:, 2 * width :].astype(f32))


def cross_kernel(
    single, layout, ready, place_ref, x_ref, cot_ref, key_own_ref, key_all_ref, small_ref,
    out_ref, x_grad_ref, grads_ref, sums_ref,
    qkv_ref, qkv_grad_ref, mixed_ref, mixed_grad, slope, act_ref, inner_ref, vec_ref, grad_ref,
):
    own = layout[1]
    load_vec(small_ref, *layout, vec_ref)
    width = x_ref.shape[1]
    count = x_ref.shape[0]
    rows = pl.ds(0, count)

    @pl.when(pl.program_id(0) == 0)
    def _():
        sums_ref[...] = jnp.zeros_like(sums_ref)

    attn_ref = ready(0)
    mask = key_own_ref[...] == key_all_ref[0]
    entry = x_ref[...]
    low_in = entry.astype(bf16)
    qkv = dot_nn(low_in, attn_ref[:, : 3 * width]) + qkv_bias(vec_ref)
    qkv_ref[...] = qkv.astype(bf16)
    heads_forward(qkv_ref, mixed_ref, [rows], width, mask)
    first_sum = entry + dot_nn(mixed_ref[...], attn_ref[:, 3 * width :]) + vec_ref[2:3, :]
    unit_one, inverse_one = normalise(first_sum)
    normed = unit_one * vec_ref[3:4, :] + vec_ref[4:5, :]
    low = normed.astype(bf16)
    up_ref = ready(1)
    total = normed + vec_ref[5:6, :]
    for part in range(4):
        cols = pl.ds(part * width, width)
        inner = dot_nn(low, up_ref[:, cols]) + vec_ref[8 + part : 9 + part, :]
        act, rate = gelu_parts(inner)
        act = act.astype(bf16)
        act_ref[:, cols] = act
        slope[:, cols] = rate
        if part == 0:
            down_ref = ready(2)
        total = total + dot_nt(act, down_ref[:, cols])
    unit_two, inverse_two = normalise(total)
    out_ref[...] = (unit_two * vec_ref[6:7, :] + vec_ref[7:8, :]).astype(bf16)

    if single:
        for part in range(small_ref.shape[0]):
            for at in range(width // 128):
                tile = small_ref[part, at * 8 : (at + 1) * 8, :]
                grad_ref[part * 8 : (part + 1) * 8, at * 128 : (at + 1) * 128] = tile.astype(f32)
        grad = grad_ref[...]
    else:
        grad = cot_ref[...].astype(f32)
    sums_ref[6:7, :] += column_sum(grad * unit_two)
    sums_ref[7:8, :] += column_sum(grad)
    second_grad = norm_back(grad, unit_two, inverse_two, vec_ref[6:7, :])
    branch = second_grad.astype(bf16)
    sums_ref[5:6, :] += column_sum(branch.astype(f32))
    total = second_grad
    for part in range(4):
        cols = pl.ds(part * width, width)
        inner = (dot_nn(branch, down_ref[:, cols]) * slope[:, cols]).astype(bf16)
        inner_ref[:, cols] = inner
        sums_ref[8 + part : 9 + part, :] += column_sum(inner.astype(f32))
        total = total + dot_nt(inner, up_ref[:, cols])
    sums_ref[3:4, :] += column_sum(total * unit_one)
    sums_ref[4:5, :] += column_sum(total)
    first = norm_back(total, unit_one, inverse_one, vec_ref[3:4, :])
    attn_low = first.astype(bf16)
    sums_ref[2:3, :] += column_sum(attn_low.astype(f32))
    mixed_grad[...] = dot_nt(attn_low, attn_ref[:, 3 * width :]).astype(bf16)
    heads_backward(qkv_ref, mixed_grad, qkv_grad_ref, rows, width, mask)
    qkv_grad = qkv_grad_ref[...]
    x_grad_ref[...] = first + dot_nt(qkv_grad, attn_ref[:, : 3 * width])
    sums_ref[0:1, :] += column_sum(qkv_grad[:, :width].astype(f32))
    sums_ref[1:2, :] += column_sum(qkv_grad[:, 2 * width :].astype(f32))

    begin = (place_ref[0] * 2 + place_ref[1]) * own
    spot = lax.broadcasted_iota(jnp.int32, (width, own), 0) - lax.broadcasted_iota(jnp.int32, (width, own), 1)
    chosen = (spot == begin).astype(f32).astype(bf16)
    start = 0
    for left, right in ((low_in, qkv_grad), (mixed_ref[...], attn_low), (low, inner_ref[...]), (branch, act_ref[...])):
        cols = right.shape[1]
        grad = dot_tn(dot_nn(left, chosen).astype(bf16), right)
        if single:
            grads_ref[:, start : start + cols] = grad.astype(bf16)
        else:

            @pl.when(pl.program_id(0) == 0)
            def _(start=start, cols=cols):
                grads_ref[:, start : start + cols] = jnp.zeros((own, cols), f32)

            grads_ref[:, start : start + cols] += grad
        start += cols
    if single:
        sums = sums_ref[0:12, :]
        sums = jnp.concatenate([sums[:, : width // 2], sums[:, width // 2 :]], 0).astype(bf16)
        grads_ref[:, start:] = jnp.concatenate([sums] * (own // 24), 0)


def row_spec(width, block=BLOCK):
    return pl.BlockSpec((block, width), lambda i: (i, 0))


def whole_spec(shape):
    return pl.BlockSpec(shape, lambda i: (0,) * len(shape), pipeline_mode=pl.Buffered(1))


def fixed_spec(shape):
    return pl.BlockSpec(shape, lambda i: (0,) * len(shape))


def params():
    return pltpu.CompilerParams(dimension_semantics=("arbitrary",), vmem_limit_bytes=VMEM_LIMIT)


def shaped(*dims, dtype=bf16):
    return jax.ShapeDtypeStruct(dims, dtype)


def cost(flops, nbytes, trans=0):
    return pl.CostEstimate(flops=int(flops), bytes_accessed=int(nbytes), transcendentals=int(trans))


def attn_forward(flat, place, attn, small, layout):
    rows, width = flat.shape
    weights = Weights(attn)
    return pl.pallas_call(
        weights.wrap(partial(attn_fwd_kernel, layout)),
        grid=(rows // BLOCK,),
        in_specs=weights.specs() + [row_spec(width), whole_spec(small.shape)],
        out_specs=[row_spec(3 * width), row_spec(width), row_spec(width)],
        out_shape=[shaped(rows, 3 * width), shaped(rows, width), shaped(rows, width, dtype=f32)],
        scratch_shapes=[pltpu.VMEM((16, width), f32)] + weights.scratch(),
        compiler_params=params(),
        cost_estimate=cost(2 * rows * width * (4 * width + 2 * SEG_LEN), rows * width * 14 + width * width * 8),
        name="seg_attn_fwd",
    )(*weights.arrays(place), flat, small)


def ffn_forward(first_sum, place, up_proj, down_proj, small, layout, parts):
    rows, width = first_sum.shape
    inner = up_proj.shape[1]
    weights = Weights(up_proj, down_proj)
    cls_shape = (parts, rows // SEG_LEN, width)
    cls_spec = fixed_spec(cls_shape)
    return pl.pallas_call(
        weights.wrap(partial(ffn_fwd_kernel, layout)),
        grid=(rows // BLOCK,),
        in_specs=weights.specs() + [row_spec(width), whole_spec(small.shape)],
        out_specs=[row_spec(width), row_spec(inner), row_spec(inner), row_spec(width), row_spec(width), cls_spec],
        out_shape=[
            shaped(rows, width), shaped(rows, inner), shaped(rows, inner), shaped(rows, width, dtype=f32),
            shaped(rows, width), shaped(*cls_shape, dtype=f32),
        ],
        scratch_shapes=[pltpu.VMEM((16, width), f32)] + weights.scratch(),
        compiler_params=params(),
        cost_estimate=cost(4 * rows * width * inner, rows * (width * 12 + inner * 4) + width * inner * 4, 2 * rows * inner),
        name="seg_ffn_fwd",
    )(*weights.arrays(place), first_sum, small)


def ffn_backward(cot, cls_grad, second_sum, first_sum, slope, place, up_proj, down_proj, small, layout):
    rows, width = first_sum.shape
    inner = up_proj.shape[1]
    weights = Weights(up_proj, down_proj)
    cls_spec = whole_spec(cls_grad.shape)
    return pl.pallas_call(
        weights.wrap(partial(ffn_bwd_kernel, layout), with_place=True),
        grid=(rows // BLOCK,),
        in_specs=weights.specs() + [
            row_spec(width), cls_spec, row_spec(width), row_spec(width), row_spec(inner), whole_spec(small.shape),
        ],
        out_specs=[row_spec(width), row_spec(inner), row_spec(width), row_spec(width), fixed_spec((16, width))],
        out_shape=[
            shaped(rows, width), shaped(rows, inner), shaped(rows, width, dtype=f32), shaped(rows, width),
            shaped(16, width, dtype=f32),
        ],
        scratch_shapes=[pltpu.VMEM((16, width), f32)] + weights.scratch(),
        compiler_params=params(),
        cost_estimate=cost(4 * rows * width * inner, rows * (width * 16 + inner * 4) + width * inner * 4),
        name="seg_ffn_bwd",
    )(*weights.arrays(place), cot, cls_grad, second_sum, first_sum, slope, small)


def attn_backward(first_grad, attn_low, qkv, place, attn, share, shares, before=()):
    rows, width = first_grad.shape
    weights = Weights(attn)
    steps = rows // BLOCK // shares
    spec = lambda cols: pl.BlockSpec((BLOCK, cols), lambda i: (i + share * steps, 0))
    kept = len(before)
    args = weights.arrays(place) + [first_grad, attn_low, qkv]

    def body(ready, *refs):
        attn_bwd_kernel(ready, *refs[:3], *refs[3 + kept :])

    return pl.pallas_call(
        weights.wrap(body),
        grid=(steps,),
        in_specs=weights.specs() + [spec(width), spec(width), spec(3 * width)] + [pl.BlockSpec(memory_space=pl.ANY)] * kept,
        out_specs=[spec(3 * width), spec(width), fixed_spec((8, width))],
        out_shape=[shaped(rows, 3 * width), shaped(rows, width, dtype=f32), shaped(8, width, dtype=f32)],
        input_output_aliases={len(args) + at: at for at in range(kept)},
        scratch_shapes=[pltpu.VMEM((BLOCK, width), bf16)] + weights.scratch(),
        compiler_params=params(),
        cost_estimate=cost(
            2 * rows * width * (4 * width + 5 * SEG_LEN) // shares, rows * width * 22 // shares + width * width * 8
        ),
        name="seg_attn_bwd",
    )(*args, *before)


def cross_layer(entry, cot, row_key, blocks, place, attn, up_proj, down_proj, small, layout):
    rows, width = entry.shape
    inner = up_proj.shape[1]
    block = rows // blocks
    spec = partial(row_spec, block=block)
    weights = Weights(attn, up_proj, down_proj)
    own = layout[1]
    both = jnp.tile(row_key.reshape(blocks, 1, block), (1, 1, 2))
    wide = (own, 3 * inner + (width // 2 if by_links() else 0))
    return pl.pallas_call(
        weights.wrap(partial(cross_kernel, by_links(), layout), with_place=True, split=None if blocks > 1 else False),
        grid=(blocks,),
        in_specs=weights.specs() + [
            spec(width), spec(width), spec(1), pl.BlockSpec((1, 1, 2 * block), lambda i: (i, 0, 0)), whole_spec(small.shape),
        ],
        out_specs=[spec(width), spec(width), fixed_spec(wide), fixed_spec((16, width))],
        out_shape=[
            shaped(rows, width), shaped(rows, width, dtype=f32), shaped(*wide, dtype=bf16 if by_links() else f32),
            shaped(16, width, dtype=f32),
        ],
        scratch_shapes=[
            pltpu.VMEM((block, 3 * width), bf16), pltpu.VMEM((block, 3 * width), bf16), pltpu.VMEM((block, width), bf16),
            pltpu.VMEM((block, width), bf16), pltpu.VMEM((block, inner), f32), pltpu.VMEM((block, inner), bf16),
            pltpu.VMEM((block, inner), bf16), pltpu.VMEM((16, width), f32), pltpu.VMEM((block, width), f32),
        ] + weights.scratch(),
        compiler_params=params(),
        cost_estimate=cost(24 * rows * width * 4 * width, rows * width * 40 + width * inner * 6),
        name="cross_layer",
    )(*weights.arrays(place), entry, cot, row_key.reshape(rows, 1), both, small)


def hop_seg(value, hops):
    size = lax.axis_size("seg")
    return lax.ppermute(value, "seg", [(at, (at + 2 * hops) % size) for at in range(size)])


def swap_core(value):
    return lax.ppermute(value, "seg", [(at, at ^ 1) for at in range(lax.axis_size("seg"))])


def swap_batch(value, flip):
    return lax.ppermute(value, "batch", [(at, at ^ flip) for at in range(lax.axis_size("batch"))])


def fence(*values):
    return lax.optimization_barrier(values)


def by_links():
    return lax.axis_size("batch") == 4 and lax.axis_size("seg") == 8


class Gather:
    def __init__(self, *shards):
        self.many = len(shards)
        self.own, self.cols = shards[0].shape
        self.quarter = self.cols // 4
        self.mine = jnp.concatenate(shards, 0) if self.many > 1 else shards[0]
        self.part = lax.dynamic_slice_in_dim(self.mine, lax.axis_index("batch") * self.quarter, self.quarter, 1)

    def run_seg(self):
        self.raw = [hop_seg(self.part, hops) for hops in (3, 2, 1)]

    def sort_wide(self, full):
        first = lax.axis_index("seg") // 2 + 1
        self.along = lax.dynamic_slice_in_dim(jnp.concatenate([full, full[:3]], 0), first, 3)

    def run_own(self):
        self.mine_too = swap_core(self.mine)

    def sort_seg(self):
        self.along = jnp.stack(self.raw)

    def run_near(self):
        self.near = [swap_batch(self.along, flip) for flip in (1, 2)]

    def run_far(self):
        half = self.mine.shape[0] // 2
        self.far = [swap_batch(self.near[1][:, :half], 1), swap_batch(self.near[0][:, half:], 2)]

    def run_core_along(self):
        self.along_too = swap_core(self.along)

    def run_core_near(self, joined):
        self.joined = joined
        if joined:
            self.near = [jnp.stack([self.along] + self.near)]
            self.near_too = [swap_core(array) for array in self.near]
        else:
            self.near_too = [self.along_too] + [swap_core(array) for array in self.near]
            self.near = [self.along] + self.near

    def run_core_far(self):
        self.far_too = [swap_core(array) for array in self.far]

    def pieces(self):
        own, cols, quarter = self.own, self.cols, self.quarter
        half = self.mine.shape[0] // 2
        arrays = [self.mine] + self.near + self.far + [self.mine_too] + self.near_too + self.far_too
        many = len(self.near)
        matrices = []
        for at in range(self.many):
            first, last = at * own, (at + 1) * own
            blocks = []
            for core in (0, 1):

                def chip(later, core=core):
                    return lambda z, c: (((z + 1 + later) & 3) * 2 + (c ^ core)) * own

                target = lambda z, c, q, core=core: ((z * 2 + (c ^ core)) * own, 0)
                blocks.append(((many + 3) * core, (slice(first, last), slice(None)), (own, cols), target))
                for later in range(3):
                    row = chip(later)
                    for flip in range(3):
                        target = lambda z, c, q, row=row, flip=flip: (row(z, c), (q ^ flip) * quarter)
                        source = (later, slice(first, last), slice(None))
                        where = (many + 3) * core + 1
                        source, where = ((flip,) + source, where) if self.joined else (source, where + flip)
                        blocks.append((where, source, (own, quarter), target))
                    for side in (0, 1):
                        lo, hi = max(first, side * half), min(last, (side + 1) * half)
                        if lo >= hi:
                            continue
                        target = lambda z, c, q, row=row, skip=lo - first: (row(z, c) + skip, (q ^ 3) * quarter)
                        source = (later, slice(lo - side * half, hi - side * half), slice(None))
                        blocks.append(((many + 3) * core + many + 1 + side, source, (hi - lo, quarter), target))
            matrices.append(Pieces((own * lax.axis_size("seg"), cols), arrays, blocks))
        return matrices


def gather_plain(shard):
    full = lax.all_gather(shard, "seg", axis=0, tiled=True)
    block = (0, (slice(None), slice(None)), full.shape, lambda z, c, q: (0, 0))
    return Pieces(full.shape, [full], [block])


def chips_exchange(value):
    return lax.all_to_all(value, "seg", 0, 0, axis_index_groups=CHIP_GROUPS, tiled=True)


def gather_seg(value):
    if not by_links():
        return lax.all_gather(value, "seg", axis=0, tiled=False)
    copies = jnp.broadcast_to(value, (lax.axis_size("seg"),) + value.shape)
    return lax.all_to_all(copies, "seg", 0, 0, tiled=True)


def plain_grad_kernel(steps, *refs):
    pairs, (out_ref,) = refs[: 2 * len(steps)], refs[2 * len(steps) :]
    begin = 0
    for at, many in enumerate(steps):

        @pl.when((pl.program_id(0) >= begin) & (pl.program_id(0) < begin + many))
        def _(at=at):
            out_ref[...] = dot_tn(pairs[2 * at][...], pairs[2 * at + 1][...]).astype(bf16)

        begin += many


def plain_grads(*pairs):
    rows, width = pairs[0][0].shape
    steps = tuple(right.shape[1] // width for _, right in pairs)
    in_specs = []
    begin = 0
    for many in steps:
        in_specs.append(whole_spec((rows, width)))
        in_specs.append(pl.BlockSpec((rows, width), lambda i, begin=begin, many=many: (0, jnp.clip(i - begin, 0, many - 1))))
        begin += many
    return pl.pallas_call(
        partial(plain_grad_kernel, steps),
        grid=(begin,),
        in_specs=in_specs,
        out_specs=pl.BlockSpec((width, width), lambda i: (0, i)),
        out_shape=shaped(width, begin * width),
        compiler_params=params(),
        cost_estimate=cost(2 * rows * width * width * begin, 2 * (rows + width) * width * begin),
        name="plain_weight_grads",
    )(*[array for pair in pairs for array in pair])


def weight_grad_kernel(steps, place_ref, *refs):
    pairs, (keep_ref, send_ref, acc_ref) = refs[: 2 * len(steps)], refs[2 * len(steps) :]
    step = pl.program_id(0)
    begin = 0
    for at, many in enumerate(steps):

        @pl.when((step >= begin) & (step < begin + many))
        def _(at=at):
            acc_ref[...] = dot_tn(pairs[2 * at][...], pairs[2 * at + 1][...])

        begin += many
    c, q = place_ref[1], place_ref[2]
    size = keep_ref.shape[2]
    for flip in range(4):
        for chip in range(4):
            for core, out_ref in ((0, keep_ref), (1, send_ref)):
                row = (chip * 2 + (c ^ core)) * (4 * size) + (q ^ flip) * size
                rows = pl.ds(pl.multiple_of(row, size), size)
                out_ref[flip, chip] = acc_ref[rows, :].astype(bf16)


def weight_grads(place, *pairs):
    rows, width = pairs[0][0].shape
    steps = tuple(right.shape[1] // width for _, right in pairs)
    size = width // 32
    in_specs = [pl.BlockSpec(memory_space=pltpu.SMEM)]
    begin = 0
    for many in steps:
        in_specs.append(whole_spec((rows, width)))
        in_specs.append(pl.BlockSpec((rows, width), lambda i, begin=begin, many=many: (0, jnp.clip(i - begin, 0, many - 1))))
        begin += many
    out_spec = pl.BlockSpec((4, 4, size, width), lambda i: (0, 0, 0, i))
    out = shaped(4, 4, size, begin * width)
    return pl.pallas_call(
        partial(weight_grad_kernel, steps),
        grid=(begin,),
        in_specs=in_specs,
        out_specs=[out_spec, out_spec],
        out_shape=[out, out],
        scratch_shapes=[pltpu.VMEM((width, width), f32)],
        compiler_params=params(),
        cost_estimate=cost(2 * rows * width * width * begin, 2 * (rows + width) * width * begin),
        name="weight_grads",
    )(place, *[array for pair in pairs for array in pair])


def wide_sum(first, *others):
    total = first.astype(f32)
    for other in others:
        total = total + other.astype(f32)
    return total


def batch_spread(value):
    value = value.astype(bf16)
    return [value] + [swap_batch(value, flip) for flip in (1, 2, 3)]


def core_sums(keep, got):
    sums = [wide_sum(keep[flip], got[flip]) for flip in range(4)]
    return sums[0], [part.astype(bf16) for part in sums[1:]]


def batch_swaps(parts):
    return [swap_batch(part, flip) for flip, part in zip((1, 2, 3), parts)]


def place_kernel(plan, place_ref, *refs):
    count = 4 * len(plan)
    blocks, outs = refs[:count], refs[count:]
    q = place_ref[2]
    for at, targets in enumerate(plan):
        for flip in range(4):
            block = blocks[4 * at + flip]
            size = block.shape[0]
            rows = pl.ds(pl.multiple_of((q ^ flip) * size, size), size)
            for source, index, target, cols in targets:
                outs[index][rows, target : target + cols] = block[:, source : source + cols].astype(f32)


def place_outputs(place, plan, groups, own, shape):
    vmem = pl.BlockSpec(memory_space=pltpu.VMEM)
    return pl.pallas_call(
        partial(place_kernel, plan),
        in_specs=[pl.BlockSpec(memory_space=pltpu.SMEM)] + [vmem] * (4 * len(groups)),
        out_specs=[vmem] * own,
        out_shape=[jax.ShapeDtypeStruct(shape, f32)] * own,
        compiler_params=pltpu.CompilerParams(vmem_limit_bytes=16 * 1024 * 1024),
        cost_estimate=cost(0, own * shape[0] * shape[1] * 6),
        name="place_outputs",
    )(place, *[block for group in groups for block in group])


def scatter_sum(matrix):
    return lax.psum_scatter(matrix.astype(bf16), "seg", scatter_dimension=0, tiled=True)


def local(
    hidden, seg_doc, seg_attn, seg_up, seg_down, seg_vec,
    cross_attn, cross_up, cross_down, cross_vec, tok_cot, cls_cot,
):
    micro, _, segments, _, length, width = hidden.shape
    own, cols = seg_attn.shape
    parts = lax.axis_size("seg")
    place = lax.axis_index("seg")
    count = micro * segments
    total = parts * count
    spot = jnp.stack([place // 2, place % 2, lax.axis_index("batch")]).astype(jnp.int32)

    flat = hidden.reshape(count * length, width)
    tiles = width // 128
    vecs = jnp.pad(jnp.concatenate([seg_vec.T, cross_vec.T], 0), ((0, 0), (0, 128 - own)))
    small = cls_cot.reshape(count, tiles, 128).transpose(1, 0, 2).reshape(count * tiles, 128)
    small = jnp.concatenate([small, vecs], 0)
    seg_layout, cross_layout = (count * tiles, own), (count * tiles + 12, own)

    docs = seg_doc[:, 0].reshape(micro, segments, parts) + (1 << 16) * jnp.arange(micro, dtype=jnp.int32)[:, None, None]
    docs = docs.transpose(2, 0, 1)
    blocks = micro if total > 256 else 1
    if blocks > 1:
        order = lambda rows: rows.reshape(parts, micro, segments, -1).transpose(1, 0, 2, 3).reshape(total, -1)
        back = lambda rows: rows.reshape(micro, parts, segments, -1).transpose(1, 0, 2, 3).reshape(total, -1)
        row_key = docs.transpose(1, 0, 2).reshape(total)
    else:
        order = back = lambda rows: rows
        row_key = docs.reshape(total)
    if by_links():
        one, two, three = Gather(seg_attn), Gather(seg_up, seg_down), Gather(cross_up, cross_down)
        one.run_seg()
        small = gather_seg(small)
        one.run_own()
        one.raw, small, two.part, two.mine = fence(one.raw, small, two.part, two.mine)
        one.sort_seg()
        one.run_near()
        two.run_seg()
        (one.near,) = fence(one.near)
        one.run_far()
        wide = jnp.broadcast_to(three.part, (4,) + three.part.shape)
        one.far, one.near, two.raw, wide, two.mine, three.mine, row_key = fence(
            one.far, one.near, two.raw, wide, two.mine, three.mine, row_key
        )
        two.sort_seg()
        two.run_near()
        two.run_core_along()
        full = chips_exchange(wide)
        one.run_core_near(True)
        one.run_core_far()
        (attn_full,) = one.pieces()
        outs = attn_forward(flat, spot, attn_full, small, seg_layout)
        two.run_own()
        three.run_own()
        (qkv, mixed, first_sum), two.near, two.along_too, full, cross_attn, two.mine_too, three.mine_too = fence(
            outs, two.near, two.along_too, full, cross_attn, two.mine_too, three.mine_too
        )
        cross_attn_full = gather_plain(cross_attn)
        two.run_far()
        two.run_core_near(False)
        (two.far, full) = fence(two.far, full)
        three.sort_wide(full)
        three.run_near()
        two.run_core_far()
        three.run_core_along()
        up_full, down_full = two.pieces()
        outs = ffn_forward(first_sum, spot, up_full, down_full, small, seg_layout, parts)
        (normed, act, slope, second_sum, tok, cls), three.near, three.along_too = fence(outs, three.near, three.along_too)
        three.run_far()
        entry = lax.all_to_all(cls, "seg", 0, 0, tiled=True).reshape(total, width)
        cot_all = entry
        three.run_core_near(False)
        entry, three.far = fence(entry, three.far)
        three.run_core_far()
        cross_up_full, cross_down_full = three.pieces()
    else:
        attn_full, up_full, down_full = [gather_plain(shard) for shard in (seg_attn, seg_up, seg_down)]
        cross_attn_full, cross_up_full, cross_down_full = [
            gather_plain(shard) for shard in (cross_attn, cross_up, cross_down)
        ]
        small = gather_seg(small)
        cot_all = small[:, : count * tiles].reshape(parts, tiles, count, 128).transpose(0, 2, 1, 3).reshape(total, width)
        qkv, mixed, first_sum = attn_forward(flat, spot, attn_full, small, seg_layout)
        normed, act, slope, second_sum, tok, cls = ffn_forward(first_sum, spot, up_full, down_full, small, seg_layout, parts)
        entry = gather_seg(cls[0]).reshape(total, width)

    cls_out, cls_grad, x_grads, x_sums = cross_layer(
        order(entry), order(cot_all), row_key, blocks, spot,
        cross_attn_full, cross_up_full, cross_down_full, small, cross_layout,
    )
    own_cols = lambda rows: lax.dynamic_slice_in_dim(rows, place * own, own, 1)
    own_rows = lambda rows: lax.dynamic_slice_in_dim(back(rows), place * count, count, 0)
    cls_out = own_rows(cls_out)
    if not by_links():
        cls_grad = own_rows(cls_grad)
    outs = ffn_backward(
        tok_cot.reshape(count * length, width),
        cls_grad, second_sum, first_sum, slope, spot, up_full, down_full, small, seg_layout,
    )

    if by_links():
        folded = lambda rows: jnp.concatenate([rows[:, : width // 2], rows[:, width // 2 :]], 0)
        unfolded = lambda rows: jnp.concatenate([rows[:12], rows[12:]], 1)
        x_came = lax.all_to_all(x_grads.reshape(4, own // 4, 3 * cols + width // 2), "batch", 0, 0, tiled=True)
        (branch, inner, first_grad, attn_low, ffn_sums), x_came = fence(outs, x_came)
        x_sum = jnp.sum(x_came.astype(f32), 0)
        cross_sums = unfolded(x_sum[:, 3 * cols :])
        x_low = x_sum[:, : 3 * cols].astype(bf16)
        x_low, branch = fence(x_low, branch)
        x_low, inner = fence(x_low, inner)
        x_near = [swap_batch(x_low, flip) for flip in (1, 2)]
        keep_up, send = weight_grads(spot, (normed, inner))
        keep_up, send, act, x_near, x_low = fence(keep_up, send, act, x_near, x_low)
        got_up = swap_core(send)
        x_far = swap_batch(x_low, 3)
        down_grad = plain_grads((branch, act), (mixed, attn_low))
        down_grad, got_up, x_far, attn_low = fence(down_grad, got_up, x_far, attn_low)
        down_part = lax.psum_scatter(down_grad, "seg", scatter_dimension=0, tiled=True)
        set_cross = [x_low] + x_near + [x_far]
        stay_up, leave = core_sums(keep_up, got_up)
        leave, attn_low = fence(leave, attn_low)
        near_up = [swap_batch(leave[0], 1), swap_batch(leave[1], 2)]
        outs = attn_backward(first_grad, attn_low, qkv, spot, attn_full, 0, 1)
        (qkv_grad, hidden_grad, attn_sums), near_up, last = fence(outs, near_up, leave[2])
        far_up = swap_batch(last, 3)
        sums = folded(jnp.concatenate([attn_sums[:2], ffn_sums[2:12]], 0))
        sums_too = swap_core(sums)
        keep, send = weight_grads(spot, (flat, qkv_grad))
        keep, send, sums, sums_too, far_up = fence(keep, send, sums, sums_too, far_up)
        got = swap_core(send)
        total_up = wide_sum(stay_up, *near_up, far_up).astype(bf16)
        raw_up = chips_exchange(total_up)
        sums = jnp.broadcast_to(sums + sums_too, (4, 24, width // 2))
        stay, leave = core_sums(keep, got)
        stay = jnp.concatenate([stay, sums], 2)
        leave = [jnp.concatenate([part, sums.astype(bf16)], 2) for part in leave]
        came = [swap_batch(part, flip) for flip, part in zip((1, 2, 3), leave)]
        shape = (own, cols)
        x_plan = (((0, 0, 0, cols), (cols, 1, 0, cols), (2 * cols, 2, 0, cols)),)
        x_placed = place_outputs(spot, x_plan, (set_cross,), 3, shape)
        came, raw_up, down_part, x_placed = fence(came, raw_up, down_part, x_placed)
        total_qkv = wide_sum(stay, *came).astype(bf16)
        raw = chips_exchange(total_qkv)
        batch_place = lax.axis_index("batch")
        shares = [lax.dynamic_slice_in_dim(down_part, (batch_place ^ flip) * (own // 4), own // 4, 0) for flip in range(4)]
        down_came = [swap_batch(shares[flip], flip) for flip in (1, 2, 3)]
        up_low = jnp.sum(raw_up.astype(f32), 0).astype(bf16)
        set_up = batch_spread(up_low)
        set_down = batch_spread(wide_sum(shares[0], *down_came))
        raw, set_down, set_up = fence(raw, set_down, set_up)
        last = jnp.sum(raw.astype(f32), 0)
        seg_sums = unfolded(last[:, 3 * width :])
        set_qkv = batch_spread(last[:, : 3 * width])
        (down_placed,) = place_outputs(spot, (((0, 0, 0, cols),),), (set_down,), 1, shape)
        (up_placed,) = place_outputs(spot, (((0, 0, 0, cols),),), (set_up,), 1, shape)
        attn_plan = (((0, 0, 0, 3 * width),), ((cols, 0, 3 * width, width),))
        (attn_placed,) = place_outputs(spot, attn_plan, (set_qkv, set_down), 1, shape)
        grads = [attn_placed, up_placed, down_placed] + list(x_placed)
    else:
        branch, inner, first_grad, attn_low, ffn_sums = outs
        qkv_grad, hidden_grad, attn_sums = attn_backward(first_grad, attn_low, qkv, spot, attn_full, 0, 1)
        x_grads = x_grads.astype(bf16)
        grads = [
            scatter_sum(jnp.concatenate([dot_tn(flat, qkv_grad), dot_tn(mixed, attn_low)], 1)),
            scatter_sum(dot_tn(normed, inner)), scatter_sum(dot_tn(branch, act)),
            x_grads[:, :cols], x_grads[:, cols : 2 * cols], x_grads[:, 2 * cols :],
        ]
        grads = [grad.astype(f32) for grad in lax.psum(tuple(grads), "batch")]
        seg_sums = lax.psum(jnp.concatenate([attn_sums[:2], ffn_sums[2:12]], 0), ("batch", "seg"))
        cross_sums = lax.psum(x_sums[:12], "batch")
    seg_vec_grad = own_cols(seg_sums).T
    cross_vec_grad = own_cols(cross_sums).T
    return (
        tok.reshape(hidden.shape), cls_out.reshape(cls_cot.shape), hidden_grad.reshape(hidden.shape),
        grads[0], grads[1], grads[2], seg_vec_grad, grads[3], grads[4], grads[5], cross_vec_grad,
    )


def solution(mesh):
    wide = P(None, "batch", None, "seg", None, None)
    rows = P("seg", None)
    cls = P(None, "batch", None, "seg", None)
    in_specs = (wide, P(None, "batch", None)) + (rows,) * 8 + (wide, cls)
    out_specs = (wide, cls, wide) + (rows,) * 8
    return jax.shard_map(local, mesh=mesh, in_specs=in_specs, out_specs=out_specs, check_vma=False)
```

```python
from functools import partial

import jax
import jax.numpy as jnp
from jax import lax
from jax.experimental import pallas as pl
from jax.experimental.pallas import tpu as pltpu
from jax.sharding import PartitionSpec as P

HEADS = 12
HEAD_DIM = 64
SEG_LEN = 128
PAIRS = HEADS // 2
PAIR = 2 * HEAD_DIM
GROUP = 6

NEG_FILL = -1e30
LN_EPS = 1e-05
SCALE = HEAD_DIM ** (-0.5)
ROOT_HALF = 0.7071067811865476
PDF_AT_ZERO = 0.3989422804014327
BLOCK = 256
CHIP_GROUPS = [[0, 2, 4, 6], [1, 3, 5, 7]]
VMEM_LIMIT = 60 * 1024 * 1024

f32 = jnp.float32
bf16 = jnp.bfloat16


def dot_nn(left, right):
    return lax.dot_general(left, right, (((1,), (0,)), ((), ())), preferred_element_type=f32)


def dot_nt(left, right):
    return lax.dot_general(left, right, (((1,), (1,)), ((), ())), preferred_element_type=f32)


def dot_tn(left, right):
    return lax.dot_general(left, right, (((0,), (0,)), ((), ())), preferred_element_type=f32)


def normalise(rows):
    centred = rows - jnp.mean(rows, -1, keepdims=True)
    spread = jnp.mean(centred * centred, -1, keepdims=True)
    inverse = lax.rsqrt(spread + LN_EPS)
    return centred * inverse, inverse


def norm_back(grad, unit, inverse, gain):
    scaled = grad * gain
    return inverse * (
        scaled
        - jnp.mean(scaled, -1, keepdims=True)
        - unit * jnp.mean(scaled * unit, -1, keepdims=True)
    )


def column_sum(rows):
    return jnp.sum(rows, 0, keepdims=True)


def gelu_parts(value):
    cdf = 0.5 * (1.0 + lax.erf(value * ROOT_HALF))
    pdf = PDF_AT_ZERO * jnp.exp(-0.5 * value * value)
    return value * cdf, cdf + value * pdf


def first_half(rows):
    return lax.broadcasted_iota(jnp.int32, (rows, PAIR), 1) < HEAD_DIM


def split_heads(rows, first):
    zero = jnp.zeros_like(rows)
    return jnp.concatenate([jnp.where(first, rows, zero), jnp.where(first, zero, rows)], 0)


def join_heads(stacked, first):
    rows = stacked.shape[0] // 2
    return jnp.where(first, stacked[:rows], stacked[rows:])


def pair_probs(query, keys, mask):
    scores = dot_nt(keys, query) * SCALE
    if mask is not None:
        scores = jnp.where(mask, scores, NEG_FILL)
    top = jnp.max(scores, 0, keepdims=True)
    expo = jnp.exp(scores - top)
    return expo * (1.0 / jnp.sum(expo, 0, keepdims=True))


def pair_parts(qkv_ref, rows, pair, width, first):
    at = pair * PAIR
    query = split_heads(qkv_ref[rows, at : at + PAIR], first)
    return query, qkv_ref[rows, width + at : width + at + PAIR], qkv_ref[rows, 2 * width + at : 2 * width + at + PAIR]


def heads_forward(qkv_ref, out_ref, spans, width, mask):
    first = first_half(spans[0].size)
    every = [(rows, pair) for rows in spans for pair in range(PAIRS)]
    parts = [pair_parts(qkv_ref, rows, pair, width, first) for rows, pair in every]
    probs = [pair_probs(query, keys, mask).astype(bf16) for query, keys, _ in parts]
    mixed = [join_heads(dot_tn(prob, values), first) for prob, (_, _, values) in zip(probs, parts)]
    for (rows, pair), value in zip(every, mixed):
        out_ref[rows, pair * PAIR : (pair + 1) * PAIR] = value.astype(bf16)


def heads_backward(qkv_ref, grad_ref, out_ref, rows, width, mask):
    first = first_half(rows.size)
    for start in range(0, PAIRS, GROUP):
        pairs = range(start, start + GROUP)
        parts = [pair_parts(qkv_ref, rows, pair, width, first) for pair in pairs]
        grads = [split_heads(grad_ref[rows, pair * PAIR : (pair + 1) * PAIR], first) for pair in pairs]
        probs = [pair_probs(query, keys, mask) for query, keys, _ in parts]
        prob_grads = [dot_nt(values, grad) for (_, _, values), grad in zip(parts, grads)]
        value_grads = [dot_nn(prob.astype(bf16), grad) for prob, grad in zip(probs, grads)]
        score_grads = [
            (prob * (grad - jnp.sum(grad * prob, 0, keepdims=True))).astype(bf16) for prob, grad in zip(probs, prob_grads)
        ]
        key_grads = [dot_nn(grad, query) * SCALE for grad, (query, _, _) in zip(score_grads, parts)]
        query_grads = [join_heads(dot_tn(grad, keys), first) * SCALE for grad, (_, keys, _) in zip(score_grads, parts)]
        for at, values in ((0, query_grads), (width, key_grads), (2 * width, value_grads)):
            for pair, value in zip(pairs, values):
                out_ref[rows, at + pair * PAIR : at + (pair + 1) * PAIR] = value.astype(bf16)


class Pieces:
    def __init__(self, shape, arrays, blocks):
        self.shape, self.arrays, self.blocks = shape, arrays, blocks

    def specs(self):
        return [pl.BlockSpec(memory_space=pl.ANY)] * len(self.arrays)

    def scratch(self):
        return [pltpu.VMEM(self.shape, bf16), pltpu.SemaphoreType.DMA((len(self.blocks),))]

    def copies(self, refs, place_ref, full_ref, sems):
        out = []
        for at, (index, source, size, target) in enumerate(self.blocks):
            row, col = target(place_ref[0], place_ref[1], place_ref[2])
            if not isinstance(row, int):
                row = pl.multiple_of(row, size[0])
            if not isinstance(col, int):
                col = pl.multiple_of(col, size[1])
            view = full_ref.at[pl.ds(row, size[0]), pl.ds(col, size[1])]
            out.append(pltpu.make_async_copy(refs[index].at[source], view, sems.at[at]))
        return out


class Weights:
    def __init__(self, *matrices):
        self.matrices = matrices

    def arrays(self, place):
        return [place] + [array for matrix in self.matrices for array in matrix.arrays]

    def specs(self):
        return [pl.BlockSpec(memory_space=pltpu.SMEM)] + [spec for matrix in self.matrices for spec in matrix.specs()]

    def scratch(self):
        return [item for matrix in self.matrices for item in matrix.scratch()]

    def wrap(self, body, with_place=False, split=None):
        many = sum(len(matrix.arrays) for matrix in self.matrices)

        def kernel(place_ref, *refs):
            given, rest = refs[:many], refs[many:]
            cut = len(rest) - 2 * len(self.matrices)
            rest, own = rest[:cut], rest[cut:]
            first = pl.program_id(0) == 0
            views, copies = [], []
            for at, matrix in enumerate(self.matrices):
                views.append(own[2 * at])
                copies.append(partial(matrix.copies, given[: len(matrix.arrays)], place_ref, own[2 * at], own[2 * at + 1]))
                given = given[len(matrix.arrays) :]

            def start():
                for group in copies:
                    for copy in group():
                        copy.start()

            def wait(at):
                for copy in copies[at]():
                    copy.wait()
                return views[at]

            def ready(at):
                pl.when(first)(lambda: (wait(at), None)[1])
                return views[at]

            call = lambda how: body(how, *([place_ref] if with_place else []), *rest)
            if split is None:
                pl.when(first)(start)
                call(ready)
            elif not split:
                start()
                call(wait)
            else:

                @pl.when(first)
                def _():
                    start()
                    call(wait)

                @pl.when(jnp.logical_not(first))
                def _():
                    call(lambda at: views[at])

        return kernel


def load_vec(small_ref, skip, own, vec_ref):
    @pl.when(pl.program_id(0) == 0)
    def _():
        for part in range(small_ref.shape[0]):
            vec_ref[0:12, part * own : (part + 1) * own] = small_ref[part, skip : skip + 12, :own].astype(f32)


def qkv_bias(vec_ref):
    query = vec_ref[0:1, :]
    return jnp.concatenate([query, jnp.zeros_like(query), vec_ref[1:2, :]], 1)


def attn_fwd_kernel(layout, ready, x_ref, small_ref, qkv_ref, mixed_ref, sum_ref, vec_ref):
    width = x_ref.shape[1]
    load_vec(small_ref, *layout, vec_ref)
    w_ref = ready(0)
    rows = x_ref[...]
    qkv = dot_nn(rows, w_ref[:, : 3 * width]) + qkv_bias(vec_ref)
    qkv_ref[...] = qkv.astype(bf16)
    spans = [pl.ds(start, SEG_LEN) for start in range(0, x_ref.shape[0], SEG_LEN)]
    heads_forward(qkv_ref, mixed_ref, spans, width, None)
    branch = dot_nn(mixed_ref[...], w_ref[:, 3 * width :])
    sum_ref[...] = rows.astype(f32) + branch + vec_ref[2:3, :]


def ffn_fwd_kernel(layout, ready, sum_ref, small_ref, norm_ref, act_ref, slope_ref, second_ref, tok_ref, cls_ref, vec_ref):
    width = sum_ref.shape[1]
    load_vec(small_ref, *layout, vec_ref)
    up_ref = ready(0)
    down_ref = ready(1)
    unit, _ = normalise(sum_ref[...])
    normed = unit * vec_ref[3:4, :] + vec_ref[4:5, :]
    low = normed.astype(bf16)
    norm_ref[...] = low
    total = normed + vec_ref[5:6, :]
    ahead = dot_nn(low, up_ref[:, :width])
    for part in range(4):
        cols = pl.ds(part * width, width)
        inner = ahead + vec_ref[8 + part : 9 + part, :]
        if part < 3:
            ahead = dot_nn(low, up_ref[:, (part + 1) * width : (part + 2) * width])
        act, slope = gelu_parts(inner)
        act = act.astype(bf16)
        act_ref[:, cols] = act
        slope_ref[:, cols] = slope.astype(bf16)
        total = total + dot_nt(act, down_ref[:, cols])
    second_ref[...] = total
    unit, _ = normalise(total)
    result = unit * vec_ref[6:7, :] + vec_ref[7:8, :]
    tok_ref[...] = result.astype(bf16)
    per = sum_ref.shape[0] // SEG_LEN
    for index in range(per):
        row = jnp.broadcast_to(result[index * SEG_LEN : index * SEG_LEN + 1, :][None], (cls_ref.shape[0], 1, width))
        cls_ref[:, pl.ds(pl.program_id(0) * per + index, 1), :] = row


def ffn_bwd_kernel(
    layout, ready, place_ref, cot_ref, cls_ref, second_ref, sum_ref, slope_ref, small_ref,
    branch_ref, inner_ref, first_ref, low_ref, sums_ref, vec_ref,
):
    width = sum_ref.shape[1]
    load_vec(small_ref, *layout, vec_ref)
    per = sum_ref.shape[0] // SEG_LEN
    begin = pl.program_id(0) * per
    if cls_ref.shape[0] > per * pl.num_programs(0):
        begin = begin + (place_ref[0] * 2 + place_ref[1]) * (per * pl.num_programs(0))

    @pl.when(pl.program_id(0) == 0)
    def _():
        sums_ref[...] = jnp.zeros_like(sums_ref)

    place = lax.broadcasted_iota(jnp.int32, (SEG_LEN, 1), 0) == 0
    parts = []
    for index in range(sum_ref.shape[0] // SEG_LEN):
        rows = cot_ref[index * SEG_LEN : (index + 1) * SEG_LEN, :].astype(f32)
        parts.append(rows + jnp.where(place, cls_ref[pl.ds(begin + index, 1), :], 0.0))
    grad = jnp.concatenate(parts, 0)
    unit, inverse = normalise(second_ref[...])
    sums_ref[6:7, :] += column_sum(grad * unit)
    sums_ref[7:8, :] += column_sum(grad)
    second_grad = norm_back(grad, unit, inverse, vec_ref[6:7, :])
    branch = second_grad.astype(bf16)
    branch_ref[...] = branch
    sums_ref[5:6, :] += column_sum(branch.astype(f32))
    up_ref = ready(0)
    down_ref = ready(1)
    total = second_grad
    ahead = dot_nn(branch, down_ref[:, :width])
    for part in range(4):
        cols = pl.ds(part * width, width)
        act_grad = ahead
        if part < 3:
            ahead = dot_nn(branch, down_ref[:, (part + 1) * width : (part + 2) * width])
        inner = (act_grad * slope_ref[:, cols].astype(f32)).astype(bf16)
        inner_ref[:, cols] = inner
        sums_ref[8 + part : 9 + part, :] += column_sum(inner.astype(f32))
        total = total + dot_nt(inner, up_ref[:, cols])
    unit, inverse = normalise(sum_ref[...])
    sums_ref[3:4, :] += column_sum(total * unit)
    sums_ref[4:5, :] += column_sum(total)
    first = norm_back(total, unit, inverse, vec_ref[3:4, :])
    first_ref[...] = first
    low = first.astype(bf16)
    low_ref[...] = low
    sums_ref[2:3, :] += column_sum(low.astype(f32))


def attn_bwd_kernel(ready, first_ref, low_ref, qkv_ref, qkv_grad_ref, x_grad_ref, sums_ref, mixed_grad):
    width = first_ref.shape[1]

    @pl.when(pl.program_id(0) == 0)
    def _():
        sums_ref[...] = jnp.zeros_like(sums_ref)

    w_ref = ready(0)
    mixed_grad[...] = dot_nt(low_ref[...], w_ref[:, 3 * width :]).astype(bf16)
    for start in range(0, first_ref.shape[0], SEG_LEN):
        heads_backward(qkv_ref, mixed_grad, qkv_grad_ref, pl.ds(start, SEG_LEN), width, None)
    qkv_grad = qkv_grad_ref[...]
    x_grad_ref[...] = first_ref[...] + dot_nt(qkv_grad, w_ref[:, : 3 * width])
    sums_ref[0:1, :] += column_sum(qkv_grad[:, :width].astype(f32))
    sums_ref[1:2, :] += column_sum(qkv_grad[:, 2 * width :].astype(f32))


def cross_kernel(
    single, layout, ready, place_ref, x_ref, cot_ref, key_own_ref, key_all_ref, small_ref,
    out_ref, x_grad_ref, grads_ref, sums_ref,
    qkv_ref, qkv_grad_ref, mixed_ref, mixed_grad, slope, act_ref, inner_ref, vec_ref, grad_ref,
):
    own = layout[1]
    load_vec(small_ref, *layout, vec_ref)
    width = x_ref.shape[1]
    count = x_ref.shape[0]
    rows = pl.ds(0, count)

    @pl.when(pl.program_id(0) == 0)
    def _():
        sums_ref[...] = jnp.zeros_like(sums_ref)

    attn_ref = ready(0)
    mask = key_own_ref[...] == key_all_ref[0]
    entry = x_ref[...]
    low_in = entry.astype(bf16)
    qkv = dot_nn(low_in, attn_ref[:, : 3 * width]) + qkv_bias(vec_ref)
    qkv_ref[...] = qkv.astype(bf16)
    heads_forward(qkv_ref, mixed_ref, [rows], width, mask)
    first_sum = entry + dot_nn(mixed_ref[...], attn_ref[:, 3 * width :]) + vec_ref[2:3, :]
    unit_one, inverse_one = normalise(first_sum)
    normed = unit_one * vec_ref[3:4, :] + vec_ref[4:5, :]
    low = normed.astype(bf16)
    up_ref = ready(1)
    total = normed + vec_ref[5:6, :]
    for part in range(4):
        cols = pl.ds(part * width, width)
        inner = dot_nn(low, up_ref[:, cols]) + vec_ref[8 + part : 9 + part, :]
        act, rate = gelu_parts(inner)
        act = act.astype(bf16)
        act_ref[:, cols] = act
        slope[:, cols] = rate
        if part == 0:
            down_ref = ready(2)
        total = total + dot_nt(act, down_ref[:, cols])
    unit_two, inverse_two = normalise(total)
    out_ref[...] = (unit_two * vec_ref[6:7, :] + vec_ref[7:8, :]).astype(bf16)

    if single:
        for part in range(small_ref.shape[0]):
            for at in range(width // 128):
                tile = small_ref[part, at * 8 : (at + 1) * 8, :]
                grad_ref[part * 8 : (part + 1) * 8, at * 128 : (at + 1) * 128] = tile.astype(f32)
        grad = grad_ref[...]
    else:
        grad = cot_ref[...].astype(f32)
    sums_ref[6:7, :] += column_sum(grad * unit_two)
    sums_ref[7:8, :] += column_sum(grad)
    second_grad = norm_back(grad, unit_two, inverse_two, vec_ref[6:7, :])
    branch = second_grad.astype(bf16)
    sums_ref[5:6, :] += column_sum(branch.astype(f32))
    total = second_grad
    for part in range(4):
        cols = pl.ds(part * width, width)
        inner = (dot_nn(branch, down_ref[:, cols]) * slope[:, cols]).astype(bf16)
        inner_ref[:, cols] = inner
        sums_ref[8 + part : 9 + part, :] += column_sum(inner.astype(f32))
        total = total + dot_nt(inner, up_ref[:, cols])
    sums_ref[3:4, :] += column_sum(total * unit_one)
    sums_ref[4:5, :] += column_sum(total)
    first = norm_back(total, unit_one, inverse_one, vec_ref[3:4, :])
    attn_low = first.astype(bf16)
    sums_ref[2:3, :] += column_sum(attn_low.astype(f32))
    mixed_grad[...] = dot_nt(attn_low, attn_ref[:, 3 * width :]).astype(bf16)
    heads_backward(qkv_ref, mixed_grad, qkv_grad_ref, rows, width, mask)
    qkv_grad = qkv_grad_ref[...]
    x_grad_ref[...] = first + dot_nt(qkv_grad, attn_ref[:, : 3 * width])
    sums_ref[0:1, :] += column_sum(qkv_grad[:, :width].astype(f32))
    sums_ref[1:2, :] += column_sum(qkv_grad[:, 2 * width :].astype(f32))

    begin = (place_ref[0] * 2 + place_ref[1]) * own
    spot = lax.broadcasted_iota(jnp.int32, (width, own), 0) - lax.broadcasted_iota(jnp.int32, (width, own), 1)
    chosen = (spot == begin).astype(f32).astype(bf16)
    start = 0
    for left, right in ((low_in, qkv_grad), (mixed_ref[...], attn_low), (low, inner_ref[...]), (branch, act_ref[...])):
        cols = right.shape[1]
        grad = dot_tn(dot_nn(left, chosen).astype(bf16), right)
        if single:
            grads_ref[:, start : start + cols] = grad.astype(bf16)
        else:

            @pl.when(pl.program_id(0) == 0)
            def _(start=start, cols=cols):
                grads_ref[:, start : start + cols] = jnp.zeros((own, cols), f32)

            grads_ref[:, start : start + cols] += grad
        start += cols
    if single:
        sums = sums_ref[0:12, :]
        sums = jnp.concatenate([sums[:, : width // 2], sums[:, width // 2 :]], 0).astype(bf16)
        grads_ref[:, start:] = jnp.concatenate([sums] * (own // 24), 0)


def row_spec(width, block=BLOCK):
    return pl.BlockSpec((block, width), lambda i: (i, 0))


def whole_spec(shape):
    return pl.BlockSpec(shape, lambda i: (0,) * len(shape), pipeline_mode=pl.Buffered(1))


def fixed_spec(shape):
    return pl.BlockSpec(shape, lambda i: (0,) * len(shape))


def params(limit=VMEM_LIMIT):
    return pltpu.CompilerParams(dimension_semantics=("arbitrary",), vmem_limit_bytes=limit)


def shaped(*dims, dtype=bf16):
    return jax.ShapeDtypeStruct(dims, dtype)


def cost(flops, nbytes, trans=0):
    return pl.CostEstimate(flops=int(flops), bytes_accessed=int(nbytes), transcendentals=int(trans))


def attn_forward(flat, place, attn, small, layout):
    rows, width = flat.shape
    weights = Weights(attn)
    return pl.pallas_call(
        weights.wrap(partial(attn_fwd_kernel, layout)),
        grid=(rows // BLOCK,),
        in_specs=weights.specs() + [row_spec(width), whole_spec(small.shape)],
        out_specs=[row_spec(3 * width), row_spec(width), row_spec(width)],
        out_shape=[shaped(rows, 3 * width), shaped(rows, width), shaped(rows, width, dtype=f32)],
        scratch_shapes=[pltpu.VMEM((16, width), f32)] + weights.scratch(),
        compiler_params=params(),
        cost_estimate=cost(2 * rows * width * (4 * width + 2 * SEG_LEN), rows * width * 14 + width * width * 8),
        name="seg_attn_fwd",
    )(*weights.arrays(place), flat, small)


def ffn_forward(first_sum, place, up_proj, down_proj, small, layout, parts):
    rows, width = first_sum.shape
    inner = up_proj.shape[1]
    weights = Weights(up_proj, down_proj)
    cls_shape = (parts, rows // SEG_LEN, width)
    cls_spec = fixed_spec(cls_shape)
    return pl.pallas_call(
        weights.wrap(partial(ffn_fwd_kernel, layout)),
        grid=(rows // BLOCK,),
        in_specs=weights.specs() + [row_spec(width), whole_spec(small.shape)],
        out_specs=[row_spec(width), row_spec(inner), row_spec(inner), row_spec(width), row_spec(width), cls_spec],
        out_shape=[
            shaped(rows, width), shaped(rows, inner), shaped(rows, inner), shaped(rows, width, dtype=f32),
            shaped(rows, width), shaped(*cls_shape, dtype=f32),
        ],
        scratch_shapes=[pltpu.VMEM((16, width), f32)] + weights.scratch(),
        compiler_params=params(),
        cost_estimate=cost(4 * rows * width * inner, rows * (width * 12 + inner * 4) + width * inner * 4, 2 * rows * inner),
        name="seg_ffn_fwd",
    )(*weights.arrays(place), first_sum, small)


def ffn_backward(cot, cls_grad, second_sum, first_sum, slope, place, up_proj, down_proj, small, layout):
    rows, width = first_sum.shape
    inner = up_proj.shape[1]
    weights = Weights(up_proj, down_proj)
    cls_spec = whole_spec(cls_grad.shape)
    return pl.pallas_call(
        weights.wrap(partial(ffn_bwd_kernel, layout), with_place=True),
        grid=(rows // BLOCK,),
        in_specs=weights.specs() + [
            row_spec(width), cls_spec, row_spec(width), row_spec(width), row_spec(inner), whole_spec(small.shape),
        ],
        out_specs=[row_spec(width), row_spec(inner), row_spec(width), row_spec(width), fixed_spec((16, width))],
        out_shape=[
            shaped(rows, width), shaped(rows, inner), shaped(rows, width, dtype=f32), shaped(rows, width),
            shaped(16, width, dtype=f32),
        ],
        scratch_shapes=[pltpu.VMEM((16, width), f32)] + weights.scratch(),
        compiler_params=params(56 * 1024 * 1024),
        cost_estimate=cost(4 * rows * width * inner, rows * (width * 16 + inner * 4) + width * inner * 4),
        name="seg_ffn_bwd",
    )(*weights.arrays(place), cot, cls_grad, second_sum, first_sum, slope, small)


def attn_backward(first_grad, attn_low, qkv, place, attn, share, shares, before=()):
    rows, width = first_grad.shape
    weights = Weights(attn)
    steps = rows // BLOCK // shares
    spec = lambda cols: pl.BlockSpec((BLOCK, cols), lambda i: (i + share * steps, 0))
    kept = len(before)
    args = weights.arrays(place) + [first_grad, attn_low, qkv]

    def body(ready, *refs):
        attn_bwd_kernel(ready, *refs[:3], *refs[3 + kept :])

    return pl.pallas_call(
        weights.wrap(body),
        grid=(steps,),
        in_specs=weights.specs() + [spec(width), spec(width), spec(3 * width)] + [pl.BlockSpec(memory_space=pl.ANY)] * kept,
        out_specs=[spec(3 * width), spec(width), fixed_spec((8, width))],
        out_shape=[shaped(rows, 3 * width), shaped(rows, width, dtype=f32), shaped(8, width, dtype=f32)],
        input_output_aliases={len(args) + at: at for at in range(kept)},
        scratch_shapes=[pltpu.VMEM((BLOCK, width), bf16)] + weights.scratch(),
        compiler_params=params(56 * 1024 * 1024),
        cost_estimate=cost(
            2 * rows * width * (4 * width + 5 * SEG_LEN) // shares, rows * width * 22 // shares + width * width * 8
        ),
        name="seg_attn_bwd",
    )(*args, *before)


def cross_layer(entry, cot, row_key, blocks, place, attn, up_proj, down_proj, small, layout):
    rows, width = entry.shape
    inner = up_proj.shape[1]
    block = rows // blocks
    spec = partial(row_spec, block=block)
    weights = Weights(attn, up_proj, down_proj)
    own = layout[1]
    both = jnp.tile(row_key.reshape(blocks, 1, block), (1, 1, 2))
    wide = (own, 3 * inner + (width // 2 if by_links() else 0))
    return pl.pallas_call(
        weights.wrap(partial(cross_kernel, by_links(), layout), with_place=True, split=None if blocks > 1 else False),
        grid=(blocks,),
        in_specs=weights.specs() + [
            spec(width), spec(width), spec(1), pl.BlockSpec((1, 1, 2 * block), lambda i: (i, 0, 0)), whole_spec(small.shape),
        ],
        out_specs=[spec(width), spec(width), fixed_spec(wide), fixed_spec((16, width))],
        out_shape=[
            shaped(rows, width), shaped(rows, width, dtype=f32), shaped(*wide, dtype=bf16 if by_links() else f32),
            shaped(16, width, dtype=f32),
        ],
        scratch_shapes=[
            pltpu.VMEM((block, 3 * width), bf16), pltpu.VMEM((block, 3 * width), bf16), pltpu.VMEM((block, width), bf16),
            pltpu.VMEM((block, width), bf16), pltpu.VMEM((block, inner), f32), pltpu.VMEM((block, inner), bf16),
            pltpu.VMEM((block, inner), bf16), pltpu.VMEM((16, width), f32), pltpu.VMEM((block, width), f32),
        ] + weights.scratch(),
        compiler_params=params(),
        cost_estimate=cost(24 * rows * width * 4 * width, rows * width * 40 + width * inner * 6),
        name="cross_layer",
    )(*weights.arrays(place), entry, cot, row_key.reshape(rows, 1), both, small)


def hop_seg(value, hops):
    size = lax.axis_size("seg")
    return lax.ppermute(value, "seg", [(at, (at + 2 * hops) % size) for at in range(size)])


def swap_core(value):
    return lax.ppermute(value, "seg", [(at, at ^ 1) for at in range(lax.axis_size("seg"))])


def swap_batch(value, flip):
    return lax.ppermute(value, "batch", [(at, at ^ flip) for at in range(lax.axis_size("batch"))])


def fence(*values):
    return lax.optimization_barrier(values)


def by_links():
    return lax.axis_size("batch") == 4 and lax.axis_size("seg") == 8


class Gather:
    def __init__(self, *shards):
        self.many = len(shards)
        self.own, self.cols = shards[0].shape
        self.quarter = self.cols // 4
        self.mine = jnp.concatenate(shards, 0) if self.many > 1 else shards[0]
        self.part = lax.dynamic_slice_in_dim(self.mine, lax.axis_index("batch") * self.quarter, self.quarter, 1)

    def run_seg(self):
        self.raw = [hop_seg(self.part, hops) for hops in (3, 2, 1)]

    def sort_wide(self, full):
        first = lax.axis_index("seg") // 2 + 1
        self.along = lax.dynamic_slice_in_dim(jnp.concatenate([full, full[:3]], 0), first, 3)

    def run_own(self):
        self.mine_too = swap_core(self.mine)

    def sort_seg(self):
        self.along = jnp.stack(self.raw)

    def run_near(self):
        self.near = [swap_batch(self.along, flip) for flip in (1, 2)]

    def run_far(self):
        half = self.mine.shape[0] // 2
        self.far = [swap_batch(self.near[1][:, :half], 1), swap_batch(self.near[0][:, half:], 2)]

    def run_core_along(self):
        self.along_too = swap_core(self.along)

    def run_core_near(self, joined):
        self.joined = joined
        if joined:
            self.near = [jnp.stack([self.along] + self.near)]
            self.near_too = [swap_core(array) for array in self.near]
        else:
            self.near_too = [self.along_too] + [swap_core(array) for array in self.near]
            self.near = [self.along] + self.near

    def run_core_far(self):
        self.far_too = [swap_core(array) for array in self.far]

    def pieces(self):
        own, cols, quarter = self.own, self.cols, self.quarter
        half = self.mine.shape[0] // 2
        arrays = [self.mine] + self.near + self.far + [self.mine_too] + self.near_too + self.far_too
        many = len(self.near)
        matrices = []
        for at in range(self.many):
            first, last = at * own, (at + 1) * own
            blocks = []
            for core in (0, 1):

                def chip(later, core=core):
                    return lambda z, c: (((z + 1 + later) & 3) * 2 + (c ^ core)) * own

                target = lambda z, c, q, core=core: ((z * 2 + (c ^ core)) * own, 0)
                blocks.append(((many + 3) * core, (slice(first, last), slice(None)), (own, cols), target))
                for later in range(3):
                    row = chip(later)
                    for flip in range(3):
                        target = lambda z, c, q, row=row, flip=flip: (row(z, c), (q ^ flip) * quarter)
                        source = (later, slice(first, last), slice(None))
                        where = (many + 3) * core + 1
                        source, where = ((flip,) + source, where) if self.joined else (source, where + flip)
                        blocks.append((where, source, (own, quarter), target))
                    for side in (0, 1):
                        lo, hi = max(first, side * half), min(last, (side + 1) * half)
                        if lo >= hi:
                            continue
                        target = lambda z, c, q, row=row, skip=lo - first: (row(z, c) + skip, (q ^ 3) * quarter)
                        source = (later, slice(lo - side * half, hi - side * half), slice(None))
                        blocks.append(((many + 3) * core + many + 1 + side, source, (hi - lo, quarter), target))
            matrices.append(Pieces((own * lax.axis_size("seg"), cols), arrays, blocks))
        return matrices


def gather_plain(shard):
    full = lax.all_gather(shard, "seg", axis=0, tiled=True)
    block = (0, (slice(None), slice(None)), full.shape, lambda z, c, q: (0, 0))
    return Pieces(full.shape, [full], [block])


def chips_exchange(value):
    return lax.all_to_all(value, "seg", 0, 0, axis_index_groups=CHIP_GROUPS, tiled=True)


def gather_seg(value):
    if not by_links():
        return lax.all_gather(value, "seg", axis=0, tiled=False)
    copies = jnp.broadcast_to(value, (lax.axis_size("seg"),) + value.shape)
    return lax.all_to_all(copies, "seg", 0, 0, tiled=True)


def plain_grad_kernel(steps, *refs):
    pairs, (out_ref,) = refs[: 2 * len(steps)], refs[2 * len(steps) :]
    begin = 0
    for at, many in enumerate(steps):

        @pl.when((pl.program_id(0) >= begin) & (pl.program_id(0) < begin + many))
        def _(at=at):
            out_ref[...] = dot_tn(pairs[2 * at][...], pairs[2 * at + 1][...]).astype(bf16)

        begin += many


def plain_grads(*pairs):
    rows, width = pairs[0][0].shape
    steps = tuple(right.shape[1] // width for _, right in pairs)
    in_specs = []
    begin = 0
    for many in steps:
        in_specs.append(whole_spec((rows, width)))
        in_specs.append(pl.BlockSpec((rows, width), lambda i, begin=begin, many=many: (0, jnp.clip(i - begin, 0, many - 1))))
        begin += many
    return pl.pallas_call(
        partial(plain_grad_kernel, steps),
        grid=(begin,),
        in_specs=in_specs,
        out_specs=pl.BlockSpec((width, width), lambda i: (0, i)),
        out_shape=shaped(width, begin * width),
        compiler_params=params(56 * 1024 * 1024),
        cost_estimate=cost(2 * rows * width * width * begin, 2 * (rows + width) * width * begin),
        name="plain_weight_grads",
    )(*[array for pair in pairs for array in pair])


def weight_grad_kernel(steps, place_ref, *refs):
    pairs, (keep_ref, send_ref, acc_ref) = refs[: 2 * len(steps)], refs[2 * len(steps) :]
    step = pl.program_id(0)
    begin = 0
    for at, many in enumerate(steps):

        @pl.when((step >= begin) & (step < begin + many))
        def _(at=at):
            acc_ref[...] = dot_tn(pairs[2 * at][...], pairs[2 * at + 1][...])

        begin += many
    c, q = place_ref[1], place_ref[2]
    size = keep_ref.shape[2]
    for flip in range(4):
        for chip in range(4):
            for core, out_ref in ((0, keep_ref), (1, send_ref)):
                row = (chip * 2 + (c ^ core)) * (4 * size) + (q ^ flip) * size
                rows = pl.ds(pl.multiple_of(row, size), size)
                out_ref[flip, chip] = acc_ref[rows, :].astype(bf16)


def weight_grads(place, *pairs):
    rows, width = pairs[0][0].shape
    steps = tuple(right.shape[1] // width for _, right in pairs)
    size = width // 32
    in_specs = [pl.BlockSpec(memory_space=pltpu.SMEM)]
    begin = 0
    for many in steps:
        in_specs.append(whole_spec((rows, width)))
        in_specs.append(pl.BlockSpec((rows, width), lambda i, begin=begin, many=many: (0, jnp.clip(i - begin, 0, many - 1))))
        begin += many
    out_spec = pl.BlockSpec((4, 4, size, width), lambda i: (0, 0, 0, i))
    out = shaped(4, 4, size, begin * width)
    return pl.pallas_call(
        partial(weight_grad_kernel, steps),
        grid=(begin,),
        in_specs=in_specs,
        out_specs=[out_spec, out_spec],
        out_shape=[out, out],
        scratch_shapes=[pltpu.VMEM((width, width), f32)],
        compiler_params=params(56 * 1024 * 1024),
        cost_estimate=cost(2 * rows * width * width * begin, 2 * (rows + width) * width * begin),
        name="weight_grads",
    )(place, *[array for pair in pairs for array in pair])


def wide_sum(first, *others):
    total = first.astype(f32)
    for other in others:
        total = total + other.astype(f32)
    return total


def batch_spread(value):
    value = value.astype(bf16)
    return [value] + [swap_batch(value, flip) for flip in (1, 2, 3)]


def core_sums(keep, got):
    sums = [wide_sum(keep[flip], got[flip]) for flip in range(4)]
    return sums[0], [part.astype(bf16) for part in sums[1:]]


def batch_swaps(parts):
    return [swap_batch(part, flip) for flip, part in zip((1, 2, 3), parts)]


def place_kernel(plan, place_ref, *refs):
    count = 4 * len(plan)
    blocks, outs = refs[:count], refs[count:]
    q = place_ref[2]
    for at, targets in enumerate(plan):
        for flip in range(4):
            block = blocks[4 * at + flip]
            size = block.shape[0]
            rows = pl.ds(pl.multiple_of((q ^ flip) * size, size), size)
            for source, index, target, cols in targets:
                outs[index][rows, target : target + cols] = block[:, source : source + cols].astype(f32)


def place_outputs(place, plan, groups, own, shape):
    vmem = pl.BlockSpec(memory_space=pltpu.VMEM)
    return pl.pallas_call(
        partial(place_kernel, plan),
        in_specs=[pl.BlockSpec(memory_space=pltpu.SMEM)] + [vmem] * (4 * len(groups)),
        out_specs=[vmem] * own,
        out_shape=[jax.ShapeDtypeStruct(shape, f32)] * own,
        compiler_params=pltpu.CompilerParams(vmem_limit_bytes=16 * 1024 * 1024),
        cost_estimate=cost(0, own * shape[0] * shape[1] * 6),
        name="place_outputs",
    )(place, *[block for group in groups for block in group])


def scatter_sum(matrix):
    return lax.psum_scatter(matrix.astype(bf16), "seg", scatter_dimension=0, tiled=True)


def local(
    hidden, seg_doc, seg_attn, seg_up, seg_down, seg_vec,
    cross_attn, cross_up, cross_down, cross_vec, tok_cot, cls_cot,
):
    micro, _, segments, _, length, width = hidden.shape
    own, cols = seg_attn.shape
    parts = lax.axis_size("seg")
    place = lax.axis_index("seg")
    count = micro * segments
    total = parts * count
    spot = jnp.stack([place // 2, place % 2, lax.axis_index("batch")]).astype(jnp.int32)

    flat = hidden.reshape(count * length, width)
    tiles = width // 128
    vecs = jnp.pad(jnp.concatenate([seg_vec.T, cross_vec.T], 0), ((0, 0), (0, 128 - own)))
    small = cls_cot.reshape(count, tiles, 128).transpose(1, 0, 2).reshape(count * tiles, 128)
    small = jnp.concatenate([small, vecs], 0)
    seg_layout, cross_layout = (count * tiles, own), (count * tiles + 12, own)

    docs = seg_doc[:, 0].reshape(micro, segments, parts) + (1 << 16) * jnp.arange(micro, dtype=jnp.int32)[:, None, None]
    docs = docs.transpose(2, 0, 1)
    blocks = micro if total > 256 else 1
    if blocks > 1:
        order = lambda rows: rows.reshape(parts, micro, segments, -1).transpose(1, 0, 2, 3).reshape(total, -1)
        back = lambda rows: rows.reshape(micro, parts, segments, -1).transpose(1, 0, 2, 3).reshape(total, -1)
        row_key = docs.transpose(1, 0, 2).reshape(total)
    else:
        order = back = lambda rows: rows
        row_key = docs.reshape(total)
    if by_links():
        one, two, three = Gather(seg_attn), Gather(seg_up, seg_down), Gather(cross_up, cross_down)
        one.run_seg()
        small = gather_seg(small)
        one.run_own()
        one.raw, small, two.part, two.mine = fence(one.raw, small, two.part, two.mine)
        one.sort_seg()
        one.run_near()
        two.run_seg()
        (one.near,) = fence(one.near)
        one.run_far()
        wide = jnp.broadcast_to(three.part, (4,) + three.part.shape)
        one.far, one.near, two.raw, wide, two.mine, three.mine, row_key = fence(
            one.far, one.near, two.raw, wide, two.mine, three.mine, row_key
        )
        two.sort_seg()
        two.run_near()
        two.run_core_along()
        full = chips_exchange(wide)
        one.run_core_near(True)
        one.run_core_far()
        (attn_full,) = one.pieces()
        outs = attn_forward(flat, spot, attn_full, small, seg_layout)
        two.run_own()
        three.run_own()
        (qkv, mixed, first_sum), two.near, two.along_too, full, cross_attn, two.mine_too, three.mine_too = fence(
            outs, two.near, two.along_too, full, cross_attn, two.mine_too, three.mine_too
        )
        cross_attn_full = gather_plain(cross_attn)
        two.run_far()
        two.run_core_near(False)
        (two.far, full) = fence(two.far, full)
        three.sort_wide(full)
        three.run_near()
        two.run_core_far()
        three.run_core_along()
        up_full, down_full = two.pieces()
        outs = ffn_forward(first_sum, spot, up_full, down_full, small, seg_layout, parts)
        (normed, act, slope, second_sum, tok, cls), three.near, three.along_too = fence(outs, three.near, three.along_too)
        three.run_far()
        entry = lax.all_to_all(cls, "seg", 0, 0, tiled=True).reshape(total, width)
        cot_all = entry
        three.run_core_near(False)
        entry, three.far = fence(entry, three.far)
        three.run_core_far()
        cross_up_full, cross_down_full = three.pieces()
    else:
        attn_full, up_full, down_full = [gather_plain(shard) for shard in (seg_attn, seg_up, seg_down)]
        cross_attn_full, cross_up_full, cross_down_full = [
            gather_plain(shard) for shard in (cross_attn, cross_up, cross_down)
        ]
        small = gather_seg(small)
        cot_all = small[:, : count * tiles].reshape(parts, tiles, count, 128).transpose(0, 2, 1, 3).reshape(total, width)
        qkv, mixed, first_sum = attn_forward(flat, spot, attn_full, small, seg_layout)
        normed, act, slope, second_sum, tok, cls = ffn_forward(first_sum, spot, up_full, down_full, small, seg_layout, parts)
        entry = gather_seg(cls[0]).reshape(total, width)

    cls_out, cls_grad, x_grads, x_sums = cross_layer(
        order(entry), order(cot_all), row_key, blocks, spot,
        cross_attn_full, cross_up_full, cross_down_full, small, cross_layout,
    )
    own_cols = lambda rows: lax.dynamic_slice_in_dim(rows, place * own, own, 1)
    own_rows = lambda rows: lax.dynamic_slice_in_dim(back(rows), place * count, count, 0)
    cls_out = own_rows(cls_out)
    if not by_links():
        cls_grad = own_rows(cls_grad)
    outs = ffn_backward(
        tok_cot.reshape(count * length, width),
        cls_grad, second_sum, first_sum, slope, spot, up_full, down_full, small, seg_layout,
    )

    if by_links():
        folded = lambda rows: jnp.concatenate([rows[:, : width // 2], rows[:, width // 2 :]], 0)
        unfolded = lambda rows: jnp.concatenate([rows[:12], rows[12:]], 1)
        x_came = lax.all_to_all(x_grads.reshape(4, own // 4, 3 * cols + width // 2), "batch", 0, 0, tiled=True)
        (branch, inner, first_grad, attn_low, ffn_sums), x_came = fence(outs, x_came)
        x_low = jnp.sum(x_came[:, :, : 3 * cols].astype(f32), 0).astype(bf16)
        cross_sums = unfolded(jnp.sum(x_came[:, :, 3 * cols :].astype(f32), 0))
        x_low, branch = fence(x_low, branch)
        x_low, inner = fence(x_low, inner)
        x_near = [swap_batch(x_low, flip) for flip in (1, 2)]
        keep_up, send = weight_grads(spot, (normed, inner))
        keep_up, send, act, x_near, x_low = fence(keep_up, send, act, x_near, x_low)
        got_up = swap_core(send)
        x_far = swap_batch(x_low, 3)
        down_grad = plain_grads((branch, act), (mixed, attn_low))
        down_grad, got_up, x_far, attn_low = fence(down_grad, got_up, x_far, attn_low)
        down_part = lax.psum_scatter(down_grad, "seg", scatter_dimension=0, tiled=True)
        set_cross = [x_low] + x_near + [x_far]
        stay_up, leave = core_sums(keep_up, got_up)
        leave, attn_low = fence(leave, attn_low)
        near_up = [swap_batch(leave[0], 1), swap_batch(leave[1], 2)]
        outs = attn_backward(first_grad, attn_low, qkv, spot, attn_full, 0, 1)
        (qkv_grad, hidden_grad, attn_sums), near_up, last = fence(outs, near_up, leave[2])
        far_up = swap_batch(last, 3)
        sums = folded(jnp.concatenate([attn_sums[:2], ffn_sums[2:12]], 0))
        sums_too = swap_core(sums)
        keep, send = weight_grads(spot, (flat, qkv_grad))
        keep, send, sums, sums_too, far_up = fence(keep, send, sums, sums_too, far_up)
        got = swap_core(send)
        total_up = wide_sum(stay_up, *near_up, far_up).astype(bf16)
        raw_up = chips_exchange(total_up)
        sums = jnp.broadcast_to(sums + sums_too, (4, 24, width // 2))
        stay, leave = core_sums(keep, got)
        stay = jnp.concatenate([stay, sums], 2)
        leave = [jnp.concatenate([part, sums.astype(bf16)], 2) for part in leave]
        came = [swap_batch(part, flip) for flip, part in zip((1, 2, 3), leave)]
        shape = (own, cols)
        x_plan = (((0, 0, 0, cols), (cols, 1, 0, cols), (2 * cols, 2, 0, cols)),)
        x_placed = place_outputs(spot, x_plan, (set_cross,), 3, shape)
        came, raw_up, down_part, x_placed = fence(came, raw_up, down_part, x_placed)
        total_qkv = wide_sum(stay, *came).astype(bf16)
        raw = chips_exchange(total_qkv)
        batch_place = lax.axis_index("batch")
        shares = [lax.dynamic_slice_in_dim(down_part, (batch_place ^ flip) * (own // 4), own // 4, 0) for flip in range(4)]
        down_came = [swap_batch(shares[flip], flip) for flip in (1, 2, 3)]
        up_low = jnp.sum(raw_up.astype(f32), 0).astype(bf16)
        set_up = batch_spread(up_low)
        set_down = batch_spread(wide_sum(shares[0], *down_came))
        raw, set_down, set_up = fence(raw, set_down, set_up)
        last = jnp.sum(raw.astype(f32), 0)
        seg_sums = unfolded(last[:, 3 * width :])
        set_qkv = batch_spread(last[:, : 3 * width])
        (down_placed,) = place_outputs(spot, (((0, 0, 0, cols),),), (set_down,), 1, shape)
        (up_placed,) = place_outputs(spot, (((0, 0, 0, cols),),), (set_up,), 1, shape)
        attn_plan = (((0, 0, 0, 3 * width),), ((cols, 0, 3 * width, width),))
        (attn_placed,) = place_outputs(spot, attn_plan, (set_qkv, set_down), 1, shape)
        grads = [attn_placed, up_placed, down_placed] + list(x_placed)
    else:
        branch, inner, first_grad, attn_low, ffn_sums = outs
        qkv_grad, hidden_grad, attn_sums = attn_backward(first_grad, attn_low, qkv, spot, attn_full, 0, 1)
        x_grads = x_grads.astype(bf16)
        grads = [
            scatter_sum(jnp.concatenate([dot_tn(flat, qkv_grad), dot_tn(mixed, attn_low)], 1)),
            scatter_sum(dot_tn(normed, inner)), scatter_sum(dot_tn(branch, act)),
            x_grads[:, :cols], x_grads[:, cols : 2 * cols], x_grads[:, 2 * cols :],
        ]
        grads = [grad.astype(f32) for grad in lax.psum(tuple(grads), "batch")]
        seg_sums = lax.psum(jnp.concatenate([attn_sums[:2], ffn_sums[2:12]], 0), ("batch", "seg"))
        cross_sums = lax.psum(x_sums[:12], "batch")
    seg_vec_grad = own_cols(seg_sums).T
    cross_vec_grad = own_cols(cross_sums).T
    return (
        tok.reshape(hidden.shape), cls_out.reshape(cls_cot.shape), hidden_grad.reshape(hidden.shape),
        grads[0], grads[1], grads[2], seg_vec_grad, grads[3], grads[4], grads[5], cross_vec_grad,
    )


def solution(mesh):
    wide = P(None, "batch", None, "seg", None, None)
    rows = P("seg", None)
    cls = P(None, "batch", None, "seg", None)
    in_specs = (wide, P(None, "batch", None)) + (rows,) * 8 + (wide, cls)
    out_specs = (wide, cls, wide) + (rows,) * 8
    return jax.shard_map(local, mesh=mesh, in_specs=in_specs, out_specs=out_specs, check_vma=False)
```
